32 devices in a mesh: replica: 4 (over x, core), fsdp: 2 (over y), seq: 4 (over z).
Axes of the slice: x: 2, y: 2, z: 4, core: 2. Of those that a mesh axis runs over, the one named last changes fastest.
Arguments:
- tokens: bfloat16 [8, 3, 1536, 768], P(('replica', 'fsdp'), None, 'seq'), may hold values from -6 to 6
- segment_ids: int32 [8, 3, 1536], P(('replica', 'fsdp')), may hold values from 0 to 7, never falling along the last dimension, each value on 1 to 768 neighbouring positions
- joined_weight: bfloat16 [768, 2304], P('fsdp'), may hold values from -0.21875 to 0.21875
- query_bias: bfloat16 [768], P('fsdp'), may hold values from -3 to 3
- value_bias: bfloat16 [768], P('fsdp'), may hold values from -3 to 3
- out_weight: bfloat16 [768, 768], P('fsdp'), may hold values from -0.875 to 0.875
- out_bias: bfloat16 [768], P('fsdp'), may hold values from -3 to 3
- norm_gain: bfloat16 [768], P('fsdp'), may hold values from 0.25 to 1.75
- norm_shift: bfloat16 [768], P('fsdp'), may hold values from -3 to 3
- up_weight: bfloat16 [768, 3072], P('fsdp'), may hold values from -0.21875 to 0.21875
- up_bias: bfloat16 [3072], P('fsdp'), may hold values from -3 to 3
- down_weight: bfloat16 [3072, 768], P('fsdp'), may hold values from -0.109375 to 0.109375
- down_bias: bfloat16 [768], P('fsdp'), may hold values from -3 to 3
- final_gain: bfloat16 [768], P('fsdp'), may hold values from 0.25 to 1.75
- final_shift: bfloat16 [768], P('fsdp'), may hold values from -3 to 3
- cotangent: bfloat16 [8, 3, 1536, 768], P(('replica', 'fsdp'), None, 'seq'), may hold values from -6 to 6
Outputs:
- output: bfloat16 [8, 3, 1536, 768], P(('replica', 'fsdp'), None, 'seq')
- grad_tokens: bfloat16 [8, 3, 1536, 768], P(('replica', 'fsdp'), None, 'seq')
- grad_joined_weight: float32 [768, 2304], P('fsdp')
- grad_query_bias: float32 [768], P('fsdp')
- grad_value_bias: float32 [768], P('fsdp')
- grad_out_weight: float32 [768, 768], P('fsdp')
- grad_out_bias: float32 [768], P('fsdp')
- grad_norm_gain: float32 [768], P('fsdp')
- grad_norm_shift: float32 [768], P('fsdp')
- grad_up_weight: float32 [768, 3072], P('fsdp')
- grad_up_bias: float32 [3072], P('fsdp')
- grad_down_weight: float32 [3072, 768], P('fsdp')
- grad_down_bias: float32 [768], P('fsdp')
- grad_final_gain: float32 [768], P('fsdp')
- grad_final_shift: float32 [768], P('fsdp')
The draws below stay inside these ranges and needn't reach their ends.
Inputs may be any that keep to these rules, and one draw needn't show every extreme that they name: `segment_ids`: in each packed sequence the ids never fall; each of the 8 documents has 1 to half of 1536 tokens, and one has exactly half of 1536.
All inputs are finite; a program needn't handle non-finite values.
Results may differ from the reference program's by a relative error of at most 0.02.
Values may be sent and summed in bfloat16 or wider, within the bound.
No kernel may reach another device: no remote copies, remote signals or barrier semaphores. Data moves between devices by JAX's collectives and lax.ppermute only.
A program may use at most 384 MiB of HBM per device.

```python
import math
import jax
import jax.numpy as jnp
import numpy as np
from jax import lax

D = 768
HEADS = 12
HEAD_DIM = 64
FF = 3072
MB = 3
DOCS = 8
SEQ = 1536
GROUPS = 8


def shard_levels(stream_key, dims, pieces, smallest, top_value):
    loudness, own = 1.0, jax.random.fold_in(stream_key, 6)
    for axis_at, shards_of in pieces:
        heights = jnp.exp(jax.random.uniform(jax.random.fold_in(own, axis_at), (shards_of,), jnp.float32, smallest / len(pieces), top_value / len(pieces)))
        loudness = loudness * jnp.repeat(heights, dims[axis_at] // shards_of).reshape([-1 if axis == axis_at else 1 for axis in range(len(dims))])
    return loudness


def profile(count, total, most, slope):
    loads = [(1 << 20) // math.isqrt(rank ** slope) + 1 for rank in range(2, count + 1)]
    surplus, given = total - most - (count - 1), [1] * (count - 1)
    while surplus > 0:
        free = [i for i in range(count - 1) if given[i] < most]
        pool, remaining = sum([loads[i] for i in free]), surplus
        for i in free:
            more = min(most - given[i], max(1, remaining * loads[i] // pool), surplus)
            given[i] = given[i] + more
            surplus = surplus - more
    return np.array([most] + given)


def uneven_parts(own_key, count, total, reach, skew):
    if count == 2:
        one = jax.random.randint(own_key, (), max(1, total - reach), min(reach, total - 1) + 1)
        return jnp.stack([one, total - one])
    tallies = jnp.asarray(profile(count, total, reach, skew), jnp.int32)
    pairs = (count - 1) // 2
    giver, sink = tallies[1:1 + 2 * pairs:2], tallies[2:2 + 2 * pairs:2]
    room = jnp.minimum(giver - 1, reach - sink)
    shifted = jax.random.randint(jax.random.fold_in(own_key, 1), (pairs,), 0, 1 << 20) % (room + 1)
    tallies = tallies.at[1:1 + 2 * pairs:2].set(giver - shifted).at[2:2 + 2 * pairs:2].set(sink + shifted)
    return tallies[jax.random.permutation(jax.random.fold_in(own_key, 2), count)]


def centred(own_key, shape, width, most, shards=(), held_as=jnp.bfloat16):
    array = jax.random.normal(own_key, shape, jnp.float32) * width
    if len(shards) > 0:
        array = shard_levels(own_key, shape, shards, -0.22, 0.18) * array
    return jnp.clip(array, min=-most, max=most).astype(held_as)


def setup_inputs(seed: int = 0) -> dict:
    arg_keys = jax.random.split(jax.random.key(seed), 17)
    tokens = centred(arg_keys[0], (GROUPS, MB, SEQ, D), 1.0, 6.0, ((0, 8), (2, 4)))
    segment_ids = jax.vmap(lambda own: jnp.searchsorted(jnp.cumsum(uneven_parts(own, DOCS, SEQ, SEQ // 2, 2)), jnp.arange(SEQ), side="right"))(jax.random.split(arg_keys[1], GROUPS * MB)).reshape((GROUPS, MB, SEQ)).astype(jnp.int32)
    joined_weight = centred(arg_keys[2], (D, 3 * D), D ** -0.5, 0.21875, ((0, 2),))
    query_bias = centred(arg_keys[3], (D,), 0.5, 3.0, ((0, 2),))
    value_bias = centred(arg_keys[4], (D,), 0.5, 3.0, ((0, 2),))
    out_weight = centred(arg_keys[5], (D, D), (D // 16) ** -0.5, 0.875, ((0, 2),))
    out_bias = centred(arg_keys[6], (D,), 0.5, 3.0, ((0, 2),))
    norm_gain = jnp.clip(1.0 + 0.15 * jax.random.normal(arg_keys[7], (D,), jnp.float32), 0.25, 1.75).astype(jnp.bfloat16)
    norm_shift = centred(arg_keys[8], (D,), 0.5, 3.0, ((0, 2),))
    up_weight = centred(arg_keys[9], (D, FF), D ** -0.5, 0.21875, ((0, 2),))
    up_bias = centred(arg_keys[10], (FF,), 0.5, 3.0, ((0, 2),))
    down_weight = centred(arg_keys[11], (FF, D), FF ** -0.5, 0.109375, ((0, 2),))
    down_bias = centred(arg_keys[12], (D,), 0.5, 3.0, ((0, 2),))
    final_gain = jnp.clip(1.0 + 0.15 * jax.random.normal(arg_keys[13], (D,), jnp.float32), 0.25, 1.75).astype(jnp.bfloat16)
    final_shift = centred(arg_keys[14], (D,), 0.5, 3.0, ((0, 2),))
    cotangent = centred(arg_keys[15], (GROUPS, MB, SEQ, D), 1.0, 6.0, ((0, 8), (2, 4)))
    return {"tokens": tokens, "segment_ids": segment_ids, "joined_weight": joined_weight, "query_bias": query_bias, "value_bias": value_bias, "out_weight": out_weight, "out_bias": out_bias, "norm_gain": norm_gain, "norm_shift": norm_shift, "up_weight": up_weight, "up_bias": up_bias, "down_weight": down_weight, "down_bias": down_bias, "final_gain": final_gain, "final_shift": final_shift, "cotangent": cotangent}


@jax.custom_vjp
def low(v):
    return lax.optimization_barrier(v.astype(jnp.bfloat16)).astype(jnp.float32)

@jax.custom_vjp
def low_back(v):
    return v

def low_keep(v):
    return (low(v), None)

def low_pass(kept, grad):
    return (grad,)

def back_keep(v):
    return (v, None)

def back_low(kept, grad):
    return (low(grad),)
low.defvjp(low_keep, low_pass)
low_back.defvjp(back_keep, back_low)
epsilon = 1e-05
masked_score = -1e+30

def matmul(left, right):
    return jnp.dot(left, right, precision=lax.Precision.HIGHEST, preferred_element_type=jnp.float32)

def layer_norm(values, gain, shift):
    centered = values - lax.optimization_barrier(jnp.mean(values, axis=-1, keepdims=True))
    inverse = lax.rsqrt(lax.optimization_barrier(jnp.mean(centered * centered, axis=-1, keepdims=True)) + epsilon)
    return centered * inverse * gain + shift

def forward(params, tokens, segments):
    joined_weight, query_bias, value_bias, out_weight, out_bias, norm_gain, norm_shift, up_weight, up_bias, down_weight, down_bias, final_gain, final_shift = params
    joined = matmul(tokens, joined_weight)
    query = low_back(low(joined[:, :D] + query_bias))
    keyed = low_back(low(joined[:, D:2 * D]))
    valued = low_back(low(joined[:, 2 * D:] + value_bias))
    key_heads = keyed.reshape(SEQ, HEADS, HEAD_DIM)
    value_heads = valued.reshape(SEQ, HEADS, HEAD_DIM)
    block = min(512, SEQ)
    scale = HEAD_DIM ** (-0.5)

    def one_block(start):
        query_part = lax.dynamic_slice_in_dim(query, start, block, 0).reshape(block, HEADS, HEAD_DIM)
        segment_part = lax.dynamic_slice_in_dim(segments, start, block, 0)
        scores = jnp.einsum('qhd,khd->hqk', query_part, key_heads, precision=lax.Precision.HIGHEST) * scale
        scores = low_back(scores)
        allowed = (segment_part[:, None] == segments[None, :])[None]
        scores = jnp.where(allowed, scores, masked_score)
        row_max = lax.optimization_barrier(jnp.max(scores, axis=-1, keepdims=True))
        weights = jnp.exp(scores - row_max)
        probs = low(weights / lax.optimization_barrier(jnp.sum(weights, axis=-1, keepdims=True)))
        mixed = jnp.einsum('hqk,khd->qhd', probs, value_heads, precision=lax.Precision.HIGHEST)
        return mixed.reshape(block, D)
    starts = jnp.arange(SEQ // block, dtype=jnp.int32) * block
    attended = low_back(low(lax.map(jax.checkpoint(one_block), starts).reshape(SEQ, D)))
    branch = low_back(matmul(attended, out_weight) + out_bias)
    hidden = layer_norm(tokens + branch, norm_gain, norm_shift)
    inner = low_back(matmul(low(hidden), up_weight) + up_bias)
    activated = low(jax.nn.gelu(inner, approximate=False))
    branch_two = low_back(matmul(activated, down_weight) + down_bias)
    return layer_norm(hidden + branch_two, final_gain, final_shift)

def reference(tokens, segment_ids, joined_weight, query_bias, value_bias, out_weight, out_bias, norm_gain, norm_shift, up_weight, up_bias, down_weight, down_bias, final_gain, final_shift, cotangent):
    params = (joined_weight.astype(jnp.float32), query_bias.astype(jnp.float32), value_bias.astype(jnp.float32), out_weight.astype(jnp.float32), out_bias.astype(jnp.float32), norm_gain.astype(jnp.float32), norm_shift.astype(jnp.float32), up_weight.astype(jnp.float32), up_bias.astype(jnp.float32), down_weight.astype(jnp.float32), down_bias.astype(jnp.float32), final_gain.astype(jnp.float32), final_shift.astype(jnp.float32))
    sequences = tokens.reshape(-1, SEQ, D)
    labels = segment_ids.reshape(-1, SEQ)
    incoming = cotangent.reshape(-1, SEQ, D)
    zeros = jax.tree.map(jnp.zeros_like, params)

    def one_sequence(totals, inputs):
        sequence, label, grad_in = inputs

        def apply_layer(weights, values):
            return forward(weights, values, label)
        result, pullback = jax.vjp(apply_layer, params, sequence.astype(jnp.float32))
        grad_params, grad_input = pullback(grad_in.astype(jnp.float32))
        totals = jax.tree.map(jnp.add, totals, grad_params)
        return (totals, (result.astype(jnp.bfloat16), grad_input.astype(jnp.bfloat16)))
    totals, (outputs, grad_inputs) = lax.scan(one_sequence, zeros, (sequences, labels, incoming))
    grad_joined, grad_query, grad_value, grad_outw, grad_outb, grad_ngain, grad_nshift, grad_upw, grad_upb, grad_downw, grad_downb, grad_fgain, grad_fshift = totals
    return (outputs.reshape(tokens.shape), grad_inputs.reshape(tokens.shape), grad_joined, grad_query, grad_value, grad_outw, grad_outb, grad_ngain, grad_nshift, grad_upw, grad_upb, grad_downw, grad_downb, grad_fgain, grad_fshift)
```

```python
import functools
import jax
import jax.numpy as jnp
from jax import lax
from jax.experimental import pallas as pl
from jax.experimental.pallas import tpu as pltpu
from jax.sharding import PartitionSpec as P

HEADS = 12
HEAD_DIM = 64
PAIR = 2 * HEAD_DIM
epsilon = 1e-05
masked_score = -1e30
scale = HEAD_DIM ** (-0.5)
TK_FWD = 256
TK_BWD = 256
ALIGN = 128
ROW_STEP = 16
VMEM_LIMIT = 62 * 1024 * 1024
FF_TILES = 4
f32 = jnp.float32
bf16 = jnp.bfloat16


def nt(left, right):
    return lax.dot_general(left, right, (((1,), (1,)), ((), ())), preferred_element_type=f32)


def tn(left, right):
    return lax.dot_general(left, right, (((0,), (0,)), ((), ())), preferred_element_type=f32)


def nn(left, right):
    return lax.dot_general(left, right, (((1,), (0,)), ((), ())), preferred_element_type=f32)


def stack_heads(pair):
    lane = lax.broadcasted_iota(jnp.int32, pair.shape, 1)
    zero = jnp.zeros_like(pair)
    return jnp.concatenate(
        [jnp.where(lane < HEAD_DIM, pair, zero), jnp.where(lane < HEAD_DIM, zero, pair)], axis=0
    )


def unstack_heads(rows):
    half = rows.shape[0] // 2
    lane = lax.broadcasted_iota(jnp.int32, (half, rows.shape[1]), 1)
    return jnp.where(lane < HEAD_DIM, rows[:half], rows[half:])


def start_pieces(offsets, first, piece_refs, full_s, sems):
    copies = []
    for at, piece in enumerate(piece_refs):
        size = piece.shape[0]
        row = pl.multiple_of(offsets[first + at], ROW_STEP)
        copy = pltpu.make_async_copy(piece, full_s.at[pl.ds(row, size), :], sems.at[first + at])
        copy.start()
        copies.append(copy)
    return copies


def start_columns(offsets, piece_refs, full_s, sems, width, at_col, size_col):
    copies = []
    for at, piece in enumerate(piece_refs):
        size = piece.shape[0]
        row = pl.multiple_of(offsets[at], ROW_STEP)
        for part in range(3):
            copy = pltpu.make_async_copy(
                piece.at[:, pl.ds(part * width + at_col, size_col)],
                full_s.at[pl.ds(row, size), pl.ds(part * size_col, size_col)],
                sems.at[at, part],
            )
            copy.start()
            copies.append(copy)
    return copies


def wait_all(copies):
    for copy in copies:
        copy.wait()


def project_window(bounds, x_refs, w_ref, bias_ref, cols, k_s, v_s, tail):
    block = x_refs[0].shape[0]
    width = k_s.shape[1]
    lo, hi = bounds[0], bounds[1]
    for at, x_ref in enumerate(x_refs):
        rows = pl.ds(at * block, block)
        active = (hi > at * block) & (lo < (at + 1) * block)

        @pl.when(active)
        def _():
            x = x_ref[...]
            k_s[rows, :] = nn(x, w_ref[:, width : 2 * width]).astype(bf16)
            v_s[rows, :] = (nn(x, w_ref[:, 2 * width :]) + bias_ref[1:2, cols]).astype(bf16)

        @pl.when(jnp.logical_not(active))
        def _():
            k_s[rows, :] = jnp.zeros((block, width), bf16)
            v_s[rows, :] = jnp.zeros((block, width), bf16)

    end = len(x_refs) * block
    k_s[end:, :] = jnp.zeros((tail, width), bf16)
    v_s[end:, :] = jnp.zeros((tail, width), bf16)


def tile_range(bounds, tk):
    low = bounds[0]
    high = bounds[1]
    start = (low // ALIGN) * ALIGN
    return start, (high - start + tk - 1) // tk


def project_queries(x_ref, w_ref, bias_ref, cols, q_s, qq_s):
    block = x_ref.shape[0]
    width = q_s.shape[1]
    q = nn(x_ref[...], w_ref[:, :width]) + bias_ref[0:1, cols]
    q_s[...] = q.astype(bf16) * jnp.asarray(scale, bf16)
    for pair in range(width // PAIR):
        here = slice(pair * PAIR, (pair + 1) * PAIR)
        qq_s[:, here] = stack_heads(q_s[:, here])


def forward_kernel(hops, pieces, first, bounds, offsets, *refs):
    count = 2 * hops + 1
    x_refs = refs[:count]
    w_refs, refs = refs[count : count + pieces], refs[count + pieces :]
    bias_ref, segq_ref, segk_ref, o_ref, lse_ref = refs[:5]
    w_ref, q_s, qq_s, k_s, v_s, top_s, sum_s, acc_s, sems = refs[5:]
    block, full_width = x_refs[0].shape
    width = o_ref.shape[1]
    tk = TK_FWD
    pairs = width // PAIR
    cols_all = slice(first * PAIR, first * PAIR + width)
    wait_all(start_columns(offsets, w_refs, w_ref, sems, full_width, first * PAIR, width))
    project_window(bounds, x_refs, w_ref, bias_ref, cols_all, k_s, v_s, tk - ALIGN)
    project_queries(x_refs[hops], w_ref, bias_ref, cols_all, q_s, qq_s)
    start, steps = tile_range(bounds, tk)
    segq = segq_ref[0:1, :]
    segq = jnp.concatenate([segq, segq], axis=1)
    top_s[...] = jnp.full(top_s.shape, masked_score, f32)
    sum_s[...] = jnp.ones(sum_s.shape, f32)
    sum_s[:pairs, :] = jnp.zeros((pairs, sum_s.shape[1]), f32)
    acc_s[...] = jnp.zeros(acc_s.shape, f32)

    @pl.loop(0, steps)
    def _(at):
        here = pl.ds(pl.multiple_of(start + at * tk, ALIGN), tk)
        allowed = segk_ref[here, 0:1] == segq
        for pair in range(pairs):
            cols = slice(pair * PAIR, (pair + 1) * PAIR)
            one = slice(pair, pair + 1)
            scores = nt(k_s[here, cols], qq_s[:, cols])
            scores = jnp.where(allowed, scores, masked_score)
            top = top_s[one, :]
            new_top = jnp.maximum(top, jnp.max(scores, axis=0, keepdims=True))
            fade = jnp.exp(top - new_top)
            weights = jnp.exp(scores - new_top)
            top_s[one, :] = new_top
            sum_s[one, :] = sum_s[one, :] * fade + jnp.sum(weights, axis=0, keepdims=True)
            acc_s[pair] = acc_s[pair] * fade + tn(v_s[here, cols], weights.astype(bf16))

    lse_ref[...] = top_s[...] + jnp.log(sum_s[...])
    for pair in range(pairs):
        cols = slice(pair * PAIR, (pair + 1) * PAIR)
        mixed = acc_s[pair] / sum_s[pair : pair + 1, :]
        o_ref[:, cols] = unstack_heads(mixed.T).astype(bf16)


def backward_kernel(hops, pieces, prev, first, skip, bounds, offsets, *refs):
    count = 2 * hops + 1
    x_refs = refs[:count]
    w_refs, refs = refs[count : count + pieces], refs[count + pieces :]
    bias_ref, segq_ref, segk_ref, o_ref, lse_ref, do_ref = refs[:6]
    prev_refs, refs = refs[6 : 6 + prev], refs[6 + prev :]
    out_refs, refs = refs[:count], refs[count:]
    dw_ref, w_ref, q_s, qq_s, gg_s, k_s, v_s, dk_s, dv_s, dw_s, stat_s, acc_s, db_s, sems = refs
    block, full_width = x_refs[0].shape
    width = q_s.shape[1]
    tk = TK_BWD
    pairs = width // PAIR
    cols_all = slice(first * PAIR, first * PAIR + width)
    copies = start_columns(offsets, w_refs, w_ref, sems, full_width, first * PAIR, width)
    dk_s[...] = jnp.zeros(dk_s.shape, f32)
    dv_s[...] = jnp.zeros(dv_s.shape, f32)
    acc_s[...] = jnp.zeros(acc_s.shape, f32)
    for pair in range(pairs):
        cols = slice(pair * PAIR, (pair + 1) * PAIR)
        far = slice((first + pair) * PAIR, (first + pair + 1) * PAIR)
        theirs = slice((skip + pair) * PAIR, (skip + pair + 1) * PAIR)
        grads = stack_heads(do_ref[:, far])
        gg_s[:, cols] = grads
        mixed = o_ref[:, theirs].astype(f32)
        product = grads.astype(f32) * jnp.concatenate([mixed, mixed], axis=0)
        stat_s[pair : pair + 1, :] = jnp.sum(product.T, axis=0, keepdims=True)
    wait_all(copies)
    project_window(bounds, x_refs, w_ref, bias_ref, cols_all, k_s, v_s, tk - ALIGN)
    project_queries(x_refs[hops], w_ref, bias_ref, cols_all, q_s, qq_s)
    lo, hi = bounds[0], bounds[1]
    actives = [(hi > at * block) & (lo < (at + 1) * block) for at in range(count)]
    start, steps = tile_range(bounds, tk)
    segq = segq_ref[0:1, :]
    segq = jnp.concatenate([segq, segq], axis=1)

    @pl.loop(0, steps)
    def _(at):
        here = pl.ds(pl.multiple_of(start + at * tk, ALIGN), tk)
        allowed = segk_ref[here, 0:1] == segq
        for pair in range(pairs):
            cols = slice(pair * PAIR, (pair + 1) * PAIR)
            keys = k_s[here, cols]
            queries = qq_s[:, cols]
            grads = gg_s[:, cols]
            scores = nt(keys, queries)
            scores = jnp.where(allowed, scores, masked_score)
            weights = jnp.exp(scores - lse_ref[skip + pair : skip + pair + 1, :])
            grad_weights = nt(v_s[here, cols], grads)
            grad_scores = (weights * (grad_weights - stat_s[pair : pair + 1, :])).astype(bf16)
            dv_s[here, cols] += nn(weights.astype(bf16), grads)
            dk_s[here, cols] += nn(grad_scores, queries)
            acc_s[pair] += tn(keys, grad_scores)

    for pair in range(pairs):
        cols = slice(pair * PAIR, (pair + 1) * PAIR)
        q_s[:, cols] = (unstack_heads(acc_s[pair].T) * scale).astype(bf16)
    dq = q_s[...]
    before = prev_refs[hops] if prev > 1 else prev_refs[0]
    dw_s[:, :width] = tn(x_refs[hops][...], dq)
    dw_s[:, width:] = jnp.zeros((full_width, 2 * width), f32)
    db_s[...] = jnp.zeros(db_s.shape, f32)
    db_s[0:1, cols_all] = jnp.sum(dq.astype(f32), axis=0, keepdims=True)
    out_refs[hops][...] = before[...] + nt(dq, w_ref[:, :width])
    for at in range(count):
        here = pl.ds(at * block, block)

        @pl.when(actives[at])
        def _():
            x = x_refs[at][...]
            dk = dk_s[here, :].astype(bf16)
            dv = dv_s[here, :].astype(bf16)
            db_s[1:2, cols_all] += jnp.sum(dv.astype(f32), axis=0, keepdims=True)
            back = nt(dk, w_ref[:, width : 2 * width]) + nt(dv, w_ref[:, 2 * width :])
            if at == hops:
                out_refs[at][...] += back
            else:
                if prev > 1:
                    back = back + prev_refs[at][...].astype(f32)
                out_refs[at][...] = back.astype(bf16)
            dw_s[:, width : 2 * width] += tn(x, dk)
            dw_s[:, 2 * width :] += tn(x, dv)

        if at != hops:
            @pl.when(jnp.logical_not(actives[at]))
            def _():
                if prev > 1:
                    out_refs[at][...] = prev_refs[at][...]
                else:
                    out_refs[at][...] = jnp.zeros((block, full_width), bf16)

    dw_ref[:, :, : 3 * width] = dw_s[...].astype(bf16).reshape(8, full_width // 8, 3 * width)
    side = jnp.concatenate([db_s[...], jnp.zeros((120, full_width), f32)], axis=0).T
    dw_ref[:, :, 3 * width :] = side.astype(bf16).reshape(8, full_width // 8, 128)


def whole():
    return pl.BlockSpec(memory_space=pltpu.VMEM)


def smem():
    return pl.BlockSpec(memory_space=pltpu.SMEM)


def raw():
    return pl.BlockSpec(memory_space=pl.ANY)


def attend_forward(span, mask, window, weight, biases):
    bounds, segq, segk = mask
    offsets, pieces = weight
    first, pairs = span
    count = len(window)
    block, full_width = window[0].shape
    width = pairs * PAIR
    padded = count * block + TK_FWD - ALIGN
    return pl.pallas_call(
        functools.partial(forward_kernel, count // 2, len(pieces), first),
        out_shape=(
            jax.ShapeDtypeStruct((block, width), bf16),
            jax.ShapeDtypeStruct((8, 2 * block), f32),
        ),
        in_specs=[smem()] * 2 + [whole()] * count + [raw()] * len(pieces) + [whole()] * 3,
        out_specs=(whole(), whole()),
        scratch_shapes=[
            pltpu.VMEM((full_width, 3 * width), bf16),
            pltpu.VMEM((block, width), bf16),
            pltpu.VMEM((2 * block, width), bf16),
            pltpu.VMEM((padded, width), bf16),
            pltpu.VMEM((padded, width), bf16),
            pltpu.VMEM((8, 2 * block), f32),
            pltpu.VMEM((8, 2 * block), f32),
            pltpu.VMEM((pairs, PAIR, 2 * block), f32),
            pltpu.SemaphoreType.DMA((len(pieces), 3)),
        ],
        compiler_params=pltpu.CompilerParams(vmem_limit_bytes=VMEM_LIMIT),
        cost_estimate=pl.CostEstimate(
            flops=2_500_000_000 * pairs, bytes_accessed=8_000_000, transcendentals=4_000_000
        ),
        name="attend_forward",
    )(bounds, offsets, *window, *pieces, biases, segq, segk)


def attend_backward(span, mask, window, weight, biases, attended, grad, before):
    bounds, segq, segk = mask
    offsets, pieces = weight
    first, pairs = span
    count = len(window)
    block, full_width = window[0].shape
    width = pairs * PAIR
    hops = count // 2
    padded = count * block + TK_BWD - ALIGN
    per_part = full_width // PAIR // len(attended)
    mixed, lse = attended[first // per_part]
    at = first // per_part * per_part
    outs = [
        jax.ShapeDtypeStruct((block, full_width), f32 if at == hops else bf16) for at in range(count)
    ]
    return pl.pallas_call(
        functools.partial(backward_kernel, hops, len(pieces), len(before), first, first - at),
        out_shape=(
            *outs,
            jax.ShapeDtypeStruct((8, full_width // 8, 3 * width + 128), bf16),
        ),
        in_specs=[smem()] * 2
        + [whole()] * count
        + [raw()] * len(pieces)
        + [whole()] * (6 + len(before)),
        out_specs=(whole(),) * (count + 1),
        scratch_shapes=[
            pltpu.VMEM((full_width, 3 * width), bf16),
            pltpu.VMEM((block, width), bf16),
            pltpu.VMEM((2 * block, width), bf16),
            pltpu.VMEM((2 * block, width), bf16),
            pltpu.VMEM((padded, width), bf16),
            pltpu.VMEM((padded, width), bf16),
            pltpu.VMEM((padded, width), f32),
            pltpu.VMEM((padded, width), f32),
            pltpu.VMEM((full_width, 3 * width), f32),
            pltpu.VMEM((8, 2 * block), f32),
            pltpu.VMEM((pairs, PAIR, 2 * block), f32),
            pltpu.VMEM((8, full_width), f32),
            pltpu.SemaphoreType.DMA((len(pieces), 3)),
        ],
        compiler_params=pltpu.CompilerParams(vmem_limit_bytes=VMEM_LIMIT),
        cost_estimate=pl.CostEstimate(
            flops=5_000_000_000 * pairs, bytes_accessed=20_000_000, transcendentals=4_000_000
        ),
        name="attend_backward",
    )(bounds, offsets, *window, *pieces, biases, segq, segk, mixed, lse, grad, *before)


def join(refs):
    if len(refs) == 1:
        return refs[0][...]
    return jnp.concatenate([ref[...] for ref in refs], axis=1)


def middle_kernel(
    counts, offsets, tokens_ref, cot_ref, vec_ref, upb_ref, *refs
):
    n_mixed, n_shared, n_down = counts
    mixed_refs, refs = refs[:n_mixed], refs[n_mixed:]
    out_own, up_own, refs = refs[0], refs[1], refs[2:]
    shared, down_p, refs = refs[:n_shared], refs[n_shared : n_shared + n_down], refs[n_shared + n_down :]
    (
        result_ref, one_ref, mixed_ref, branch_ref, hidden_ref, inner_ref, act_ref, two_ref,
        small_ref, gupb_ref,
    ) = refs[:10]
    wo_s, up_s, down_s, slope_s, sems = refs[10:]
    width = wo_s.shape[1]
    out_copies, up_copies, down_copies = [], [], []

    def begin(copies, at, source, target):
        row = pl.multiple_of(offsets[at], ROW_STEP)
        copy = pltpu.make_async_copy(
            source, target.at[pl.ds(row, source.shape[0]), :], sems.at[at, len(copies) % 2]
        )
        copy.start()
        copies.append(copy)

    begin(out_copies, 0, out_own, wo_s)
    for at, piece in enumerate(shared):
        row = pl.multiple_of(offsets[2 + at], ROW_STEP)
        copy = pltpu.make_async_copy(
            piece.at[:, pl.ds(0, width)], wo_s.at[pl.ds(row, piece.shape[0]), :], sems.at[2 + at, 0]
        )
        copy.start()
        out_copies.append(copy)
    begin(up_copies, 1, up_own, up_s)
    for at, piece in enumerate(shared):
        row = pl.multiple_of(offsets[2 + at], ROW_STEP)
        copy = pltpu.make_async_copy(
            piece.at[:, pl.ds(width, up_s.shape[1])],
            up_s.at[pl.ds(row, piece.shape[0]), :],
            sems.at[2 + at, 1],
        )
        copy.start()
        up_copies.append(copy)
    for at, piece in enumerate(down_p):
        row = pl.multiple_of(offsets[2 + n_shared + at], ROW_STEP)
        copy = pltpu.make_async_copy(
            piece, down_s.at[pl.ds(row, piece.shape[0]), :], sems.at[2 + n_shared + at, 0]
        )
        copy.start()
        down_copies.append(copy)
    inner_width = up_s.shape[1]
    tile = inner_width // FF_TILES
    out_bias, norm_gain, norm_shift = vec_ref[0:1, :], vec_ref[1:2, :], vec_ref[2:3, :]
    down_bias, final_gain, final_shift = vec_ref[3:4, :], vec_ref[4:5, :], vec_ref[5:6, :]
    wait_all(out_copies)
    values = tokens_ref[...].astype(f32) + (nn(join(mixed_refs), wo_s[...]) + out_bias)
    centered = values - jnp.mean(values, axis=1, keepdims=True)
    inverse_one = lax.rsqrt(jnp.mean(centered * centered, axis=1, keepdims=True) + epsilon)
    normed_one = centered * inverse_one
    hidden = normed_one * norm_gain + norm_shift
    hidden_low = hidden.astype(bf16)
    hidden_ref[...] = hidden_low
    wait_all(up_copies)
    branch_two = None
    for at in range(FF_TILES):
        cols = slice(at * tile, (at + 1) * tile)
        inner = nn(hidden_low, up_s[:, cols]) + upb_ref[0:1, cols]
        normal = 0.5 * (1.0 + lax.erf(inner * 0.7071067811865476))
        density = jnp.exp(-0.5 * inner * inner) * 0.3989422804014327
        slope_s[:, cols] = normal + inner * density
        activated = (inner * normal).astype(bf16)
        act_ref[:, cols] = activated
        if at == 0:
            wait_all(down_copies)
        term = nn(activated, down_s[cols, :])
        branch_two = term if branch_two is None else branch_two + term
    values = hidden + (branch_two + down_bias)
    centered = values - jnp.mean(values, axis=1, keepdims=True)
    inverse_two = lax.rsqrt(jnp.mean(centered * centered, axis=1, keepdims=True) + epsilon)
    normed_two = centered * inverse_two
    result_ref[...] = (normed_two * final_gain + final_shift).astype(bf16)
    cot = cot_ref[...].astype(f32)
    small_ref[4:5, :] = jnp.sum(cot * normed_two, axis=0, keepdims=True)
    small_ref[5:6, :] = jnp.sum(cot, axis=0, keepdims=True)
    scaled = cot * final_gain
    first = jnp.mean(scaled, axis=1, keepdims=True)
    second = jnp.mean(scaled * normed_two, axis=1, keepdims=True)
    grad_two = inverse_two * (scaled - first - normed_two * second)
    grad_low = grad_two.astype(bf16)
    two_ref[...] = grad_low
    small_ref[3:4, :] = jnp.sum(grad_low.astype(f32), axis=0, keepdims=True)
    grad_hidden = grad_two
    gupb_ref[...] = jnp.zeros(gupb_ref.shape, f32)
    for at in range(FF_TILES):
        cols = slice(at * tile, (at + 1) * tile)
        grad_inner = (nt(grad_low, down_s[cols, :]) * slope_s[:, cols]).astype(bf16)
        inner_ref[:, cols] = grad_inner
        gupb_ref[0:1, cols] = jnp.sum(grad_inner.astype(f32), axis=0, keepdims=True)
        grad_hidden = grad_hidden + nt(grad_inner, up_s[:, cols])
    small_ref[1:2, :] = jnp.sum(grad_hidden * normed_one, axis=0, keepdims=True)
    small_ref[2:3, :] = jnp.sum(grad_hidden, axis=0, keepdims=True)
    scaled = grad_hidden * norm_gain
    first = jnp.mean(scaled, axis=1, keepdims=True)
    second = jnp.mean(scaled * normed_one, axis=1, keepdims=True)
    grad_one = inverse_one * (scaled - first - normed_one * second)
    one_ref[...] = grad_one
    grad_branch = grad_one.astype(bf16)
    branch_ref[...] = grad_branch
    small_ref[0:1, :] = jnp.sum(grad_branch.astype(f32), axis=0, keepdims=True)
    small_ref[6:8, :] = jnp.zeros((2, small_ref.shape[1]), f32)
    mixed_ref[...] = nt(grad_branch, wo_s[...]).astype(bf16)


def middle(attended, tokens, cotangent, weights, vectors, up_bias):
    offsets, out_own, up_own, shared, down = weights
    counts = (len(attended), len(shared), len(down))
    pieces = [out_own, up_own, *shared, *down]
    block, width = tokens.shape
    inner_width = up_bias.shape[1]
    return pl.pallas_call(
        functools.partial(middle_kernel, counts),
        out_shape=(
            jax.ShapeDtypeStruct((block, width), bf16),
            jax.ShapeDtypeStruct((block, width), f32),
            jax.ShapeDtypeStruct((block, width), bf16),
            jax.ShapeDtypeStruct((block, width), bf16),
            jax.ShapeDtypeStruct((block, width), bf16),
            jax.ShapeDtypeStruct((block, inner_width), bf16),
            jax.ShapeDtypeStruct((block, inner_width), bf16),
            jax.ShapeDtypeStruct((block, width), bf16),
            jax.ShapeDtypeStruct((8, width), f32),
            jax.ShapeDtypeStruct((8, inner_width), f32),
        ),
        in_specs=[smem()] + [whole()] * (4 + len(attended)) + [raw()] * len(pieces),
        out_specs=(whole(),) * 10,
        scratch_shapes=[
            pltpu.VMEM((width, width), bf16),
            pltpu.VMEM((width, inner_width), bf16),
            pltpu.VMEM((inner_width, width), bf16),
            pltpu.VMEM((block, inner_width), f32),
            pltpu.SemaphoreType.DMA((len(pieces), 2)),
        ],
        compiler_params=pltpu.CompilerParams(vmem_limit_bytes=VMEM_LIMIT),
        cost_estimate=pl.CostEstimate(flops=24_000_000_000, bytes_accessed=20_000_000, transcendentals=4_000_000),
        name="middle",
    )(offsets, tokens, cotangent, vectors, up_bias, *attended, *pieces)


def grad_down_kernel(micro, *refs):
    act_refs, two_refs, side_ref, out_ref = refs[:micro], refs[micro : 2 * micro], refs[-2], refs[-1]
    total = sum(tn(act[...], two[...]) for act, two in zip(act_refs, two_refs))
    rows, width = total.shape
    parts = out_ref.shape[0]
    out_ref[:, :, :width] = total.astype(bf16).reshape(parts, rows // parts, width)
    side = jnp.concatenate([side_ref[...], jnp.zeros((120, rows), f32)], axis=0).T
    out_ref[:, :, width:] = side.astype(bf16).reshape(parts, rows // parts, 128)


def weight_grad_down(activated, grad_low, side):
    micro = len(activated)
    block, inner_width = activated[0].shape
    width = grad_low[0].shape[1]
    tile = inner_width // FF_TILES
    return pl.pallas_call(
        functools.partial(grad_down_kernel, micro),
        out_shape=jax.ShapeDtypeStruct((8, inner_width // 8, width + 128), bf16),
        grid=(FF_TILES,),
        in_specs=[pl.BlockSpec((block, tile), lambda at: (0, at))] * micro
        + [pl.BlockSpec((block, width), lambda at: (0, 0))] * micro
        + [pl.BlockSpec((8, tile), lambda at: (0, at))],
        out_specs=pl.BlockSpec((8 // FF_TILES, inner_width // 8, width + 128), lambda at: (at, 0, 0)),
        compiler_params=pltpu.CompilerParams(vmem_limit_bytes=VMEM_LIMIT),
        cost_estimate=pl.CostEstimate(flops=5_400_000_000, bytes_accessed=14_000_000, transcendentals=0),
        name="weight_grad_down",
    )(*activated, *grad_low, side)


def grad_up_kernel(micro, counts, *refs):
    hidden, inner = refs[:micro], refs[micro : 2 * micro]
    out_ref, refs = refs[-1], refs[2 * micro : -1]
    if not counts:
        total = sum(tn(one[...], two[...]) for one, two in zip(hidden, inner))
        out_ref[...] = total.astype(bf16).reshape(out_ref.shape)
        return
    branch, refs = refs[:micro], refs[micro:]
    mixed = []
    for size in counts:
        mixed.append(refs[:size])
        refs = refs[size:]
    last = pl.num_programs(0) - 1

    @pl.when(pl.program_id(0) < last)
    def _():
        total = sum(tn(one[...], two[...]) for one, two in zip(hidden, inner))
        out_ref[...] = total.astype(bf16).reshape(out_ref.shape)

    @pl.when(pl.program_id(0) == last)
    def _():
        total = sum(tn(join(one), two[...]) for one, two in zip(mixed, branch))
        out_ref[...] = total.astype(bf16).reshape(out_ref.shape)


def weight_grad_up(hidden_low, grad_inner, first, tiles, attended=(), grad_branch=()):
    micro = len(hidden_low)
    block, width = hidden_low[0].shape
    steps = tiles + (1 if attended else 0)
    fixed = [pl.BlockSpec((block, width), lambda at: (0, 0))] * micro
    parts = [part for one in attended for part in one]
    return pl.pallas_call(
        functools.partial(grad_up_kernel, micro, tuple(len(one) for one in attended)),
        out_shape=jax.ShapeDtypeStruct((8, width // 8, steps * width), bf16),
        grid=(steps,),
        in_specs=fixed
        + [pl.BlockSpec((block, width), lambda at: (0, first + jnp.minimum(at, tiles - 1)))] * micro
        + (fixed if attended else [])
        + [pl.BlockSpec(part.shape, lambda at: (0, 0)) for part in parts],
        out_specs=pl.BlockSpec((8, width // 8, width), lambda at: (0, 0, at)),
        compiler_params=pltpu.CompilerParams(vmem_limit_bytes=VMEM_LIMIT),
        cost_estimate=pl.CostEstimate(
            flops=1_400_000_000 * steps, bytes_accessed=3_000_000 * steps, transcendentals=0
        ),
        name="weight_grad_up",
    )(*hidden_low, *grad_inner, *grad_branch, *parts)


def permute(value, axis, pairs):
    return lax.ppermute(value, axis, pairs)


def swap_pairs(size, distance):
    return [(at, at ^ distance) for at in range(size)]


def shift_pairs(size, by):
    return [(at, at + by) for at in range(size) if 0 <= at + by < size]


def pick(array, index, axis=0):
    return lax.dynamic_index_in_dim(array, index, axis, keepdims=False)


def ordered(first_here, mine, other, axis=0):
    first = jnp.where(first_here, mine, other)
    second = jnp.where(first_here, other, mine)
    return jnp.concatenate([first, second], axis=axis)


def two_level(mesh_shape):
    return mesh_shape["replica"] == 4 and mesh_shape["fsdp"] == 2 and mesh_shape["seq"] == 4


def sync(*values):
    return lax.optimization_barrier(values)


class Fetch:
    def __init__(self, fast):
        self.fast = fast
        self.here = lax.axis_index("fsdp")
        self.spot = 2 * lax.axis_index("x") + lax.axis_index("core") if fast else None

    def quarter(self, shard):
        if not self.fast:
            return shard
        size = shard.shape[0] // 4
        return lax.dynamic_slice_in_dim(shard, self.spot * size, size, 0)

    def far(self, quarter):
        if not self.fast:
            return [lax.all_gather(quarter, "fsdp", axis=0, tiled=True)]
        return [permute(quarter, "fsdp", swap_pairs(2, 1))]

    def across(self, held):
        if not self.fast:
            return held
        return held + [permute(held[0], "x", swap_pairs(2, 1)), permute(held[0], "core", swap_pairs(2, 1))]

    def corner(self, held):
        if not self.fast:
            return held
        return held + [permute(held[1], "core", swap_pairs(2, 1))]

    def offsets(self, rows):
        size = rows // 4
        there = (1 - self.here) * rows
        return [self.here * rows], [there + (self.spot ^ flip) * size for flip in (0, 2, 1, 3)]

    def one_weight(self, shard, held):
        if not self.fast:
            return jnp.zeros((1,), jnp.int32), held
        mine, others = self.offsets(shard.shape[0])
        return jnp.stack(mine + others).astype(jnp.int32), [shard] + held

    def middle_weights(self, out_shard, up_shard, down_shard, shared, down):
        if not self.fast:
            width = shared[0].shape[0]
            return (jnp.zeros((3,), jnp.int32), shared[0][:, :width], shared[0][:, width:], [], down)
        mine, others = self.offsets(out_shard.shape[0])
        own, rest = self.offsets(down_shard.shape[0])
        offsets = jnp.stack(mine + mine + others + own + rest).astype(jnp.int32)
        return offsets, out_shard, up_shard, shared, [down_shard] + down

    def vectors(self, shards):
        if not self.fast:
            return [lax.all_gather(shard, "fsdp", axis=0, tiled=True) for shard in shards]
        far = permute(jnp.concatenate(shards), "fsdp", swap_pairs(2, 1))
        full, at = [], 0
        for shard in shards:
            size = shard.shape[0]
            full.append(ordered(self.here == 0, shard, far[at : at + size]))
            at += size
        return full


def add_low(left, right):
    return (left.astype(f32) + right.astype(f32)).astype(bf16)


class Chain:
    def __init__(self, fast, parts):
        self.fast = fast
        self.name = None
        self.pair = parts.reshape(2, 2, 2, *parts.shape[1:]) if fast else parts

    def settle(self):
        name, pair = self.name, self.pair
        if name is None:
            return pair
        if name in ("core", "y", "x", "z1", "z2"):
            return add_low(*pair)
        if name == "z3":
            return ordered(lax.axis_index("seq") % 2 == 0, *pair)
        if name == "spread_x":
            return both_ways(lax.axis_index("x") == 0, *pair)
        return both_ways(lax.axis_index("core") == 0, *pair)

    def go(self, name):
        if not self.fast:
            return
        held = self.settle()
        self.name = name
        if name == "core":
            here, axis, dim = lax.axis_index("core"), "core", 1
        elif name == "y":
            here, axis, dim = lax.axis_index("fsdp"), "fsdp", 0
        elif name == "x":
            here, axis, dim = lax.axis_index("x"), "x", 0
        elif name == "z1":
            here, axis, dim = lax.axis_index("seq") % 2, "seq", 0
            held = held.reshape(2, held.shape[0] // 2, held.shape[1])
        else:
            axis = {"z2": "seq", "z3": "seq", "spread_x": "x", "spread_core": "core"}[name]
            pairs = {"z2": swap_pairs(4, 2), "z3": swap_pairs(4, 1)}.get(name, swap_pairs(2, 1))
            self.pair = (held, permute(held, axis, pairs))
            return
        pairs = swap_pairs(4 if axis == "seq" else 2, 1)
        self.pair = (pick(held, here, dim), permute(pick(held, 1 - here, dim), axis, pairs))

    def final(self):
        if not self.fast:
            parts = self.pair
            share = lax.psum_scatter(
                parts.reshape(-1, parts.shape[2]), "fsdp", scatter_dimension=0, tiled=True
            )
            return lax.psum(share, ("replica", "seq")).astype(f32)
        full = self.settle()
        return full.reshape(-1, full.shape[-1]).astype(f32)


def both_ways(first_here, mine, other):
    return jnp.stack([jnp.where(first_here, mine, other), jnp.where(first_here, other, mine)])


def settle_all(chains, *values):
    pairs, *values = sync([chain.pair for chain in chains], *values)
    for chain, pair in zip(chains, pairs):
        chain.pair = pair
    return values


def body(
    fast,
    tokens,
    segment_ids,
    joined_weight,
    query_bias,
    value_bias,
    out_weight,
    out_bias,
    norm_gain,
    norm_shift,
    up_weight,
    up_bias,
    down_weight,
    down_bias,
    final_gain,
    final_shift,
    cotangent,
):
    micro, block, width = tokens.shape[1:]
    length = segment_ids.shape[-1]
    size = lax.axis_size("seq")
    place = lax.axis_index("seq")
    hops = min(size - 1, (length // 2 - 2) // block + 1)
    count = 2 * hops + 1
    inner_width = up_weight.shape[1]
    all_pairs = width // PAIR
    half_pairs = all_pairs // 2
    spans = [(0, half_pairs), (half_pairs, half_pairs)]
    fetch = Fetch(fast)

    masks = []
    for batch in range(micro):
        ids = segment_ids[0, batch]
        padded = jnp.concatenate(
            [jnp.full((hops * block,), -1, jnp.int32), ids, jnp.full((hops * block,), 1000, jnp.int32)]
        )
        near = lax.dynamic_slice_in_dim(padded, place * block, count * block, 0)
        rows = lax.dynamic_slice_in_dim(ids, place * block, block, 0)
        bounds = jnp.stack([jnp.sum(near < rows[0]), jnp.sum(near <= rows[-1])]).astype(jnp.int32)
        segq = jnp.broadcast_to(rows[None, :], (8, block))
        tail = jnp.full((TK_FWD - ALIGN,), 1000, jnp.int32)
        segk = jnp.broadcast_to(jnp.concatenate([near, tail])[:, None], (count * block + TK_FWD - ALIGN, 128))
        masks.append((bounds, segq, segk))

    def hop_out(moved):
        left, right = moved
        return (
            left + [permute(left[-1], "seq", shift_pairs(size, 1))],
            right + [permute(right[-1], "seq", shift_pairs(size, -1))],
        )

    def window(moved):
        left, right = moved
        return left[:0:-1] + [left[0]] + right[1:]

    own = [tokens[0, batch] for batch in range(micro)]
    moves = [([one], [one]) for one in own]
    moves[0] = hop_out(moves[0])
    joined = fetch.far(fetch.quarter(joined_weight))
    vectors = fetch.vectors(
        [
            query_bias,
            value_bias,
            out_bias,
            norm_gain,
            norm_shift,
            down_bias,
            final_gain,
            final_shift,
            up_bias,
        ]
    )
    biases = jnp.pad(jnp.stack(vectors[:2]).astype(f32), ((0, 6), (0, 0)))
    rows_six = jnp.pad(jnp.stack(vectors[2:8]).astype(f32), ((0, 2), (0, 0)))
    up_row = jnp.pad(vectors[8].astype(f32)[None, :], ((0, 7), (0, 0)))
    quarters = [
        jnp.concatenate([fetch.quarter(out_weight), fetch.quarter(up_weight)], axis=1),
        fetch.quarter(down_weight),
    ]
    moves[0], joined, quarters, own, biases, rows_six, up_row, masks = sync(
        moves[0], joined, quarters, own, biases, rows_six, up_row, masks
    )

    for _ in range(hops - 1):
        moves[0] = hop_out(moves[0])
    joined = fetch.across(joined)
    shared = fetch.far(quarters[0])
    moves[0], joined, quarters[1] = sync(moves[0], joined, quarters[1])
    joined = fetch.corner(joined)
    moves[0], joined, shared, quarters[1] = sync(moves[0], joined, shared, quarters[1])

    attended = [[] for _ in range(micro)]
    windows = [window(moves[0])] + [None] * (micro - 1)
    weight = fetch.one_weight(joined_weight, joined)
    for batch in range(1, micro):
        moves[batch] = ([own[batch]], [own[batch]])

    nxt = min(1, micro - 1)
    if micro > 1:
        moves[1] = hop_out(moves[1])
    shared = fetch.across(shared)
    down = fetch.far(quarters[1])
    attended[0].append(tuple(attend_forward(spans[0], masks[0], windows[0], weight, biases)))
    attended[0], moves[nxt], shared, down, masks, windows[0] = sync(
        attended[0], moves[nxt], shared, down, masks, windows[0]
    )
    for _ in range(hops - 1 if micro > 1 else 0):
        moves[1] = hop_out(moves[1])
    shared = fetch.corner(shared)
    down = fetch.across(down)
    attended[0].append(tuple(attend_forward(spans[1], masks[0], windows[0], weight, biases)))
    attended[0], moves[nxt], shared, down = sync(attended[0], moves[nxt], shared, down)
    down = fetch.corner(down)
    attended[0], down, own = sync(attended[0], down, own)
    middle_weights = fetch.middle_weights(out_weight, up_weight, down_weight, shared, down)

    middles = []
    for batch in range(micro):
        later = batch + 2
        if batch > 0:
            windows[batch] = window(moves[batch])
            if batch + 1 < micro:
                for _ in range(hops - 1):
                    moves[batch + 1] = hop_out(moves[batch + 1])
            attended[batch].append(
                tuple(attend_forward((0, all_pairs), masks[batch], windows[batch], weight, biases))
            )
            if batch + 1 < micro:
                attended[batch], moves[batch + 1] = sync(attended[batch], moves[batch + 1])
        if later < micro:
            moves[later] = hop_out(moves[later])
        middles.append(
            middle(
                [one[0] for one in attended[batch]],
                own[batch],
                cotangent[0, batch],
                middle_weights,
                rows_six,
                up_row,
            )
        )
        if later < micro:
            middles[-1], moves[later], masks = sync(middles[-1], moves[later], masks)
        else:
            middles[-1], masks = sync(middles[-1], masks)

    outs = list(zip(*middles))
    small = sum(outs[8])
    grad_upb = sum(outs[9])
    half = width // 2
    gap = inner_width // 2 - half
    spread = jnp.pad(small[:6].reshape(6, 2, half), ((0, 0), (0, 0), (0, gap))).reshape(6, inner_width)
    side = jnp.concatenate([grad_upb[:1], spread, jnp.zeros((1, inner_width), f32)], axis=0)
    down = Chain(fast, weight_grad_down(outs[6], outs[7], side))
    up_ins = (outs[4], outs[5], [[part[0] for part in one] for one in attended], outs[3])
    (up_ins,) = settle_all([down], up_ins)
    down.go("core")
    tiles = inner_width // width
    up_one = Chain(fast, weight_grad_up(up_ins[0], up_ins[1], 0, tiles // 2))
    (up_ins,) = settle_all([down, up_one], up_ins)
    down.go("y")
    up_one.go("core")
    up_two = Chain(
        fast, weight_grad_up(up_ins[0], up_ins[1], tiles // 2, tiles - tiles // 2, up_ins[2], up_ins[3])
    )
    (masks,) = settle_all([up_one, up_two], list(masks))

    backs = [None] * micro
    coming = [None] * micro
    joined_sums = [[], []]
    last = micro - 1

    def run_back(which, batch, chains, moving=()):
        before = [outs[1][batch]] if which == 0 else backs[batch]
        *parts, grad_joined = attend_backward(
            spans[which], masks[batch], windows[batch], weight, biases, attended[batch], outs[2][batch], before
        )
        moved = [coming[at] for at in moving]
        backs[batch], grad_joined, masks[:], moved = settle_all(chains, parts, grad_joined, list(masks), moved)
        for at, one in zip(moving, moved):
            coming[at] = one
        joined_sums[which].append(grad_joined)

    def hop_back(batch, step):
        far = hops - step
        sent = []
        for at, by, sign in ((0, 1, 1), (1, -1, -1)):
            part = backs[batch][hops + sign * far]
            if step > 0:
                part = add_low(part, coming[batch][at])
            sent.append(permute(part, "seq", shift_pairs(size, by)))
        coming[batch] = sent

    def total_of(which):
        return Chain(fast, sum(part.astype(f32) for part in joined_sums[which]).astype(bf16))

    up_two.go("core")
    run_back(0, 0, [up_two, down])
    down.go("x")
    up_one.go("y")
    run_back(1, 0, [down, up_one])
    down.go("z1")
    up_one.go("x")
    up_two.go("y")
    hop_back(0, 0)
    run_back(0, 1, [down, up_one, up_two], [0])
    down.go("z2")
    up_one.go("z1")
    up_two.go("x")
    for step in range(1, hops):
        hop_back(0, step)
    for batch in range(2, micro):
        run_back(0, batch, [down, up_one, up_two], [0])
    joined_one = total_of(0)
    joined_one.go("core")
    down.go("z3")
    up_one.go("z2")
    up_two.go("z1")
    for batch in range(1, last):
        run_back(1, batch, [down, up_one, up_two, joined_one])
        hop_back(batch, 0)
    joined_one.go("y")
    down.go("spread_x")
    up_one.go("z3")
    up_two.go("z2")
    run_back(1, last, [down, up_one, up_two, joined_one], list(range(1, last)))

    joined_two = total_of(1)
    joined_two.go("core")
    joined_one.go("x")
    hop_back(last, 0)
    (coming,) = settle_all([joined_two, joined_one], coming)
    joined_two.go("y")
    joined_one.go("z1")
    up_two.go("z3")
    down.go("spread_core")
    up_one.go("spread_x")
    (coming, backs) = settle_all([joined_two, joined_one, up_two, down, up_one], coming, backs)
    joined_two.go("x")
    joined_one.go("z2")
    for batch in range(1, micro):
        for step in range(1, hops):
            hop_back(batch, step)
    up_one.go("spread_core")
    up_two.go("spread_x")
    settle_all([joined_two, joined_one])
    joined_two.go("z1")
    joined_one.go("z3")
    settle_all([joined_two, joined_one, up_two])
    joined_two.go("z2")
    joined_one.go("spread_x")
    up_two.go("spread_core")
    settle_all([joined_two, joined_one])
    joined_two.go("z3")
    joined_one.go("spread_core")
    settle_all([joined_two])
    joined_two.go("spread_x")
    joined_two.go("spread_core")

    final_down = down.final()
    final_up_one, final_up_two = up_one.final(), up_two.final()
    final_up = jnp.concatenate([final_up_one, final_up_two[:, : inner_width - final_up_one.shape[1]]], axis=1)
    final_out = final_up_two[:, inner_width - final_up_one.shape[1] :]
    final_a, final_b = joined_one.final(), joined_two.final()
    grad_tokens = []
    for batch in range(micro):
        total = backs[batch][hops] + coming[batch][0].astype(f32) + coming[batch][1].astype(f32)
        grad_tokens.append(total.astype(bf16))
    low, high = spans[0][1] * PAIR, spans[1][1] * PAIR
    final_joined = jnp.concatenate(
        [
            part
            for at in range(3)
            for part in (final_a[:, at * low : (at + 1) * low], final_b[:, at * high : (at + 1) * high])
        ],
        axis=1,
    )
    bias_sums = final_a[:, 3 * low : 3 * low + 2] + final_b[:, 3 * high : 3 * high + 2]
    if fast:
        own_rows = width // lax.axis_size("fsdp")
        smalls = [final_down[:own_rows, width + 1 + at] for at in range(6)]
    else:
        smalls = [
            lax.psum_scatter(lax.psum(small[at], ("replica", "seq")), "fsdp", scatter_dimension=0, tiled=True)
            for at in range(6)
        ]
    return (
        jnp.stack(outs[0], axis=0)[None],
        jnp.stack(grad_tokens, axis=0)[None],
        final_joined,
        bias_sums[:, 0],
        bias_sums[:, 1],
        final_out,
        smalls[0],
        smalls[1],
        smalls[2],
        final_up,
        final_down[:, width],
        final_down[:, :width],
        smalls[3],
        smalls[4],
        smalls[5],
    )


def solution(mesh):
    fast = two_level(dict(mesh.shape))
    groups = ("replica", "fsdp")
    if fast:
        mesh = jax.sharding.Mesh(mesh.devices.reshape(2, 2, 2, 4), ("x", "core", "fsdp", "seq"))
        groups = ("x", "core", "fsdp")
    rows = P(groups, None, "seq", None)
    matrix, vector = P("fsdp", None), P("fsdp")
    in_specs = (
        rows,
        P(groups, None, None),
        matrix,
        vector,
        vector,
        matrix,
        vector,
        vector,
        vector,
        matrix,
        vector,
        matrix,
        vector,
        vector,
        vector,
        rows,
    )
    out_specs = (
        rows,
        rows,
        matrix,
        vector,
        vector,
        matrix,
        vector,
        vector,
        vector,
        matrix,
        vector,
        matrix,
        vector,
        vector,
        vector,
    )
    return jax.shard_map(
        functools.partial(body, fast),
        mesh=mesh,
        in_specs=in_specs,
        out_specs=out_specs,
        check_vma=False,
    )
```

```python
import functools
import jax
import jax.numpy as jnp
from jax import lax
from jax.experimental import pallas as pl
from jax.experimental.pallas import tpu as pltpu
from jax.sharding import PartitionSpec as P

HEADS = 12
HEAD_DIM = 64
PAIR = 2 * HEAD_DIM
epsilon = 1e-05
masked_score = -1e30
scale = HEAD_DIM ** (-0.5)
TK_FWD = 256
TK_BWD = 256
ALIGN = 128
ROW_STEP = 16
VMEM_LIMIT = 62 * 1024 * 1024
FF_TILES = 4
f32 = jnp.float32
bf16 = jnp.bfloat16


def nt(left, right):
    return lax.dot_general(left, right, (((1,), (1,)), ((), ())), preferred_element_type=f32)


def tn(left, right):
    return lax.dot_general(left, right, (((0,), (0,)), ((), ())), preferred_element_type=f32)


def nn(left, right):
    return lax.dot_general(left, right, (((1,), (0,)), ((), ())), preferred_element_type=f32)


def stack_heads(pair):
    lane = lax.broadcasted_iota(jnp.int32, pair.shape, 1)
    zero = jnp.zeros_like(pair)
    return jnp.concatenate(
        [jnp.where(lane < HEAD_DIM, pair, zero), jnp.where(lane < HEAD_DIM, zero, pair)], axis=0
    )


def unstack_heads(rows):
    half = rows.shape[0] // 2
    lane = lax.broadcasted_iota(jnp.int32, (half, rows.shape[1]), 1)
    return jnp.where(lane < HEAD_DIM, rows[:half], rows[half:])


def split_pieces(refs):
    pieces = []
    for ref in refs:
        if len(ref.shape) == 2:
            pieces.append(ref)
        else:
            pieces.extend(ref.at[at] for at in range(ref.shape[0]))
    return pieces


def count_pieces(arrays):
    return sum(1 if len(one.shape) == 2 else one.shape[0] for one in arrays)


def start_columns(offsets, piece_refs, full_s, sems, width, at_col, size_col):
    copies = []
    for at, piece in enumerate(split_pieces(piece_refs)):
        size = piece.shape[0]
        row = pl.multiple_of(offsets[at], ROW_STEP)
        for part in range(3):
            copy = pltpu.make_async_copy(
                piece.at[:, pl.ds(part * width + at_col, size_col)],
                full_s.at[pl.ds(row, size), pl.ds(part * size_col, size_col)],
                sems.at[at, part],
            )
            copy.start()
            copies.append(copy)
    return copies


def wait_all(copies):
    for copy in copies:
        copy.wait()


def project_window(bounds, x_refs, w_ref, bias_ref, cols, k_s, v_s, tail):
    block = x_refs[0].shape[0]
    width = k_s.shape[1]
    lo, hi = bounds[0], bounds[1]
    for at, x_ref in enumerate(x_refs):
        rows = pl.ds(at * block, block)
        active = (hi > at * block) & (lo < (at + 1) * block)

        @pl.when(active)
        def _():
            x = x_ref[...]
            k_s[rows, :] = nn(x, w_ref[:, width : 2 * width]).astype(bf16)
            v_s[rows, :] = (nn(x, w_ref[:, 2 * width :]) + bias_ref[1:2, cols]).astype(bf16)

        @pl.when(jnp.logical_not(active))
        def _():
            k_s[rows, :] = jnp.zeros((block, width), bf16)
            v_s[rows, :] = jnp.zeros((block, width), bf16)

    end = len(x_refs) * block
    k_s[end:, :] = jnp.zeros((tail, width), bf16)
    v_s[end:, :] = jnp.zeros((tail, width), bf16)


def tile_range(bounds, tk):
    low = bounds[0]
    high = bounds[1]
    start = (low // ALIGN) * ALIGN
    return start, (high - start + tk - 1) // tk


def project_queries(x_ref, w_ref, bias_ref, cols, q_s, qq_s):
    block = x_ref.shape[0]
    width = q_s.shape[1]
    q = nn(x_ref[...], w_ref[:, :width]) + bias_ref[0:1, cols]
    q_s[...] = q.astype(bf16) * jnp.asarray(scale, bf16)
    for pair in range(width // PAIR):
        here = slice(pair * PAIR, (pair + 1) * PAIR)
        qq_s[:, here] = stack_heads(q_s[:, here])


def forward_kernel(hops, pieces, first, bounds, offsets, *refs):
    count = 2 * hops + 1
    x_refs = refs[:count]
    w_refs, refs = refs[count : count + pieces], refs[count + pieces :]
    bias_ref, segq_ref, segk_ref, o_ref, lse_ref = refs[:5]
    w_ref, q_s, qq_s, k_s, v_s, top_s, sum_s, acc_s, sems = refs[5:]
    block, full_width = x_refs[0].shape
    width = o_ref.shape[1]
    tk = TK_FWD
    pairs = width // PAIR
    cols_all = slice(first * PAIR, first * PAIR + width)
    wait_all(start_columns(offsets, w_refs, w_ref, sems, full_width, first * PAIR, width))
    project_window(bounds, x_refs, w_ref, bias_ref, cols_all, k_s, v_s, tk - ALIGN)
    project_queries(x_refs[hops], w_ref, bias_ref, cols_all, q_s, qq_s)
    start, steps = tile_range(bounds, tk)
    segq = segq_ref[0:1, :]
    segq = jnp.concatenate([segq, segq], axis=1)
    top_s[...] = jnp.full(top_s.shape, masked_score, f32)
    sum_s[...] = jnp.ones(sum_s.shape, f32)
    sum_s[:pairs, :] = jnp.zeros((pairs, sum_s.shape[1]), f32)
    acc_s[...] = jnp.zeros(acc_s.shape, f32)

    @pl.loop(0, steps)
    def _(at):
        here = pl.ds(pl.multiple_of(start + at * tk, ALIGN), tk)
        allowed = segk_ref[here, 0:1] == segq
        for pair in range(pairs):
            cols = slice(pair * PAIR, (pair + 1) * PAIR)
            one = slice(pair, pair + 1)
            scores = nt(k_s[here, cols], qq_s[:, cols])
            scores = jnp.where(allowed, scores, masked_score)
            top = top_s[one, :]
            new_top = jnp.maximum(top, jnp.max(scores, axis=0, keepdims=True))
            fade = jnp.exp(top - new_top)
            weights = jnp.exp(scores - new_top)
            top_s[one, :] = new_top
            sum_s[one, :] = sum_s[one, :] * fade + jnp.sum(weights, axis=0, keepdims=True)
            acc_s[pair] = acc_s[pair] * fade + tn(v_s[here, cols], weights.astype(bf16))

    lse_ref[...] = top_s[...] + jnp.log(sum_s[...])
    for pair in range(pairs):
        cols = slice(pair * PAIR, (pair + 1) * PAIR)
        mixed = acc_s[pair] / sum_s[pair : pair + 1, :]
        o_ref[:, cols] = unstack_heads(mixed.T).astype(bf16)


def backward_kernel(hops, pieces, prev, first, skip, bounds, offsets, *refs):
    count = 2 * hops + 1
    x_refs = refs[:count]
    w_refs, refs = refs[count : count + pieces], refs[count + pieces :]
    bias_ref, segq_ref, segk_ref, o_ref, lse_ref, do_ref = refs[:6]
    prev_refs, refs = refs[6 : 6 + prev], refs[6 + prev :]
    out_refs, refs = refs[:count], refs[count:]
    dw_ref, w_ref, q_s, qq_s, gg_s, k_s, v_s, dk_s, dv_s, dw_s, stat_s, acc_s, db_s, sems = refs
    block, full_width = x_refs[0].shape
    width = q_s.shape[1]
    tk = TK_BWD
    pairs = width // PAIR
    cols_all = slice(first * PAIR, first * PAIR + width)
    copies = start_columns(offsets, w_refs, w_ref, sems, full_width, first * PAIR, width)
    dk_s[...] = jnp.zeros(dk_s.shape, f32)
    dv_s[...] = jnp.zeros(dv_s.shape, f32)
    acc_s[...] = jnp.zeros(acc_s.shape, f32)
    for pair in range(pairs):
        cols = slice(pair * PAIR, (pair + 1) * PAIR)
        far = slice((first + pair) * PAIR, (first + pair + 1) * PAIR)
        theirs = slice((skip + pair) * PAIR, (skip + pair + 1) * PAIR)
        grads = stack_heads(do_ref[:, far])
        gg_s[:, cols] = grads
        mixed = o_ref[:, theirs].astype(f32)
        product = grads.astype(f32) * jnp.concatenate([mixed, mixed], axis=0)
        stat_s[pair : pair + 1, :] = jnp.sum(product.T, axis=0, keepdims=True)
    wait_all(copies)
    project_window(bounds, x_refs, w_ref, bias_ref, cols_all, k_s, v_s, tk - ALIGN)
    project_queries(x_refs[hops], w_ref, bias_ref, cols_all, q_s, qq_s)
    lo, hi = bounds[0], bounds[1]
    actives = [(hi > at * block) & (lo < (at + 1) * block) for at in range(count)]
    start, steps = tile_range(bounds, tk)
    segq = segq_ref[0:1, :]
    segq = jnp.concatenate([segq, segq], axis=1)

    @pl.loop(0, steps)
    def _(at):
        here = pl.ds(pl.multiple_of(start + at * tk, ALIGN), tk)
        allowed = segk_ref[here, 0:1] == segq
        for pair in range(pairs):
            cols = slice(pair * PAIR, (pair + 1) * PAIR)
            keys = k_s[here, cols]
            queries = qq_s[:, cols]
            grads = gg_s[:, cols]
            scores = nt(keys, queries)
            scores = jnp.where(allowed, scores, masked_score)
            weights = jnp.exp(scores - lse_ref[skip + pair : skip + pair + 1, :])
            grad_weights = nt(v_s[here, cols], grads)
            grad_scores = (weights * (grad_weights - stat_s[pair : pair + 1, :])).astype(bf16)
            dv_s[here, cols] += nn(weights.astype(bf16), grads)
            dk_s[here, cols] += nn(grad_scores, queries)
            acc_s[pair] += tn(keys, grad_scores)

    for pair in range(pairs):
        cols = slice(pair * PAIR, (pair + 1) * PAIR)
        q_s[:, cols] = (unstack_heads(acc_s[pair].T) * scale).astype(bf16)
    dq = q_s[...]
    before = prev_refs[hops] if prev > 1 else prev_refs[0]
    dw_s[:, :width] = tn(x_refs[hops][...], dq)
    dw_s[:, width:] = jnp.zeros((full_width, 2 * width), f32)
    db_s[...] = jnp.zeros(db_s.shape, f32)
    db_s[0:1, cols_all] = jnp.sum(dq.astype(f32), axis=0, keepdims=True)
    out_refs[hops][...] = before[...] + nt(dq, w_ref[:, :width])
    for at in range(count):
        here = pl.ds(at * block, block)

        @pl.when(actives[at])
        def _():
            x = x_refs[at][...]
            dk = dk_s[here, :].astype(bf16)
            dv = dv_s[here, :].astype(bf16)
            db_s[1:2, cols_all] += jnp.sum(dv.astype(f32), axis=0, keepdims=True)
            back = nt(dk, w_ref[:, width : 2 * width]) + nt(dv, w_ref[:, 2 * width :])
            if at == hops:
                out_refs[at][...] += back
            else:
                if prev > 1:
                    back = back + prev_refs[at][...].astype(f32)
                out_refs[at][...] = back.astype(bf16)
            dw_s[:, width : 2 * width] += tn(x, dk)
            dw_s[:, 2 * width :] += tn(x, dv)

        if at != hops:
            @pl.when(jnp.logical_not(actives[at]))
            def _():
                if prev > 1:
                    out_refs[at][...] = prev_refs[at][...]
                else:
                    out_refs[at][...] = jnp.zeros((block, full_width), bf16)

    dw_ref[:, :, : 3 * width] = dw_s[...].astype(bf16).reshape(8, full_width // 8, 3 * width)
    side = jnp.concatenate([db_s[...], jnp.zeros((120, full_width), f32)], axis=0).T
    dw_ref[:, :, 3 * width :] = side.astype(bf16).reshape(8, full_width // 8, 128)


def whole():
    return pl.BlockSpec(memory_space=pltpu.VMEM)


def smem():
    return pl.BlockSpec(memory_space=pltpu.SMEM)


def raw():
    return pl.BlockSpec(memory_space=pl.ANY)


def attend_forward(span, mask, window, weight, biases):
    bounds, segq, segk = mask
    offsets, pieces = weight
    first, pairs = span
    count = len(window)
    block, full_width = window[0].shape
    width = pairs * PAIR
    padded = count * block + TK_FWD - ALIGN
    return pl.pallas_call(
        functools.partial(forward_kernel, count // 2, len(pieces), first),
        out_shape=(
            jax.ShapeDtypeStruct((block, width), bf16),
            jax.ShapeDtypeStruct((8, 2 * block), f32),
        ),
        in_specs=[smem()] * 2 + [whole()] * count + [raw()] * len(pieces) + [whole()] * 3,
        out_specs=(whole(), whole()),
        scratch_shapes=[
            pltpu.VMEM((full_width, 3 * width), bf16),
            pltpu.VMEM((block, width), bf16),
            pltpu.VMEM((2 * block, width), bf16),
            pltpu.VMEM((padded, width), bf16),
            pltpu.VMEM((padded, width), bf16),
            pltpu.VMEM((8, 2 * block), f32),
            pltpu.VMEM((8, 2 * block), f32),
            pltpu.VMEM((pairs, PAIR, 2 * block), f32),
            pltpu.SemaphoreType.DMA((count_pieces(pieces), 3)),
        ],
        compiler_params=pltpu.CompilerParams(vmem_limit_bytes=VMEM_LIMIT),
        cost_estimate=pl.CostEstimate(
            flops=2_500_000_000 * pairs, bytes_accessed=8_000_000, transcendentals=4_000_000
        ),
        name="attend_forward",
    )(bounds, offsets, *window, *pieces, biases, segq, segk)


def attend_backward(span, mask, window, weight, biases, attended, grad, before):
    bounds, segq, segk = mask
    offsets, pieces = weight
    first, pairs = span
    count = len(window)
    block, full_width = window[0].shape
    width = pairs * PAIR
    hops = count // 2
    padded = count * block + TK_BWD - ALIGN
    per_part = full_width // PAIR // len(attended)
    mixed, lse = attended[first // per_part]
    at = first // per_part * per_part
    outs = [
        jax.ShapeDtypeStruct((block, full_width), f32 if at == hops else bf16) for at in range(count)
    ]
    return pl.pallas_call(
        functools.partial(backward_kernel, hops, len(pieces), len(before), first, first - at),
        out_shape=(
            *outs,
            jax.ShapeDtypeStruct((8, full_width // 8, 3 * width + 128), bf16),
        ),
        in_specs=[smem()] * 2
        + [whole()] * count
        + [raw()] * len(pieces)
        + [whole()] * (6 + len(before)),
        out_specs=(whole(),) * (count + 1),
        scratch_shapes=[
            pltpu.VMEM((full_width, 3 * width), bf16),
            pltpu.VMEM((block, width), bf16),
            pltpu.VMEM((2 * block, width), bf16),
            pltpu.VMEM((2 * block, width), bf16),
            pltpu.VMEM((padded, width), bf16),
            pltpu.VMEM((padded, width), bf16),
            pltpu.VMEM((padded, width), f32),
            pltpu.VMEM((padded, width), f32),
            pltpu.VMEM((full_width, 3 * width), f32),
            pltpu.VMEM((8, 2 * block), f32),
            pltpu.VMEM((pairs, PAIR, 2 * block), f32),
            pltpu.VMEM((8, full_width), f32),
            pltpu.SemaphoreType.DMA((count_pieces(pieces), 3)),
        ],
        compiler_params=pltpu.CompilerParams(vmem_limit_bytes=VMEM_LIMIT),
        cost_estimate=pl.CostEstimate(
            flops=5_000_000_000 * pairs, bytes_accessed=20_000_000, transcendentals=4_000_000
        ),
        name="attend_backward",
    )(bounds, offsets, *window, *pieces, biases, segq, segk, mixed, lse, grad, *before)


def join(refs):
    if len(refs) == 1:
        return refs[0][...]
    return jnp.concatenate([ref[...] for ref in refs], axis=1)


def middle_kernel(
    counts, offsets, tokens_ref, cot_ref, vec_ref, upb_ref, *refs
):
    n_mixed, n_shared, n_down = counts
    mixed_refs, refs = refs[:n_mixed], refs[n_mixed:]
    out_own, up_own, refs = refs[0], refs[1], refs[2:]
    shared, down_p = split_pieces(refs[:n_shared]), split_pieces(refs[n_shared : n_shared + n_down])
    refs = refs[n_shared + n_down :]
    n_shared = len(shared)
    (
        result_ref, one_ref, mixed_ref, branch_ref, hidden_ref, inner_ref, act_ref, two_ref,
        small_ref, gupb_ref,
    ) = refs[:10]
    wo_s, up_s, down_s, slope_s, sems = refs[10:]
    width = wo_s.shape[1]
    out_copies, up_copies, down_copies = [], [], []

    def begin(copies, at, source, target):
        row = pl.multiple_of(offsets[at], ROW_STEP)
        copy = pltpu.make_async_copy(
            source, target.at[pl.ds(row, source.shape[0]), :], sems.at[at, len(copies) % 2]
        )
        copy.start()
        copies.append(copy)

    begin(out_copies, 0, out_own, wo_s)
    for at, piece in enumerate(shared):
        row = pl.multiple_of(offsets[2 + at], ROW_STEP)
        copy = pltpu.make_async_copy(
            piece.at[:, pl.ds(0, width)], wo_s.at[pl.ds(row, piece.shape[0]), :], sems.at[2 + at, 0]
        )
        copy.start()
        out_copies.append(copy)
    begin(up_copies, 1, up_own, up_s)
    for at, piece in enumerate(shared):
        row = pl.multiple_of(offsets[2 + at], ROW_STEP)
        copy = pltpu.make_async_copy(
            piece.at[:, pl.ds(width, up_s.shape[1])],
            up_s.at[pl.ds(row, piece.shape[0]), :],
            sems.at[2 + at, 1],
        )
        copy.start()
        up_copies.append(copy)
    for at, piece in enumerate(down_p):
        row = pl.multiple_of(offsets[2 + n_shared + at], ROW_STEP)
        copy = pltpu.make_async_copy(
            piece, down_s.at[pl.ds(row, piece.shape[0]), :], sems.at[2 + n_shared + at, 0]
        )
        copy.start()
        down_copies.append(copy)
    inner_width = up_s.shape[1]
    tile = inner_width // FF_TILES
    out_bias, norm_gain, norm_shift = vec_ref[0:1, :], vec_ref[1:2, :], vec_ref[2:3, :]
    down_bias, final_gain, final_shift = vec_ref[3:4, :], vec_ref[4:5, :], vec_ref[5:6, :]
    wait_all(out_copies)
    values = tokens_ref[...].astype(f32) + (nn(join(mixed_refs), wo_s[...]) + out_bias)
    centered = values - jnp.mean(values, axis=1, keepdims=True)
    inverse_one = lax.rsqrt(jnp.mean(centered * centered, axis=1, keepdims=True) + epsilon)
    normed_one = centered * inverse_one
    hidden = normed_one * norm_gain + norm_shift
    hidden_low = hidden.astype(bf16)
    hidden_ref[...] = hidden_low
    wait_all(up_copies)
    branch_two = None
    for at in range(FF_TILES):
        cols = slice(at * tile, (at + 1) * tile)
        inner = nn(hidden_low, up_s[:, cols]) + upb_ref[0:1, cols]
        normal = 0.5 * (1.0 + lax.erf(inner * 0.7071067811865476))
        density = jnp.exp(-0.5 * inner * inner) * 0.3989422804014327
        slope_s[:, cols] = normal + inner * density
        activated = (inner * normal).astype(bf16)
        act_ref[:, cols] = activated
        if at == 0:
            wait_all(down_copies)
        term = nn(activated, down_s[cols, :])
        branch_two = term if branch_two is None else branch_two + term
    values = hidden + (branch_two + down_bias)
    centered = values - jnp.mean(values, axis=1, keepdims=True)
    inverse_two = lax.rsqrt(jnp.mean(centered * centered, axis=1, keepdims=True) + epsilon)
    normed_two = centered * inverse_two
    result_ref[...] = (normed_two * final_gain + final_shift).astype(bf16)
    cot = cot_ref[...].astype(f32)
    small_ref[4:5, :] = jnp.sum(cot * normed_two, axis=0, keepdims=True)
    small_ref[5:6, :] = jnp.sum(cot, axis=0, keepdims=True)
    scaled = cot * final_gain
    first = jnp.mean(scaled, axis=1, keepdims=True)
    second = jnp.mean(scaled * normed_two, axis=1, keepdims=True)
    grad_two = inverse_two * (scaled - first - normed_two * second)
    grad_low = grad_two.astype(bf16)
    two_ref[...] = grad_low
    small_ref[3:4, :] = jnp.sum(grad_low.astype(f32), axis=0, keepdims=True)
    grad_hidden = grad_two
    gupb_ref[...] = jnp.zeros(gupb_ref.shape, f32)
    for at in range(FF_TILES):
        cols = slice(at * tile, (at + 1) * tile)
        grad_inner = (nt(grad_low, down_s[cols, :]) * slope_s[:, cols]).astype(bf16)
        inner_ref[:, cols] = grad_inner
        gupb_ref[0:1, cols] = jnp.sum(grad_inner.astype(f32), axis=0, keepdims=True)
        grad_hidden = grad_hidden + nt(grad_inner, up_s[:, cols])
    small_ref[1:2, :] = jnp.sum(grad_hidden * normed_one, axis=0, keepdims=True)
    small_ref[2:3, :] = jnp.sum(grad_hidden, axis=0, keepdims=True)
    scaled = grad_hidden * norm_gain
    first = jnp.mean(scaled, axis=1, keepdims=True)
    second = jnp.mean(scaled * normed_one, axis=1, keepdims=True)
    grad_one = inverse_one * (scaled - first - normed_one * second)
    one_ref[...] = grad_one
    grad_branch = grad_one.astype(bf16)
    branch_ref[...] = grad_branch
    small_ref[0:1, :] = jnp.sum(grad_branch.astype(f32), axis=0, keepdims=True)
    small_ref[6:8, :] = jnp.zeros((2, small_ref.shape[1]), f32)
    mixed_ref[...] = nt(grad_branch, wo_s[...]).astype(bf16)


def middle(attended, tokens, cotangent, weights, vectors, up_bias):
    offsets, out_own, up_own, shared, down = weights
    counts = (len(attended), len(shared), len(down))
    pieces = [out_own, up_own, *shared, *down]
    block, width = tokens.shape
    inner_width = up_bias.shape[1]
    return pl.pallas_call(
        functools.partial(middle_kernel, counts),
        out_shape=(
            jax.ShapeDtypeStruct((block, width), bf16),
            jax.ShapeDtypeStruct((block, width), f32),
            jax.ShapeDtypeStruct((block, width), bf16),
            jax.ShapeDtypeStruct((block, width), bf16),
            jax.ShapeDtypeStruct((block, width), bf16),
            jax.ShapeDtypeStruct((block, inner_width), bf16),
            jax.ShapeDtypeStruct((block, inner_width), bf16),
            jax.ShapeDtypeStruct((block, width), bf16),
            jax.ShapeDtypeStruct((8, width), f32),
            jax.ShapeDtypeStruct((8, inner_width), f32),
        ),
        in_specs=[smem()] + [whole()] * (4 + len(attended)) + [raw()] * len(pieces),
        out_specs=(whole(),) * 10,
        scratch_shapes=[
            pltpu.VMEM((width, width), bf16),
            pltpu.VMEM((width, inner_width), bf16),
            pltpu.VMEM((inner_width, width), bf16),
            pltpu.VMEM((block, inner_width), f32),
            pltpu.SemaphoreType.DMA((count_pieces(pieces), 2)),
        ],
        compiler_params=pltpu.CompilerParams(vmem_limit_bytes=VMEM_LIMIT),
        cost_estimate=pl.CostEstimate(flops=24_000_000_000, bytes_accessed=20_000_000, transcendentals=4_000_000),
        name="middle",
    )(offsets, tokens, cotangent, vectors, up_bias, *attended, *pieces)


def grad_down_kernel(micro, *refs):
    act_refs, two_refs, side_ref, out_ref = refs[:micro], refs[micro : 2 * micro], refs[-2], refs[-1]
    total = sum(tn(act[...], two[...]) for act, two in zip(act_refs, two_refs))
    rows, width = total.shape
    parts = out_ref.shape[0]
    out_ref[:, :, :width] = total.astype(bf16).reshape(parts, rows // parts, width)
    side = jnp.concatenate([side_ref[...], jnp.zeros((120, rows), f32)], axis=0).T
    out_ref[:, :, width:] = side.astype(bf16).reshape(parts, rows // parts, 128)


def weight_grad_down(activated, grad_low, side):
    micro = len(activated)
    block, inner_width = activated[0].shape
    width = grad_low[0].shape[1]
    tile = inner_width // FF_TILES
    return pl.pallas_call(
        functools.partial(grad_down_kernel, micro),
        out_shape=jax.ShapeDtypeStruct((8, inner_width // 8, width + 128), bf16),
        grid=(FF_TILES,),
        in_specs=[pl.BlockSpec((block, tile), lambda at: (0, at))] * micro
        + [pl.BlockSpec((block, width), lambda at: (0, 0))] * micro
        + [pl.BlockSpec((8, tile), lambda at: (0, at))],
        out_specs=pl.BlockSpec((8 // FF_TILES, inner_width // 8, width + 128), lambda at: (at, 0, 0)),
        compiler_params=pltpu.CompilerParams(vmem_limit_bytes=VMEM_LIMIT),
        cost_estimate=pl.CostEstimate(flops=5_400_000_000, bytes_accessed=14_000_000, transcendentals=0),
        name="weight_grad_down",
    )(*activated, *grad_low, side)


def grad_up_kernel(micro, counts, *refs):
    hidden, inner = refs[:micro], refs[micro : 2 * micro]
    out_ref, refs = refs[-1], refs[2 * micro : -1]
    if not counts:
        total = sum(tn(one[...], two[...]) for one, two in zip(hidden, inner))
        out_ref[...] = total.astype(bf16).reshape(out_ref.shape)
        return
    branch, refs = refs[:micro], refs[micro:]
    mixed = []
    for size in counts:
        mixed.append(refs[:size])
        refs = refs[size:]
    last = pl.num_programs(0) - 1

    @pl.when(pl.program_id(0) < last)
    def _():
        total = sum(tn(one[...], two[...]) for one, two in zip(hidden, inner))
        out_ref[...] = total.astype(bf16).reshape(out_ref.shape)

    @pl.when(pl.program_id(0) == last)
    def _():
        total = sum(tn(join(one), two[...]) for one, two in zip(mixed, branch))
        out_ref[...] = total.astype(bf16).reshape(out_ref.shape)


def weight_grad_up(hidden_low, grad_inner, first, tiles, attended=(), grad_branch=()):
    micro = len(hidden_low)
    block, width = hidden_low[0].shape
    steps = tiles + (1 if attended else 0)
    fixed = [pl.BlockSpec((block, width), lambda at: (0, 0))] * micro
    parts = [part for one in attended for part in one]
    return pl.pallas_call(
        functools.partial(grad_up_kernel, micro, tuple(len(one) for one in attended)),
        out_shape=jax.ShapeDtypeStruct((8, width // 8, steps * width), bf16),
        grid=(steps,),
        in_specs=fixed
        + [pl.BlockSpec((block, width), lambda at: (0, first + jnp.minimum(at, tiles - 1)))] * micro
        + (fixed if attended else [])
        + [pl.BlockSpec(part.shape, lambda at: (0, 0)) for part in parts],
        out_specs=pl.BlockSpec((8, width // 8, width), lambda at: (0, 0, at)),
        compiler_params=pltpu.CompilerParams(vmem_limit_bytes=VMEM_LIMIT),
        cost_estimate=pl.CostEstimate(
            flops=1_400_000_000 * steps, bytes_accessed=3_000_000 * steps, transcendentals=0
        ),
        name="weight_grad_up",
    )(*hidden_low, *grad_inner, *grad_branch, *parts)


def permute(value, axis, pairs):
    return lax.ppermute(value, axis, pairs)


def swap_pairs(size, distance):
    return [(at, at ^ distance) for at in range(size)]


def shift_pairs(size, by):
    return [(at, at + by) for at in range(size) if 0 <= at + by < size]


def pick(array, index, axis=0):
    return lax.dynamic_index_in_dim(array, index, axis, keepdims=False)


def ordered(first_here, mine, other, axis=0):
    first = jnp.where(first_here, mine, other)
    second = jnp.where(first_here, other, mine)
    return jnp.concatenate([first, second], axis=axis)


def two_level(mesh_shape):
    return mesh_shape["replica"] == 4 and mesh_shape["fsdp"] == 2 and mesh_shape["seq"] == 4


def sync(*values):
    return lax.optimization_barrier(values)


class Fetch:
    def __init__(self, fast):
        self.fast = fast
        self.here = lax.axis_index("fsdp")
        self.spot = 2 * lax.axis_index("x") + lax.axis_index("core") if fast else None

    def quarter(self, shard):
        if not self.fast:
            return shard
        size = shard.shape[0] // 4
        return lax.dynamic_slice_in_dim(shard, self.spot * size, size, 0)

    def far(self, quarter):
        if not self.fast:
            return [lax.all_gather(quarter, "fsdp", axis=0, tiled=True)]
        return [permute(quarter, "fsdp", swap_pairs(2, 1))]

    def across(self, held):
        if not self.fast:
            return held
        return held + [permute(held[0], "x", swap_pairs(2, 1))]

    def beside(self, held):
        if not self.fast:
            return held
        pair = jnp.stack(held)
        return [pair, permute(pair, "core", swap_pairs(2, 1))]

    def offsets(self, rows):
        size = rows // 4
        there = (1 - self.here) * rows
        return [self.here * rows], [there + (self.spot ^ flip) * size for flip in (0, 2, 1, 3)]

    def one_weight(self, shard, held):
        if not self.fast:
            return jnp.zeros((1,), jnp.int32), held
        mine, others = self.offsets(shard.shape[0])
        return jnp.stack(mine + others).astype(jnp.int32), [shard] + held

    def middle_weights(self, out_shard, up_shard, down_shard, shared, down):
        if not self.fast:
            width = shared[0].shape[0]
            return (jnp.zeros((3,), jnp.int32), shared[0][:, :width], shared[0][:, width:], [], down)
        mine, others = self.offsets(out_shard.shape[0])
        own, rest = self.offsets(down_shard.shape[0])
        offsets = jnp.stack(mine + mine + others + own + rest).astype(jnp.int32)
        return offsets, out_shard, up_shard, shared, [down_shard] + down

    def with_vectors(self, quarter, shards):
        if not self.fast:
            return quarter
        return jnp.concatenate([quarter, jnp.concatenate(shards).reshape(-1, quarter.shape[1])], axis=0)

    def without_vectors(self, held, shards):
        if not self.fast:
            return held, [lax.all_gather(shard, "fsdp", axis=0, tiled=True) for shard in shards]
        moved = held[0]
        rows = sum(shard.shape[0] for shard in shards) // moved.shape[1]
        far = moved[moved.shape[0] - rows :].reshape(-1)
        full, at = [], 0
        for shard in shards:
            size = shard.shape[0]
            full.append(ordered(self.here == 0, shard, far[at : at + size]))
            at += size
        return [moved[: moved.shape[0] - rows]], full


def add_low(left, right):
    return (left.astype(f32) + right.astype(f32)).astype(bf16)


class Chain:
    def __init__(self, fast, *parts):
        self.fast = fast
        self.name = None
        self.pair = [part.reshape(2, 2, 2, *part.shape[1:]) if fast else part for part in parts]

    def settle(self):
        name, pair = self.name, self.pair
        if name in ("core", "y", "x", "z1", "z2"):
            return add_low(*pair)
        if name == "z3":
            return ordered(lax.axis_index("seq") % 2 == 0, *pair)
        if name == "spread_x":
            return both_ways(lax.axis_index("x") == 0, *pair)
        return both_ways(lax.axis_index("core") == 0, *pair)

    def slices(self, index, dim):
        if self.name is None:
            parts = [pick(part, index, dim).astype(f32) for part in self.pair]
            return sum(parts).astype(bf16) if len(parts) > 1 else pick(self.pair[0], index, dim)
        if self.name in ("core", "y", "x"):
            return add_low(*[pick(part, index, dim) for part in self.pair])
        return pick(self.settle(), index, dim)

    def go(self, name):
        if not self.fast:
            return
        if name in ("z2", "z3", "spread_x", "spread_core"):
            held = self.settle()
            axis = {"z2": "seq", "z3": "seq", "spread_x": "x", "spread_core": "core"}[name]
            pairs = {"z2": swap_pairs(4, 2), "z3": swap_pairs(4, 1)}.get(name, swap_pairs(2, 1))
            self.name, self.pair = name, (held, permute(held, axis, pairs))
            return
        axis, dim = {"core": ("core", 1), "y": ("fsdp", 0), "x": ("x", 0), "z1": ("seq", 0)}[name]
        here = lax.axis_index(axis)
        if name == "z1":
            here = here % 2
            self.pair = [part.reshape(2, part.shape[0] // 2, part.shape[1]) for part in self.pair]
        sent = self.slices(1 - here, dim)
        pairs = swap_pairs(4 if axis == "seq" else 2, 1)
        moved = permute(sent, axis, pairs)
        self.pair = (self.slices(here, dim), moved)
        self.name = name

    def final(self):
        if not self.fast:
            parts = sum(part.astype(f32) for part in self.pair).astype(bf16)
            share = lax.psum_scatter(
                parts.reshape(-1, parts.shape[2]), "fsdp", scatter_dimension=0, tiled=True
            )
            return lax.psum(share, ("replica", "seq")).astype(f32)
        full = self.settle()
        return full.reshape(-1, full.shape[-1]).astype(f32)


def both_ways(first_here, mine, other):
    return jnp.stack([jnp.where(first_here, mine, other), jnp.where(first_here, other, mine)])


def settle_all(chains, *values):
    pairs, *values = sync([chain.pair for chain in chains], *values)
    for chain, pair in zip(chains, pairs):
        chain.pair = pair
    return values


def body(
    fast,
    tokens,
    segment_ids,
    joined_weight,
    query_bias,
    value_bias,
    out_weight,
    out_bias,
    norm_gain,
    norm_shift,
    up_weight,
    up_bias,
    down_weight,
    down_bias,
    final_gain,
    final_shift,
    cotangent,
):
    micro, block, width = tokens.shape[1:]
    length = segment_ids.shape[-1]
    size = lax.axis_size("seq")
    place = lax.axis_index("seq")
    hops = min(size - 1, (length // 2 - 2) // block + 1)
    count = 2 * hops + 1
    inner_width = up_weight.shape[1]
    all_pairs = width // PAIR
    half_pairs = all_pairs // 2
    spans = [(0, half_pairs), (half_pairs, half_pairs)]
    fetch = Fetch(fast)

    masks = []
    for batch in range(micro):
        ids = segment_ids[0, batch]
        padded = jnp.concatenate(
            [jnp.full((hops * block,), -1, jnp.int32), ids, jnp.full((hops * block,), 1000, jnp.int32)]
        )
        near = lax.dynamic_slice_in_dim(padded, place * block, count * block, 0)
        rows = lax.dynamic_slice_in_dim(ids, place * block, block, 0)
        bounds = jnp.stack([jnp.sum(near < rows[0]), jnp.sum(near <= rows[-1])]).astype(jnp.int32)
        segq = jnp.broadcast_to(rows[None, :], (8, block))
        tail = jnp.full((TK_FWD - ALIGN,), 1000, jnp.int32)
        segk = jnp.broadcast_to(jnp.concatenate([near, tail])[:, None], (count * block + TK_FWD - ALIGN, 128))
        masks.append((bounds, segq, segk))

    def send_out(one):
        return [permute(one, "seq", shift_pairs(size, -far)) for far in range(-hops, 0)] + [
            permute(one, "seq", shift_pairs(size, -far)) for far in range(1, hops + 1)
        ]

    def window(moved, one):
        return moved[:hops] + [one] + moved[hops:]

    own = [tokens[0, batch] for batch in range(micro)]
    moves = [None] * micro
    small_shards = [
        query_bias,
        value_bias,
        out_bias,
        norm_gain,
        norm_shift,
        down_bias,
        final_gain,
        final_shift,
        up_bias,
    ]
    joined = fetch.far(fetch.with_vectors(fetch.quarter(joined_weight), small_shards))
    moves[0] = send_out(own[0])
    quarters = [
        jnp.concatenate([fetch.quarter(out_weight), fetch.quarter(up_weight)], axis=1),
        fetch.quarter(down_weight),
    ]
    joined, own, quarters = sync(joined, own, quarters)
    joined, vectors = fetch.without_vectors(joined, small_shards)
    biases = jnp.pad(jnp.stack(vectors[:2]).astype(f32), ((0, 6), (0, 0)))
    rows_six = jnp.pad(jnp.stack(vectors[2:8]).astype(f32), ((0, 2), (0, 0)))
    up_row = jnp.pad(vectors[8].astype(f32)[None, :], ((0, 7), (0, 0)))
    joined = fetch.across(joined)
    joined, quarters = sync(joined, quarters)
    joined = fetch.beside(joined)
    shared = fetch.far(quarters[0])
    moves[0], joined, own, biases, rows_six, up_row, masks, quarters = sync(
        moves[0], joined, own, biases, rows_six, up_row, masks, quarters
    )

    attended = [[] for _ in range(micro)]
    windows = [window(moves[0], own[0])] + [None] * (micro - 1)
    weight = fetch.one_weight(joined_weight, joined)

    def hop_out(batch, step):
        left, right = moves[batch] or ([own[batch]], [own[batch]])
        moves[batch] = (
            left + [permute(left[-1], "seq", shift_pairs(size, 1))],
            right + [permute(right[-1], "seq", shift_pairs(size, -1))],
        )

    shared = fetch.across(shared)
    down = fetch.far(quarters[1])
    if micro > 1:
        hop_out(1, 0)
    attended[0].append(tuple(attend_forward(spans[0], masks[0], windows[0], weight, biases)))
    attended[0], shared, down, masks, windows[0], moves[1:2] = sync(
        attended[0], shared, down, masks, windows[0], moves[1:2]
    )
    down = fetch.across(down)
    shared = fetch.beside(shared)
    for step in range(1, hops if micro > 1 else 0):
        hop_out(1, step)
    attended[0].append(tuple(attend_forward(spans[1], masks[0], windows[0], weight, biases)))
    attended[0], moves[1:2], shared, down = sync(attended[0], moves[1:2], shared, down)
    down = fetch.beside(down)
    attended[0], down, own = sync(attended[0], down, own)
    middle_weights = fetch.middle_weights(out_weight, up_weight, down_weight, shared, down)

    middles = []
    for batch in range(micro):
        later = batch + 1
        if batch > 0:
            left, right = moves[batch]
            windows[batch] = left[:0:-1] + [left[0]] + right[1:]
            for step in range(1, hops if later < micro else 0):
                hop_out(later, step)
            attended[batch].append(
                tuple(attend_forward((0, all_pairs), masks[batch], windows[batch], weight, biases))
            )
            if later < micro:
                attended[batch], moves[later] = sync(attended[batch], moves[later])
        if later + 1 < micro:
            hop_out(later + 1, 0)
        middles.append(
            middle(
                [one[0] for one in attended[batch]],
                own[batch],
                cotangent[0, batch],
                middle_weights,
                rows_six,
                up_row,
            )
        )
        if later + 1 < micro:
            middles[-1], masks, moves[later + 1] = sync(middles[-1], masks, moves[later + 1])
        else:
            middles[-1], masks = sync(middles[-1], masks)

    outs = list(zip(*middles))
    small = sum(outs[8])
    grad_upb = sum(outs[9])
    half = width // 2
    gap = inner_width // 2 - half
    spread = jnp.pad(small[:6].reshape(6, 2, half), ((0, 0), (0, 0), (0, gap))).reshape(6, inner_width)
    side = jnp.concatenate([grad_upb[:1], spread, jnp.zeros((1, inner_width), f32)], axis=0)
    down = Chain(fast, weight_grad_down(outs[6], outs[7], side))
    up_ins = (outs[4], outs[5], [[part[0] for part in one] for one in attended], outs[3])
    (up_ins,) = settle_all([down], up_ins)
    down.go("core")
    tiles = inner_width // width
    up = Chain(fast, weight_grad_up(up_ins[0], up_ins[1], 0, tiles, up_ins[2], up_ins[3]))
    (masks,) = settle_all([down, up], list(masks))

    backs = [None] * micro
    coming = [None] * micro
    joined_sums = [[], []]
    last = micro - 1

    def run_back(which, batch, chains, moving=()):
        before = [outs[1][batch]] if which == 0 else backs[batch]
        *parts, grad_joined = attend_backward(
            spans[which], masks[batch], windows[batch], weight, biases, attended[batch], outs[2][batch], before
        )
        moved = [coming[at] for at in moving]
        backs[batch], grad_joined, masks[:], moved = settle_all(chains, parts, grad_joined, list(masks), moved)
        for at, one in zip(moving, moved):
            coming[at] = one
        joined_sums[which].append(grad_joined)

    def send_back(batch):
        coming[batch] = [
            permute(backs[batch][hops + far], "seq", shift_pairs(size, far))
            for far in range(-hops, hops + 1)
            if far != 0
        ]

    def total_of(which):
        return Chain(fast, *joined_sums[which])

    def hop_back(batch, step):
        far = hops - step
        sent = []
        for at, by, sign in ((0, 1, 1), (1, -1, -1)):
            part = backs[batch][hops + sign * far]
            if step > 0:
                part = add_low(part, coming[batch][at])
            sent.append(permute(part, "seq", shift_pairs(size, by)))
        coming[batch] = sent

    down.go("y")
    up.go("core")
    run_back(0, 0, [up, down])
    down.go("x")
    up.go("y")
    run_back(1, 0, [down])
    down.go("z1")
    hop_back(0, 0)
    run_back(0, 1, [down, up], [0])
    down.go("z2")
    up.go("x")
    for step in range(1, hops):
        hop_back(0, step)
    for batch in range(2, micro):
        run_back(0, batch, [down, up], [0])
    joined_one = total_of(0)
    joined_one.go("core")
    down.go("z3")
    up.go("z1")
    for batch in range(1, last):
        run_back(1, batch, [down, up, joined_one])
    joined_one.go("y")
    down.go("spread_x")
    up.go("z2")
    for batch in range(1, last):
        hop_back(batch, 0)
    run_back(1, last, [down, up, joined_one], list(range(1, last)))

    joined_two = total_of(1)
    joined_two.go("core")
    joined_one.go("x")
    up.go("z3")
    (backs,) = settle_all([joined_two], backs)
    joined_two.go("y")
    down.go("spread_core")
    (backs,) = settle_all([joined_one, up, down], backs)
    joined_one.go("z1")
    up.go("spread_x")
    for batch in range(1, last):
        for step in range(1, hops):
            hop_back(batch, step)
    settle_all([joined_two, joined_one])
    joined_two.go("x")
    joined_one.go("z2")
    send_back(last)
    settle_all([joined_two, joined_one, up])
    joined_two.go("z1")
    joined_one.go("z3")
    up.go("spread_core")
    settle_all([joined_two, joined_one])
    joined_two.go("z2")
    joined_one.go("spread_x")
    settle_all([joined_two, joined_one])
    joined_two.go("z3")
    joined_one.go("spread_core")
    settle_all([joined_two])
    joined_two.go("spread_x")
    joined_two.go("spread_core")

    final_down = down.final()
    final_up = up.final()
    final_up, final_out = final_up[:, :inner_width], final_up[:, inner_width:]
    final_a, final_b = joined_one.final(), joined_two.final()
    grad_tokens = []
    for batch in range(micro):
        total = backs[batch][hops] + sum(one.astype(f32) for one in coming[batch])
        grad_tokens.append(total.astype(bf16))
    low, high = spans[0][1] * PAIR, spans[1][1] * PAIR
    final_joined = jnp.concatenate(
        [
            part
            for at in range(3)
            for part in (final_a[:, at * low : (at + 1) * low], final_b[:, at * high : (at + 1) * high])
        ],
        axis=1,
    )
    bias_sums = final_a[:, 3 * low : 3 * low + 2] + final_b[:, 3 * high : 3 * high + 2]
    if fast:
        own_rows = width // lax.axis_size("fsdp")
        smalls = [final_down[:own_rows, width + 1 + at] for at in range(6)]
    else:
        smalls = [
            lax.psum_scatter(lax.psum(small[at], ("replica", "seq")), "fsdp", scatter_dimension=0, tiled=True)
            for at in range(6)
        ]
    return (
        jnp.stack(outs[0], axis=0)[None],
        jnp.stack(grad_tokens, axis=0)[None],
        final_joined,
        bias_sums[:, 0],
        bias_sums[:, 1],
        final_out,
        smalls[0],
        smalls[1],
        smalls[2],
        final_up,
        final_down[:, width],
        final_down[:, :width],
        smalls[3],
        smalls[4],
        smalls[5],
    )


def solution(mesh):
    fast = two_level(dict(mesh.shape))
    groups = ("replica", "fsdp")
    if fast:
        mesh = jax.sharding.Mesh(mesh.devices.reshape(2, 2, 2, 4), ("x", "core", "fsdp", "seq"))
        groups = ("x", "core", "fsdp")
    rows = P(groups, None, "seq", None)
    matrix, vector = P("fsdp", None), P("fsdp")
    in_specs = (
        rows,
        P(groups, None, None),
        matrix,
        vector,
        vector,
        matrix,
        vector,
        vector,
        vector,
        matrix,
        vector,
        matrix,
        vector,
        vector,
        vector,
        rows,
    )
    out_specs = (
        rows,
        rows,
        matrix,
        vector,
        vector,
        matrix,
        vector,
        vector,
        vector,
        matrix,
        vector,
        matrix,
        vector,
        vector,
        vector,
    )
    return jax.shard_map(
        functools.partial(body, fast),
        mesh=mesh,
        in_specs=in_specs,
        out_specs=out_specs,
        check_vma=False,
    )
```

```python
import functools
import jax
import jax.numpy as jnp
from jax import lax
from jax.experimental import pallas as pl
from jax.experimental.pallas import tpu as pltpu
from jax.sharding import PartitionSpec as P

HEADS = 12
HEAD_DIM = 64
PAIR = 2 * HEAD_DIM
epsilon = 1e-05
masked_score = -1e30
scale = HEAD_DIM ** (-0.5)
TK_FWD = 256
TK_BWD = 256
ALIGN = 128
ROW_STEP = 16
VMEM_LIMIT = 62 * 1024 * 1024
FF_TILES = 4
f32 = jnp.float32
bf16 = jnp.bfloat16


def nt(left, right):
    return lax.dot_general(left, right, (((1,), (1,)), ((), ())), preferred_element_type=f32)


def tn(left, right):
    return lax.dot_general(left, right, (((0,), (0,)), ((), ())), preferred_element_type=f32)


def nn(left, right):
    return lax.dot_general(left, right, (((1,), (0,)), ((), ())), preferred_element_type=f32)


def stack_heads(pair):
    lane = lax.broadcasted_iota(jnp.int32, pair.shape, 1)
    zero = jnp.zeros_like(pair)
    return jnp.concatenate(
        [jnp.where(lane < HEAD_DIM, pair, zero), jnp.where(lane < HEAD_DIM, zero, pair)], axis=0
    )


def unstack_heads(rows):
    half = rows.shape[0] // 2
    lane = lax.broadcasted_iota(jnp.int32, (half, rows.shape[1]), 1)
    return jnp.where(lane < HEAD_DIM, rows[:half], rows[half:])


def split_pieces(refs):
    pieces = []
    for ref in refs:
        if len(ref.shape) == 2:
            pieces.append(ref)
        else:
            pieces.extend(ref.at[at] for at in range(ref.shape[0]))
    return pieces


def count_pieces(arrays):
    return sum(1 if len(one.shape) == 2 else one.shape[0] for one in arrays)


def start_columns(offsets, piece_refs, full_s, sems, width, at_col, size_col):
    copies = []
    for at, piece in enumerate(split_pieces(piece_refs)):
        size = piece.shape[0]
        row = pl.multiple_of(offsets[at], ROW_STEP)
        for part in range(3):
            copy = pltpu.make_async_copy(
                piece.at[:, pl.ds(part * width + at_col, size_col)],
                full_s.at[pl.ds(row, size), pl.ds(part * size_col, size_col)],
                sems.at[at, part],
            )
            copy.start()
            copies.append(copy)
    return copies


def wait_all(copies):
    for copy in copies:
        copy.wait()


def project_window(bounds, x_refs, w_ref, bias_ref, cols, k_s, v_s, tail):
    block = x_refs[0].shape[0]
    width = k_s.shape[1]
    lo, hi = bounds[0], bounds[1]
    for at, x_ref in enumerate(x_refs):
        rows = pl.ds(at * block, block)
        active = (hi > at * block) & (lo < (at + 1) * block)

        @pl.when(active)
        def _():
            x = x_ref[...]
            k_s[rows, :] = nn(x, w_ref[:, width : 2 * width]).astype(bf16)
            v_s[rows, :] = (nn(x, w_ref[:, 2 * width :]) + bias_ref[1:2, cols]).astype(bf16)

        @pl.when(jnp.logical_not(active))
        def _():
            k_s[rows, :] = jnp.zeros((block, width), bf16)
            v_s[rows, :] = jnp.zeros((block, width), bf16)

    end = len(x_refs) * block
    k_s[end:, :] = jnp.zeros((tail, width), bf16)
    v_s[end:, :] = jnp.zeros((tail, width), bf16)


def tile_range(bounds, tk):
    low = bounds[0]
    high = bounds[1]
    start = (low // ALIGN) * ALIGN
    return start, (high - start + tk - 1) // tk


def project_queries(x_ref, w_ref, bias_ref, cols, q_s, qq_s):
    block = x_ref.shape[0]
    width = q_s.shape[1]
    q = nn(x_ref[...], w_ref[:, :width]) + bias_ref[0:1, cols]
    q_s[...] = q.astype(bf16) * jnp.asarray(scale, bf16)
    for pair in range(width // PAIR):
        here = slice(pair * PAIR, (pair + 1) * PAIR)
        qq_s[:, here] = stack_heads(q_s[:, here])


def forward_kernel(hops, pieces, first, bounds, offsets, *refs):
    count = 2 * hops + 1
    x_refs = refs[:count]
    w_refs, refs = refs[count : count + pieces], refs[count + pieces :]
    bias_ref, segq_ref, segk_ref, o_ref, lse_ref = refs[:5]
    w_ref, q_s, qq_s, k_s, v_s, top_s, sum_s, acc_s, sems = refs[5:]
    block, full_width = x_refs[0].shape
    width = o_ref.shape[1]
    tk = TK_FWD
    pairs = width // PAIR
    cols_all = slice(first * PAIR, first * PAIR + width)
    wait_all(start_columns(offsets, w_refs, w_ref, sems, full_width, first * PAIR, width))
    project_window(bounds, x_refs, w_ref, bias_ref, cols_all, k_s, v_s, tk - ALIGN)
    project_queries(x_refs[hops], w_ref, bias_ref, cols_all, q_s, qq_s)
    start, steps = tile_range(bounds, tk)
    segq = segq_ref[0:1, :]
    segq = jnp.concatenate([segq, segq], axis=1)
    top_s[...] = jnp.full(top_s.shape, masked_score, f32)
    sum_s[...] = jnp.ones(sum_s.shape, f32)
    sum_s[:pairs, :] = jnp.zeros((pairs, sum_s.shape[1]), f32)
    acc_s[...] = jnp.zeros(acc_s.shape, f32)

    @pl.loop(0, steps)
    def _(at):
        here = pl.ds(pl.multiple_of(start + at * tk, ALIGN), tk)
        allowed = segk_ref[here, 0:1] == segq
        for pair in range(pairs):
            cols = slice(pair * PAIR, (pair + 1) * PAIR)
            one = slice(pair, pair + 1)
            scores = nt(k_s[here, cols], qq_s[:, cols])
            scores = jnp.where(allowed, scores, masked_score)
            top = top_s[one, :]
            new_top = jnp.maximum(top, jnp.max(scores, axis=0, keepdims=True))
            fade = jnp.exp(top - new_top)
            weights = jnp.exp(scores - new_top)
            top_s[one, :] = new_top
            sum_s[one, :] = sum_s[one, :] * fade + jnp.sum(weights, axis=0, keepdims=True)
            acc_s[pair] = acc_s[pair] * fade + tn(v_s[here, cols], weights.astype(bf16))

    lse_ref[...] = top_s[...] + jnp.log(sum_s[...])
    for pair in range(pairs):
        cols = slice(pair * PAIR, (pair + 1) * PAIR)
        mixed = acc_s[pair] / sum_s[pair : pair + 1, :]
        o_ref[:, cols] = unstack_heads(mixed.T).astype(bf16)


def backward_kernel(hops, pieces, prev, first, skip, bounds, offsets, core_ref, *refs):
    count = 2 * hops + 1
    x_refs = refs[:count]
    w_refs, refs = refs[count : count + pieces], refs[count + pieces :]
    bias_ref, segq_ref, segk_ref, o_ref, lse_ref, do_ref = refs[:6]
    prev_refs, refs = refs[6 : 6 + prev], refs[6 + prev :]
    out_refs, refs = refs[:count], refs[count:]
    keep_ref, send_ref, w_ref, q_s, qq_s, gg_s, k_s, v_s, dk_s, dv_s, dw_s, stat_s, acc_s, db_s, sems = refs
    block, full_width = x_refs[0].shape
    width = q_s.shape[1]
    tk = TK_BWD
    pairs = width // PAIR
    cols_all = slice(first * PAIR, first * PAIR + width)
    copies = start_columns(offsets, w_refs, w_ref, sems, full_width, first * PAIR, width)
    dk_s[...] = jnp.zeros(dk_s.shape, f32)
    dv_s[...] = jnp.zeros(dv_s.shape, f32)
    acc_s[...] = jnp.zeros(acc_s.shape, f32)
    for pair in range(pairs):
        cols = slice(pair * PAIR, (pair + 1) * PAIR)
        far = slice((first + pair) * PAIR, (first + pair + 1) * PAIR)
        theirs = slice((skip + pair) * PAIR, (skip + pair + 1) * PAIR)
        grads = stack_heads(do_ref[:, far])
        gg_s[:, cols] = grads
        mixed = o_ref[:, theirs].astype(f32)
        product = grads.astype(f32) * jnp.concatenate([mixed, mixed], axis=0)
        stat_s[pair : pair + 1, :] = jnp.sum(product.T, axis=0, keepdims=True)
    wait_all(copies)
    project_window(bounds, x_refs, w_ref, bias_ref, cols_all, k_s, v_s, tk - ALIGN)
    project_queries(x_refs[hops], w_ref, bias_ref, cols_all, q_s, qq_s)
    lo, hi = bounds[0], bounds[1]
    actives = [(hi > at * block) & (lo < (at + 1) * block) for at in range(count)]
    start, steps = tile_range(bounds, tk)
    segq = segq_ref[0:1, :]
    segq = jnp.concatenate([segq, segq], axis=1)

    @pl.loop(0, steps)
    def _(at):
        here = pl.ds(pl.multiple_of(start + at * tk, ALIGN), tk)
        allowed = segk_ref[here, 0:1] == segq
        for pair in range(pairs):
            cols = slice(pair * PAIR, (pair + 1) * PAIR)
            keys = k_s[here, cols]
            queries = qq_s[:, cols]
            grads = gg_s[:, cols]
            scores = nt(keys, queries)
            scores = jnp.where(allowed, scores, masked_score)
            weights = jnp.exp(scores - lse_ref[skip + pair : skip + pair + 1, :])
            grad_weights = nt(v_s[here, cols], grads)
            grad_scores = (weights * (grad_weights - stat_s[pair : pair + 1, :])).astype(bf16)
            dv_s[here, cols] += nn(weights.astype(bf16), grads)
            dk_s[here, cols] += nn(grad_scores, queries)
            acc_s[pair] += tn(keys, grad_scores)

    for pair in range(pairs):
        cols = slice(pair * PAIR, (pair + 1) * PAIR)
        q_s[:, cols] = (unstack_heads(acc_s[pair].T) * scale).astype(bf16)
    dq = q_s[...]
    before = prev_refs[hops] if prev > 1 else prev_refs[0]
    dw_s[:, :width] = tn(x_refs[hops][...], dq)
    dw_s[:, width:] = jnp.zeros((full_width, 2 * width), f32)
    db_s[...] = jnp.zeros(db_s.shape, f32)
    db_s[0:1, cols_all] = jnp.sum(dq.astype(f32), axis=0, keepdims=True)
    out_refs[hops][...] = before[...] + nt(dq, w_ref[:, :width])
    for at in range(count):
        here = pl.ds(at * block, block)

        @pl.when(actives[at])
        def _():
            x = x_refs[at][...]
            dk = dk_s[here, :].astype(bf16)
            dv = dv_s[here, :].astype(bf16)
            db_s[1:2, cols_all] += jnp.sum(dv.astype(f32), axis=0, keepdims=True)
            back = nt(dk, w_ref[:, width : 2 * width]) + nt(dv, w_ref[:, 2 * width :])
            if at == hops:
                out_refs[at][...] += back
            else:
                if prev > 1:
                    back = back + prev_refs[at][...].astype(f32)
                out_refs[at][...] = back.astype(bf16)
            dw_s[:, width : 2 * width] += tn(x, dk)
            dw_s[:, 2 * width :] += tn(x, dv)

        if at != hops:
            @pl.when(jnp.logical_not(actives[at]))
            def _():
                if prev > 1:
                    out_refs[at][...] = prev_refs[at][...]
                else:
                    out_refs[at][...] = jnp.zeros((block, full_width), bf16)

    put_halves(core_ref[0], keep_ref, send_ref, slice(0, 3 * width), dw_s[...].astype(bf16))
    side = jnp.concatenate([db_s[...], jnp.zeros((120, full_width), f32)], axis=0).T
    put_halves(core_ref[0], keep_ref, send_ref, slice(3 * width, 3 * width + 128), side.astype(bf16))


def whole():
    return pl.BlockSpec(memory_space=pltpu.VMEM)


def smem():
    return pl.BlockSpec(memory_space=pltpu.SMEM)


def raw():
    return pl.BlockSpec(memory_space=pl.ANY)


def attend_forward(span, mask, window, weight, biases):
    bounds, segq, segk = mask
    offsets, pieces = weight
    first, pairs = span
    count = len(window)
    block, full_width = window[0].shape
    width = pairs * PAIR
    padded = count * block + TK_FWD - ALIGN
    return pl.pallas_call(
        functools.partial(forward_kernel, count // 2, len(pieces), first),
        out_shape=(
            jax.ShapeDtypeStruct((block, width), bf16),
            jax.ShapeDtypeStruct((8, 2 * block), f32),
        ),
        in_specs=[smem()] * 2 + [whole()] * count + [raw()] * len(pieces) + [whole()] * 3,
        out_specs=(whole(), whole()),
        scratch_shapes=[
            pltpu.VMEM((full_width, 3 * width), bf16),
            pltpu.VMEM((block, width), bf16),
            pltpu.VMEM((2 * block, width), bf16),
            pltpu.VMEM((padded, width), bf16),
            pltpu.VMEM((padded, width), bf16),
            pltpu.VMEM((8, 2 * block), f32),
            pltpu.VMEM((8, 2 * block), f32),
            pltpu.VMEM((pairs, PAIR, 2 * block), f32),
            pltpu.SemaphoreType.DMA((count_pieces(pieces), 3)),
        ],
        compiler_params=pltpu.CompilerParams(vmem_limit_bytes=VMEM_LIMIT),
        cost_estimate=pl.CostEstimate(
            flops=2_500_000_000 * pairs, bytes_accessed=8_000_000, transcendentals=4_000_000
        ),
        name="attend_forward",
    )(bounds, offsets, *window, *pieces, biases, segq, segk)


def attend_backward(core, span, mask, window, weight, biases, attended, grad, before):
    bounds, segq, segk = mask
    offsets, pieces = weight
    first, pairs = span
    count = len(window)
    block, full_width = window[0].shape
    width = pairs * PAIR
    hops = count // 2
    padded = count * block + TK_BWD - ALIGN
    per_part = full_width // PAIR // len(attended)
    mixed, lse = attended[first // per_part]
    at = first // per_part * per_part
    outs = [
        jax.ShapeDtypeStruct((block, full_width), f32 if at == hops else bf16) for at in range(count)
    ]
    return pl.pallas_call(
        functools.partial(backward_kernel, hops, len(pieces), len(before), first, first - at),
        out_shape=(
            *outs,
            jax.ShapeDtypeStruct((2, full_width // 4, 3 * width + 128), bf16),
            jax.ShapeDtypeStruct((2, full_width // 4, 3 * width + 128), bf16),
        ),
        in_specs=[smem()] * 3
        + [whole()] * count
        + [raw()] * len(pieces)
        + [whole()] * (6 + len(before)),
        out_specs=(whole(),) * (count + 2),
        scratch_shapes=[
            pltpu.VMEM((full_width, 3 * width), bf16),
            pltpu.VMEM((block, width), bf16),
            pltpu.VMEM((2 * block, width), bf16),
            pltpu.VMEM((2 * block, width), bf16),
            pltpu.VMEM((padded, width), bf16),
            pltpu.VMEM((padded, width), bf16),
            pltpu.VMEM((padded, width), f32),
            pltpu.VMEM((padded, width), f32),
            pltpu.VMEM((full_width, 3 * width), f32),
            pltpu.VMEM((8, 2 * block), f32),
            pltpu.VMEM((pairs, PAIR, 2 * block), f32),
            pltpu.VMEM((8, full_width), f32),
            pltpu.SemaphoreType.DMA((count_pieces(pieces), 3)),
        ],
        compiler_params=pltpu.CompilerParams(vmem_limit_bytes=VMEM_LIMIT),
        cost_estimate=pl.CostEstimate(
            flops=5_000_000_000 * pairs, bytes_accessed=20_000_000, transcendentals=4_000_000
        ),
        name="attend_backward",
    )(bounds, offsets, core, *window, *pieces, biases, segq, segk, mixed, lse, grad, *before)


def join(refs):
    if len(refs) == 1:
        return refs[0][...]
    return jnp.concatenate([ref[...] for ref in refs], axis=1)


def middle_kernel(
    counts, offsets, tokens_ref, cot_ref, vec_ref, upb_ref, *refs
):
    n_mixed, n_shared, n_down = counts
    mixed_refs, refs = refs[:n_mixed], refs[n_mixed:]
    out_own, up_own, refs = refs[0], refs[1], refs[2:]
    shared, down_p = split_pieces(refs[:n_shared]), split_pieces(refs[n_shared : n_shared + n_down])
    refs = refs[n_shared + n_down :]
    n_shared = len(shared)
    (
        result_ref, one_ref, mixed_ref, branch_ref, hidden_ref, inner_ref, act_ref, two_ref,
        small_ref, gupb_ref,
    ) = refs[:10]
    wo_s, up_s, down_s, slope_s, sems = refs[10:]
    width = wo_s.shape[1]
    out_copies, up_copies, down_copies = [], [], []

    def begin(copies, at, source, target):
        row = pl.multiple_of(offsets[at], ROW_STEP)
        copy = pltpu.make_async_copy(
            source, target.at[pl.ds(row, source.shape[0]), :], sems.at[at, len(copies) % 2]
        )
        copy.start()
        copies.append(copy)

    begin(out_copies, 0, out_own, wo_s)
    for at, piece in enumerate(shared):
        row = pl.multiple_of(offsets[2 + at], ROW_STEP)
        copy = pltpu.make_async_copy(
            piece.at[:, pl.ds(0, width)], wo_s.at[pl.ds(row, piece.shape[0]), :], sems.at[2 + at, 0]
        )
        copy.start()
        out_copies.append(copy)
    begin(up_copies, 1, up_own, up_s)
    for at, piece in enumerate(shared):
        row = pl.multiple_of(offsets[2 + at], ROW_STEP)
        copy = pltpu.make_async_copy(
            piece.at[:, pl.ds(width, up_s.shape[1])],
            up_s.at[pl.ds(row, piece.shape[0]), :],
            sems.at[2 + at, 1],
        )
        copy.start()
        up_copies.append(copy)
    for at, piece in enumerate(down_p):
        row = pl.multiple_of(offsets[2 + n_shared + at], ROW_STEP)
        copy = pltpu.make_async_copy(
            piece, down_s.at[pl.ds(row, piece.shape[0]), :], sems.at[2 + n_shared + at, 0]
        )
        copy.start()
        down_copies.append(copy)
    inner_width = up_s.shape[1]
    tile = inner_width // FF_TILES
    out_bias, norm_gain, norm_shift = vec_ref[0:1, :], vec_ref[1:2, :], vec_ref[2:3, :]
    down_bias, final_gain, final_shift = vec_ref[3:4, :], vec_ref[4:5, :], vec_ref[5:6, :]
    wait_all(out_copies)
    values = tokens_ref[...].astype(f32) + (nn(join(mixed_refs), wo_s[...]) + out_bias)
    centered = values - jnp.mean(values, axis=1, keepdims=True)
    inverse_one = lax.rsqrt(jnp.mean(centered * centered, axis=1, keepdims=True) + epsilon)
    normed_one = centered * inverse_one
    hidden = normed_one * norm_gain + norm_shift
    hidden_low = hidden.astype(bf16)
    hidden_ref[...] = hidden_low
    wait_all(up_copies)
    branch_two = None
    for at in range(FF_TILES):
        cols = slice(at * tile, (at + 1) * tile)
        inner = nn(hidden_low, up_s[:, cols]) + upb_ref[0:1, cols]
        normal = 0.5 * (1.0 + lax.erf(inner * 0.7071067811865476))
        density = jnp.exp(-0.5 * inner * inner) * 0.3989422804014327
        slope_s[:, cols] = normal + inner * density
        activated = (inner * normal).astype(bf16)
        act_ref[:, cols] = activated
        if at == 0:
            wait_all(down_copies)
        term = nn(activated, down_s[cols, :])
        branch_two = term if branch_two is None else branch_two + term
    values = hidden + (branch_two + down_bias)
    centered = values - jnp.mean(values, axis=1, keepdims=True)
    inverse_two = lax.rsqrt(jnp.mean(centered * centered, axis=1, keepdims=True) + epsilon)
    normed_two = centered * inverse_two
    result_ref[...] = (normed_two * final_gain + final_shift).astype(bf16)
    cot = cot_ref[...].astype(f32)
    small_ref[4:5, :] = jnp.sum(cot * normed_two, axis=0, keepdims=True)
    small_ref[5:6, :] = jnp.sum(cot, axis=0, keepdims=True)
    scaled = cot * final_gain
    first = jnp.mean(scaled, axis=1, keepdims=True)
    second = jnp.mean(scaled * normed_two, axis=1, keepdims=True)
    grad_two = inverse_two * (scaled - first - normed_two * second)
    grad_low = grad_two.astype(bf16)
    two_ref[...] = grad_low
    small_ref[3:4, :] = jnp.sum(grad_low.astype(f32), axis=0, keepdims=True)
    grad_hidden = grad_two
    gupb_ref[...] = jnp.zeros(gupb_ref.shape, f32)
    for at in range(FF_TILES):
        cols = slice(at * tile, (at + 1) * tile)
        grad_inner = (nt(grad_low, down_s[cols, :]) * slope_s[:, cols]).astype(bf16)
        inner_ref[:, cols] = grad_inner
        gupb_ref[0:1, cols] = jnp.sum(grad_inner.astype(f32), axis=0, keepdims=True)
        grad_hidden = grad_hidden + nt(grad_inner, up_s[:, cols])
    small_ref[1:2, :] = jnp.sum(grad_hidden * normed_one, axis=0, keepdims=True)
    small_ref[2:3, :] = jnp.sum(grad_hidden, axis=0, keepdims=True)
    scaled = grad_hidden * norm_gain
    first = jnp.mean(scaled, axis=1, keepdims=True)
    second = jnp.mean(scaled * normed_one, axis=1, keepdims=True)
    grad_one = inverse_one * (scaled - first - normed_one * second)
    one_ref[...] = grad_one
    grad_branch = grad_one.astype(bf16)
    branch_ref[...] = grad_branch
    small_ref[0:1, :] = jnp.sum(grad_branch.astype(f32), axis=0, keepdims=True)
    small_ref[6:8, :] = jnp.zeros((2, small_ref.shape[1]), f32)
    mixed_ref[...] = nt(grad_branch, wo_s[...]).astype(bf16)


def middle(attended, tokens, cotangent, weights, vectors, up_bias):
    offsets, out_own, up_own, shared, down = weights
    counts = (len(attended), len(shared), len(down))
    pieces = [out_own, up_own, *shared, *down]
    block, width = tokens.shape
    inner_width = up_bias.shape[1]
    return pl.pallas_call(
        functools.partial(middle_kernel, counts),
        out_shape=(
            jax.ShapeDtypeStruct((block, width), bf16),
            jax.ShapeDtypeStruct((block, width), f32),
            jax.ShapeDtypeStruct((block, width), bf16),
            jax.ShapeDtypeStruct((block, width), bf16),
            jax.ShapeDtypeStruct((block, width), bf16),
            jax.ShapeDtypeStruct((block, inner_width), bf16),
            jax.ShapeDtypeStruct((block, inner_width), bf16),
            jax.ShapeDtypeStruct((block, width), bf16),
            jax.ShapeDtypeStruct((8, width), f32),
            jax.ShapeDtypeStruct((8, inner_width), f32),
        ),
        in_specs=[smem()] + [whole()] * (4 + len(attended)) + [raw()] * len(pieces),
        out_specs=(whole(),) * 10,
        scratch_shapes=[
            pltpu.VMEM((width, width), bf16),
            pltpu.VMEM((width, inner_width), bf16),
            pltpu.VMEM((inner_width, width), bf16),
            pltpu.VMEM((block, inner_width), f32),
            pltpu.SemaphoreType.DMA((count_pieces(pieces), 2)),
        ],
        compiler_params=pltpu.CompilerParams(vmem_limit_bytes=VMEM_LIMIT),
        cost_estimate=pl.CostEstimate(flops=24_000_000_000, bytes_accessed=20_000_000, transcendentals=4_000_000),
        name="middle",
    )(offsets, tokens, cotangent, vectors, up_bias, *attended, *pieces)


def grad_down_kernel(micro, core_ref, *refs):
    act_refs, two_refs, side_ref = refs[:micro], refs[micro : 2 * micro], refs[-3]
    total = sum(tn(act[...], two[...]) for act, two in zip(act_refs, two_refs))
    rows, width = total.shape
    side = jnp.concatenate([side_ref[...], jnp.zeros((120, rows), f32)], axis=0).T

    def put(ref):
        ref[0, :, :width] = total.astype(bf16)
        ref[0, :, width:] = side.astype(bf16)

    @pl.when(pl.program_id(0) % 2 == 0)
    def _():
        put(refs[-1])

    @pl.when(pl.program_id(0) % 2 == 1)
    def _():
        put(refs[-2])


def put_halves(core, keep_ref, send_ref, cols, value):
    rows, width = value.shape
    halves = value.reshape(2, 2, rows // 4, width)

    @pl.when(core == 0)
    def _():
        keep_ref[:, :, cols] = halves[:, 0]
        send_ref[:, :, cols] = halves[:, 1]

    @pl.when(core == 1)
    def _():
        keep_ref[:, :, cols] = halves[:, 1]
        send_ref[:, :, cols] = halves[:, 0]


def weight_grad_down(core, activated, grad_low, side):
    micro = len(activated)
    block, inner_width = activated[0].shape
    width = grad_low[0].shape[1]
    tile = inner_width // 4

    def spot(at, core_ref):
        core = core_ref[0]
        return (0, 2 * (at // 2) + jnp.where(at % 2 == 0, 1 - core, core))

    half = jax.ShapeDtypeStruct((2, tile, width + 128), bf16)
    return pl.pallas_call(
        functools.partial(grad_down_kernel, micro),
        out_shape=(half, half),
        grid_spec=pltpu.PrefetchScalarGridSpec(
            num_scalar_prefetch=1,
            grid=(4,),
            in_specs=[pl.BlockSpec((block, tile), spot)] * micro
            + [pl.BlockSpec((block, width), lambda at, core_ref: (0, 0))] * micro
            + [pl.BlockSpec((8, tile), spot)],
            out_specs=[pl.BlockSpec((1, tile, width + 128), lambda at, core_ref: (at // 2, 0, 0))] * 2,
        ),
        compiler_params=pltpu.CompilerParams(vmem_limit_bytes=VMEM_LIMIT),
        cost_estimate=pl.CostEstimate(flops=5_400_000_000, bytes_accessed=14_000_000, transcendentals=0),
        name="weight_grad_down",
    )(core, *activated, *grad_low, side)


def grad_up_kernel(counts, core_ref, *refs):
    micro = len(counts)
    hidden, inner, branch = (refs[at * micro : (at + 1) * micro] for at in range(3))
    keep_ref, send_ref, refs = refs[-2], refs[-1], refs[3 * micro : -2]
    mixed = []
    for size in counts:
        mixed.append(refs[:size])
        refs = refs[size:]
    last = pl.num_programs(0) - 1
    core = core_ref[0]

    @pl.when(pl.program_id(0) < last)
    def _():
        total = sum(tn(one[...], two[...]) for one, two in zip(hidden, inner))
        put_halves(core, keep_ref, send_ref, slice(None), total.astype(bf16))

    @pl.when(pl.program_id(0) == last)
    def _():
        total = sum(tn(join(one), two[...]) for one, two in zip(mixed, branch))
        put_halves(core, keep_ref, send_ref, slice(None), total.astype(bf16))


def weight_grad_up(core, hidden_low, grad_inner, attended, grad_branch):
    micro = len(hidden_low)
    block, width = hidden_low[0].shape
    tiles = grad_inner[0].shape[1] // width
    fixed = [pl.BlockSpec((block, width), lambda at, core_ref: (0, 0))] * micro
    parts = [part for one in attended for part in one]
    half = jax.ShapeDtypeStruct((2, width // 4, (tiles + 1) * width), bf16)
    return pl.pallas_call(
        functools.partial(grad_up_kernel, tuple(len(one) for one in attended)),
        out_shape=(half, half),
        grid_spec=pltpu.PrefetchScalarGridSpec(
            num_scalar_prefetch=1,
            grid=(tiles + 1,),
            in_specs=fixed
            + [pl.BlockSpec((block, width), lambda at, core_ref: (0, jnp.minimum(at, tiles - 1)))] * micro
            + fixed
            + [pl.BlockSpec(part.shape, lambda at, core_ref: (0, 0)) for part in parts],
            out_specs=[pl.BlockSpec((2, width // 4, width), lambda at, core_ref: (0, 0, at))] * 2,
        ),
        compiler_params=pltpu.CompilerParams(vmem_limit_bytes=VMEM_LIMIT),
        cost_estimate=pl.CostEstimate(flops=6_800_000_000, bytes_accessed=16_000_000, transcendentals=0),
        name="weight_grad_up",
    )(core, *hidden_low, *grad_inner, *grad_branch, *parts)


def permute(value, axis, pairs):
    return lax.ppermute(value, axis, pairs)


def swap_pairs(size, distance):
    return [(at, at ^ distance) for at in range(size)]


def shift_pairs(size, by):
    return [(at, at + by) for at in range(size) if 0 <= at + by < size]


def pick(array, index, axis=0):
    return lax.dynamic_index_in_dim(array, index, axis, keepdims=False)


def ordered(first_here, mine, other, axis=0):
    first = jnp.where(first_here, mine, other)
    second = jnp.where(first_here, other, mine)
    return jnp.concatenate([first, second], axis=axis)


def two_level(mesh_shape):
    return mesh_shape["replica"] == 4 and mesh_shape["fsdp"] == 2 and mesh_shape["seq"] == 4


def sync(*values):
    return lax.optimization_barrier(values)


class Fetch:
    def __init__(self, fast):
        self.fast = fast
        self.here = lax.axis_index("fsdp")
        self.spot = 2 * lax.axis_index("x") + lax.axis_index("core") if fast else None

    def quarter(self, shard):
        if not self.fast:
            return shard
        size = shard.shape[0] // 4
        return lax.dynamic_slice_in_dim(shard, self.spot * size, size, 0)

    def far(self, quarter):
        if not self.fast:
            return [lax.all_gather(quarter, "fsdp", axis=0, tiled=True)]
        return [permute(quarter, "fsdp", swap_pairs(2, 1))]

    def across(self, held):
        if not self.fast:
            return held
        return held + [permute(held[0], "x", swap_pairs(2, 1))]

    def beside(self, held):
        if not self.fast:
            return held
        pair = jnp.stack(held)
        return [pair, permute(pair, "core", swap_pairs(2, 1))]

    def offsets(self, rows):
        size = rows // 4
        there = (1 - self.here) * rows
        return [self.here * rows], [there + (self.spot ^ flip) * size for flip in (0, 2, 1, 3)]

    def one_weight(self, shard, held):
        if not self.fast:
            return jnp.zeros((1,), jnp.int32), held
        mine, others = self.offsets(shard.shape[0])
        return jnp.stack(mine + others).astype(jnp.int32), [shard] + held

    def middle_weights(self, out_shard, up_shard, down_shard, shared, down):
        if not self.fast:
            width = shared[0].shape[0]
            return (jnp.zeros((3,), jnp.int32), shared[0][:, :width], shared[0][:, width:], [], down)
        mine, others = self.offsets(out_shard.shape[0])
        own, rest = self.offsets(down_shard.shape[0])
        offsets = jnp.stack(mine + mine + others + own + rest).astype(jnp.int32)
        return offsets, out_shard, up_shard, shared, [down_shard] + down

    def with_vectors(self, quarter, shards):
        if not self.fast:
            return quarter
        return jnp.concatenate([quarter, jnp.concatenate(shards).reshape(-1, quarter.shape[1])], axis=0)

    def without_vectors(self, held, shards):
        if not self.fast:
            return held, [lax.all_gather(shard, "fsdp", axis=0, tiled=True) for shard in shards]
        moved = held[0]
        rows = sum(shard.shape[0] for shard in shards) // moved.shape[1]
        far = moved[moved.shape[0] - rows :].reshape(-1)
        full, at = [], 0
        for shard in shards:
            size = shard.shape[0]
            full.append(ordered(self.here == 0, shard, far[at : at + size]))
            at += size
        return [moved[: moved.shape[0] - rows]], full


def add_low(left, right):
    return (left.astype(f32) + right.astype(f32)).astype(bf16)


class Chain:
    def __init__(self, fast, *parts):
        self.fast = fast
        self.name = None
        self.pair = list(parts)

    def settle(self):
        name, pair = self.name, self.pair
        if name in ("core", "y", "x", "z1", "z2"):
            return add_low(*pair)
        if name == "z3":
            return ordered(lax.axis_index("seq") % 2 == 0, *pair)
        if name == "spread_x":
            return both_ways(lax.axis_index("x") == 0, *pair)
        return both_ways(lax.axis_index("core") == 0, *pair)

    def slices(self, index, dim):
        parts = [pick(part, index, dim) for part in self.pair]
        if self.name in ("core", "y", "x"):
            return add_low(*parts)
        return pick(self.settle(), index, dim)

    def go(self, name):
        if not self.fast:
            return
        if name == "core":
            keep, send = (
                sum(part[at].astype(f32) for part in self.pair).astype(bf16) if len(self.pair) > 1 else self.pair[0][at]
                for at in (0, 1)
            )
            self.name = name
            moved = permute(send, "core", swap_pairs(2, 1))
            split = lambda one: one.reshape(2, 2, one.shape[1] // 2, one.shape[2])
            self.pair = (split(keep), split(moved))
            return
        if name in ("z2", "z3", "spread_x", "spread_core"):
            held = self.settle()
            axis = {"z2": "seq", "z3": "seq", "spread_x": "x", "spread_core": "core"}[name]
            pairs = {"z2": swap_pairs(4, 2), "z3": swap_pairs(4, 1)}.get(name, swap_pairs(2, 1))
            self.name, self.pair = name, (held, permute(held, axis, pairs))
            return
        axis, dim = {"y": ("fsdp", 0), "x": ("x", 0), "z1": ("seq", 0)}[name]
        here = lax.axis_index(axis)
        if name == "z1":
            here = here % 2
            self.pair = [part.reshape(2, part.shape[0] // 2, part.shape[1]) for part in self.pair]
        sent = self.slices(1 - here, dim)
        pairs = swap_pairs(4 if axis == "seq" else 2, 1)
        moved = permute(sent, axis, pairs)
        self.pair = (self.slices(here, dim), moved)
        self.name = name

    def final(self):
        if not self.fast:
            keep, send = (sum(part[at].astype(f32) for part in self.pair) for at in (0, 1))
            parts = jnp.stack([keep, send], axis=1).astype(bf16)
            share = lax.psum_scatter(
                parts.reshape(-1, parts.shape[3]), "fsdp", scatter_dimension=0, tiled=True
            )
            return lax.psum(share, ("replica", "seq")).astype(f32)
        full = self.settle()
        return full.reshape(-1, full.shape[-1]).astype(f32)


def both_ways(first_here, mine, other):
    return jnp.stack([jnp.where(first_here, mine, other), jnp.where(first_here, other, mine)])


def settle_all(chains, *values):
    pairs, *values = sync([chain.pair for chain in chains], *values)
    for chain, pair in zip(chains, pairs):
        chain.pair = pair
    return values


def body(
    fast,
    tokens,
    segment_ids,
    joined_weight,
    query_bias,
    value_bias,
    out_weight,
    out_bias,
    norm_gain,
    norm_shift,
    up_weight,
    up_bias,
    down_weight,
    down_bias,
    final_gain,
    final_shift,
    cotangent,
):
    micro, block, width = tokens.shape[1:]
    length = segment_ids.shape[-1]
    size = lax.axis_size("seq")
    place = lax.axis_index("seq")
    hops = min(size - 1, (length // 2 - 2) // block + 1)
    count = 2 * hops + 1
    inner_width = up_weight.shape[1]
    all_pairs = width // PAIR
    half_pairs = all_pairs // 2
    spans = [(0, half_pairs), (half_pairs, half_pairs)]
    fetch = Fetch(fast)

    masks = []
    for batch in range(micro):
        ids = segment_ids[0, batch]
        padded = jnp.concatenate(
            [jnp.full((hops * block,), -1, jnp.int32), ids, jnp.full((hops * block,), 1000, jnp.int32)]
        )
        near = lax.dynamic_slice_in_dim(padded, place * block, count * block, 0)
        rows = lax.dynamic_slice_in_dim(ids, place * block, block, 0)
        bounds = jnp.stack([jnp.sum(near < rows[0]), jnp.sum(near <= rows[-1])]).astype(jnp.int32)
        segq = jnp.broadcast_to(rows[None, :], (8, block))
        tail = jnp.full((TK_FWD - ALIGN,), 1000, jnp.int32)
        segk = jnp.broadcast_to(jnp.concatenate([near, tail])[:, None], (count * block + TK_FWD - ALIGN, 128))
        masks.append((bounds, segq, segk))

    own = [tokens[0, batch] for batch in range(micro)]
    moves = [None] * micro
    small_shards = [
        query_bias,
        value_bias,
        out_bias,
        norm_gain,
        norm_shift,
        down_bias,
        final_gain,
        final_shift,
        up_bias,
    ]
    def hop_out(batch, step):
        left, right = moves[batch] or ([own[batch]], [own[batch]])
        moves[batch] = (
            left + [permute(left[-1], "seq", shift_pairs(size, 1))],
            right + [permute(right[-1], "seq", shift_pairs(size, -1))],
        )

    joined = fetch.far(fetch.with_vectors(fetch.quarter(joined_weight), small_shards))
    hop_out(0, 0)
    quarters = [
        jnp.concatenate([fetch.quarter(out_weight), fetch.quarter(up_weight)], axis=1),
        fetch.quarter(down_weight),
    ]
    joined, quarters, moves[0] = sync(joined, quarters, moves[0])
    joined, vectors = fetch.without_vectors(joined, small_shards)
    joined = fetch.across(joined)
    for step in range(1, hops):
        hop_out(0, step)
    shared = fetch.far(quarters[0])
    joined, quarters = sync(joined, quarters)
    joined = fetch.beside(joined)
    biases = jnp.pad(jnp.stack(vectors[:2]).astype(f32), ((0, 6), (0, 0)))
    rows_six = jnp.pad(jnp.stack(vectors[2:8]).astype(f32), ((0, 2), (0, 0)))
    up_row = jnp.pad(vectors[8].astype(f32)[None, :], ((0, 7), (0, 0)))
    moves[0], joined, own[1:], biases, rows_six, up_row, masks, quarters = sync(
        moves[0], joined, own[1:], biases, rows_six, up_row, masks, quarters
    )

    attended = [[] for _ in range(micro)]
    def window(batch):
        left, right = moves[batch]
        return left[:0:-1] + [left[0]] + right[1:]

    windows = [window(0)] + [None] * (micro - 1)
    weight = fetch.one_weight(joined_weight, joined)

    shared = fetch.across(shared)
    down = fetch.far(quarters[1])
    if micro > 1:
        hop_out(1, 0)
    attended[0].append(tuple(attend_forward(spans[0], masks[0], windows[0], weight, biases)))
    attended[0], shared, down, masks, windows[0], moves[1:2] = sync(
        attended[0], shared, down, masks, windows[0], moves[1:2]
    )
    down = fetch.across(down)
    shared = fetch.beside(shared)
    for step in range(1, hops if micro > 1 else 0):
        hop_out(1, step)
    attended[0].append(tuple(attend_forward(spans[1], masks[0], windows[0], weight, biases)))
    attended[0], moves[1:2], shared, down = sync(attended[0], moves[1:2], shared, down)
    down = fetch.beside(down)
    attended[0], down, own = sync(attended[0], down, own)
    middle_weights = fetch.middle_weights(out_weight, up_weight, down_weight, shared, down)

    middles = []
    for batch in range(micro):
        later = batch + 1
        if batch > 0:
            windows[batch] = window(batch)
            for step in range(1, hops if later < micro else 0):
                hop_out(later, step)
            attended[batch].append(
                tuple(attend_forward((0, all_pairs), masks[batch], windows[batch], weight, biases))
            )
            if later < micro:
                attended[batch], moves[later] = sync(attended[batch], moves[later])
        if later + 1 < micro:
            hop_out(later + 1, 0)
        middles.append(
            middle(
                [one[0] for one in attended[batch]],
                own[batch],
                cotangent[0, batch],
                middle_weights,
                rows_six,
                up_row,
            )
        )
        if later + 1 < micro:
            middles[-1], masks, moves[later + 1] = sync(middles[-1], masks, moves[later + 1])
        else:
            middles[-1], masks = sync(middles[-1], masks)

    core = lax.axis_index("core") if fast else jnp.zeros((), jnp.int32)
    core = core.astype(jnp.int32).reshape(1)
    outs = list(zip(*middles))
    small = sum(outs[8])
    grad_upb = sum(outs[9])
    half = width // 2
    gap = inner_width // 2 - half
    spread = jnp.pad(small[:6].reshape(6, 2, half), ((0, 0), (0, 0), (0, gap))).reshape(6, inner_width)
    side = jnp.concatenate([grad_upb[:1], spread, jnp.zeros((1, inner_width), f32)], axis=0)
    down = Chain(fast, weight_grad_down(core, outs[6], outs[7], side))
    up_ins = (outs[4], outs[5], [[part[0] for part in one] for one in attended], outs[3])
    (up_ins,) = settle_all([down], up_ins)
    down.go("core")
    up = Chain(fast, weight_grad_up(core, *up_ins))
    (masks,) = settle_all([down, up], list(masks))

    backs = [None] * micro
    coming = [None] * micro
    joined_sums = [[], []]
    last = micro - 1

    def run_back(which, batch, chains, moving=()):
        before = [outs[1][batch]] if which == 0 else backs[batch]
        *parts, keep, send = attend_backward(
            core, spans[which], masks[batch], windows[batch], weight, biases, attended[batch], outs[2][batch], before
        )
        moved = [coming[at] for at in moving]
        backs[batch], grad_joined, masks[:], moved = settle_all(chains, parts, (keep, send), list(masks), moved)
        for at, one in zip(moving, moved):
            coming[at] = one
        joined_sums[which].append(grad_joined)

    def send_back(batch):
        coming[batch] = [
            permute(backs[batch][hops + far], "seq", shift_pairs(size, far))
            for far in range(-hops, hops + 1)
            if far != 0
        ]

    def total_of(which):
        return Chain(fast, *joined_sums[which])

    def hop_back(batch, step):
        far = hops - step
        sent = []
        for at, by, sign in ((0, 1, 1), (1, -1, -1)):
            part = backs[batch][hops + sign * far]
            if step > 0:
                part = add_low(part, coming[batch][at])
            sent.append(permute(part, "seq", shift_pairs(size, by)))
        coming[batch] = sent

    down.go("y")
    up.go("core")
    run_back(0, 0, [up, down])
    down.go("x")
    up.go("y")
    run_back(1, 0, [down])
    middle_steps = [
        ([(down, "z1")], [down, up]),
        ([(down, "z2"), (up, "x")], [down, up]),
        ([(down, "z3"), (up, "z1")], [down, up]),
        ([(down, "spread_x"), (up, "z2")], [down, up]),
    ]
    for batch in range(1, micro):
        for which in (0, 1):
            begin, end = middle_steps.pop(0) if middle_steps else ([], [])
            for chain, name in begin:
                chain.go(name)
            moving = []
            if which == 0:
                hop_back(batch - 1, 0)
                moving = [batch - 1]
            else:
                for step in range(1, hops):
                    hop_back(batch - 1, step)
                moving = [batch - 1]
            if batch == last and which == 1:
                joined_one = total_of(0)
                joined_one.go("core")
                end = end + [joined_one]
            run_back(which, batch, end, moving)

    joined_two = total_of(1)
    joined_two.go("core")
    joined_one.go("y")
    hop_back(last, 0)
    (backs,) = settle_all([joined_two], backs)
    joined_two.go("y")
    up.go("z3")
    down.go("spread_core")
    coming, backs = settle_all([joined_one, down], coming, backs)
    joined_one.go("x")
    for step in range(1, hops):
        hop_back(last, step)
    settle_all([joined_two, joined_one, up])
    joined_two.go("x")
    joined_one.go("z1")
    up.go("spread_x")
    (coming,) = settle_all([joined_two, joined_one], coming)
    joined_two.go("z1")
    joined_one.go("z2")
    settle_all([joined_two, joined_one, up])
    joined_two.go("z2")
    joined_one.go("z3")
    up.go("spread_core")
    settle_all([joined_two, joined_one])
    joined_two.go("z3")
    joined_one.go("spread_x")
    settle_all([joined_two, joined_one])
    joined_two.go("spread_x")
    joined_one.go("spread_core")
    settle_all([joined_two])
    joined_two.go("spread_core")

    final_down = down.final()
    final_up = up.final()
    final_up, final_out = final_up[:, :inner_width], final_up[:, inner_width:]
    final_a, final_b = joined_one.final(), joined_two.final()
    grad_tokens = []
    for batch in range(micro):
        total = backs[batch][hops] + sum(one.astype(f32) for one in coming[batch])
        grad_tokens.append(total.astype(bf16))
    low, high = spans[0][1] * PAIR, spans[1][1] * PAIR
    final_joined = jnp.concatenate(
        [
            part
            for at in range(3)
            for part in (final_a[:, at * low : (at + 1) * low], final_b[:, at * high : (at + 1) * high])
        ],
        axis=1,
    )
    bias_sums = final_a[:, 3 * low : 3 * low + 2] + final_b[:, 3 * high : 3 * high + 2]
    if fast:
        own_rows = width // lax.axis_size("fsdp")
        smalls = [final_down[:own_rows, width + 1 + at] for at in range(6)]
    else:
        smalls = [
            lax.psum_scatter(lax.psum(small[at], ("replica", "seq")), "fsdp", scatter_dimension=0, tiled=True)
            for at in range(6)
        ]
    return (
        jnp.stack(outs[0], axis=0)[None],
        jnp.stack(grad_tokens, axis=0)[None],
        final_joined,
        bias_sums[:, 0],
        bias_sums[:, 1],
        final_out,
        smalls[0],
        smalls[1],
        smalls[2],
        final_up,
        final_down[:, width],
        final_down[:, :width],
        smalls[3],
        smalls[4],
        smalls[5],
    )


def solution(mesh):
    fast = two_level(dict(mesh.shape))
    groups = ("replica", "fsdp")
    if fast:
        mesh = jax.sharding.Mesh(mesh.devices.reshape(2, 2, 2, 4), ("x", "core", "fsdp", "seq"))
        groups = ("x", "core", "fsdp")
    rows = P(groups, None, "seq", None)
    matrix, vector = P("fsdp", None), P("fsdp")
    in_specs = (
        rows,
        P(groups, None, None),
        matrix,
        vector,
        vector,
        matrix,
        vector,
        vector,
        vector,
        matrix,
        vector,
        matrix,
        vector,
        vector,
        vector,
        rows,
    )
    out_specs = (
        rows,
        rows,
        matrix,
        vector,
        vector,
        matrix,
        vector,
        vector,
        vector,
        matrix,
        vector,
        matrix,
        vector,
        vector,
        vector,
    )
    return jax.shard_map(
        functools.partial(body, fast),
        mesh=mesh,
        in_specs=in_specs,
        out_specs=out_specs,
        check_vma=False,
    )
```

```python
import functools
import jax
import jax.numpy as jnp
from jax import lax
from jax.experimental import pallas as pl
from jax.experimental.pallas import tpu as pltpu
from jax.sharding import PartitionSpec as P

HEADS = 12
HEAD_DIM = 64
PAIR = 2 * HEAD_DIM
epsilon = 1e-05
masked_score = -1e30
scale = HEAD_DIM ** (-0.5)
TK_FWD = 256
TK_BWD = 256
ALIGN = 128
ROW_STEP = 16
VMEM_LIMIT = 62 * 1024 * 1024
FF_TILES = 4
f32 = jnp.float32
bf16 = jnp.bfloat16


def nt(left, right):
    return lax.dot_general(left, right, (((1,), (1,)), ((), ())), preferred_element_type=f32)


def tn(left, right):
    return lax.dot_general(left, right, (((0,), (0,)), ((), ())), preferred_element_type=f32)


def nn(left, right):
    return lax.dot_general(left, right, (((1,), (0,)), ((), ())), preferred_element_type=f32)


def stack_heads(pair):
    lane = lax.broadcasted_iota(jnp.int32, pair.shape, 1)
    zero = jnp.zeros_like(pair)
    return jnp.concatenate(
        [jnp.where(lane < HEAD_DIM, pair, zero), jnp.where(lane < HEAD_DIM, zero, pair)], axis=0
    )


def unstack_heads(rows):
    half = rows.shape[0] // 2
    lane = lax.broadcasted_iota(jnp.int32, (half, rows.shape[1]), 1)
    return jnp.where(lane < HEAD_DIM, rows[:half], rows[half:])


def split_pieces(refs):
    pieces = []
    for ref in refs:
        if len(ref.shape) == 2:
            pieces.append(ref)
        else:
            pieces.extend(ref.at[at] for at in range(ref.shape[0]))
    return pieces


def count_pieces(arrays):
    return sum(1 if len(one.shape) == 2 else one.shape[0] for one in arrays)


def start_columns(offsets, piece_refs, full_s, sems, width, at_col, size_col):
    copies = []
    for at, piece in enumerate(split_pieces(piece_refs)):
        size = piece.shape[0]
        row = pl.multiple_of(offsets[at], ROW_STEP)
        for part in range(3):
            copy = pltpu.make_async_copy(
                piece.at[:, pl.ds(part * width + at_col, size_col)],
                full_s.at[pl.ds(row, size), pl.ds(part * size_col, size_col)],
                sems.at[at, part],
            )
            copy.start()
            copies.append(copy)
    return copies


def wait_all(copies):
    for copy in copies:
        copy.wait()


def first_row(bounds, at, count, block):
    middle = count // 2
    return pl.multiple_of((middle + bounds[2] * (at - middle)) * block, ALIGN)


def reached(bounds, at, count, block):
    row = first_row(bounds, at, count, block)
    return (bounds[1] > row) & (bounds[0] < row + block)


def block_copy(bounds, x_refs, x_s, sems, at):
    block = x_refs[at].shape[0]
    row = first_row(bounds, at, len(x_refs), block)
    return pltpu.make_async_copy(x_refs[at], x_s.at[pl.ds(row, block), :], sems.at[at])


def fetch_window(bounds, x_refs, x_s, sems):
    for at in range(len(x_refs)):

        @pl.when(reached(bounds, at, len(x_refs), x_refs[at].shape[0]))
        def _():
            block_copy(bounds, x_refs, x_s, sems, at).start()


def project_window(bounds, x_refs, x_s, sems, w_ref, bias_ref, cols, k_s, v_s, tail):
    block = x_refs[0].shape[0]
    width = k_s.shape[1]
    for at in range(len(x_refs)):
        rows = pl.ds(first_row(bounds, at, len(x_refs), block), block)
        active = reached(bounds, at, len(x_refs), block)

        @pl.when(active)
        def _():
            block_copy(bounds, x_refs, x_s, sems, at).wait()
            x = x_s[rows, :]
            both = nn(x, w_ref[:, width:])
            k_s[rows, :] = both[:, :width].astype(bf16)
            v_s[rows, :] = (both[:, width:] + bias_ref[1:2, cols]).astype(bf16)

        @pl.when(jnp.logical_not(active))
        def _():
            k_s[rows, :] = jnp.zeros((block, width), bf16)
            v_s[rows, :] = jnp.zeros((block, width), bf16)

    end = len(x_refs) * block
    k_s[end:, :] = jnp.zeros((tail, width), bf16)
    v_s[end:, :] = jnp.zeros((tail, width), bf16)


def tile_range(bounds, tk):
    low = bounds[0]
    high = bounds[1]
    start = (low // ALIGN) * ALIGN
    return start, (high - start + tk - 1) // tk


def project_queries(x, w_ref, bias_ref, cols, q_s, qq_s):
    width = q_s.shape[1]
    q = nn(x, w_ref[:, :width]) + bias_ref[0:1, cols]
    q_s[...] = q.astype(bf16) * jnp.asarray(scale, bf16)
    for pair in range(width // PAIR):
        here = slice(pair * PAIR, (pair + 1) * PAIR)
        qq_s[:, here] = stack_heads(q_s[:, here])


def forward_kernel(batch, hops, pieces, first, all_bounds, offsets, *refs):
    bounds = [all_bounds[3 * batch + at] for at in range(3)]
    count = 2 * hops + 1
    x_refs = refs[:count]
    w_refs, refs = refs[count : count + pieces], refs[count + pieces :]
    bias_ref, segq_ref, segk_any, o_ref, lse_ref = refs[:5]
    segk_ref, seg_sem, x_s, w_ref, q_s, qq_s, k_s, v_s, top_s, sum_s, acc_s, x_sems, sems = refs[5:]
    seg_copy = pltpu.make_async_copy(segk_any.at[batch], segk_ref, seg_sem)
    seg_copy.start()
    block, full_width = x_refs[0].shape
    width = o_ref.shape[1]
    own_rows = slice(hops * block, (hops + 1) * block)
    tk = TK_FWD
    pairs = width // PAIR
    cols_all = slice(first * PAIR, first * PAIR + width)
    copies = start_columns(offsets, w_refs, w_ref, sems, full_width, first * PAIR, width)
    fetch_window(bounds, x_refs, x_s, x_sems)
    wait_all(copies)
    project_window(bounds, x_refs, x_s, x_sems, w_ref, bias_ref, cols_all, k_s, v_s, tk - ALIGN)
    project_queries(x_s[own_rows, :], w_ref, bias_ref, cols_all, q_s, qq_s)
    start, steps = tile_range(bounds, tk)
    seg_copy.wait()
    segq = segq_ref[batch, 0:1, :]
    segq = jnp.concatenate([segq, segq], axis=1)
    top_s[...] = jnp.full(top_s.shape, masked_score, f32)
    sum_s[...] = jnp.ones(sum_s.shape, f32)
    sum_s[:pairs, :] = jnp.zeros((pairs, sum_s.shape[1]), f32)
    acc_s[...] = jnp.zeros(acc_s.shape, f32)

    @pl.loop(0, steps)
    def _(at):
        here = pl.ds(pl.multiple_of(start + at * tk, ALIGN), tk)
        allowed = segk_ref[here, 0:1] == segq
        for pair in range(pairs):
            cols = slice(pair * PAIR, (pair + 1) * PAIR)
            one = slice(pair, pair + 1)
            scores = nt(k_s[here, cols], qq_s[:, cols])
            scores = jnp.where(allowed, scores, masked_score)
            top = top_s[one, :]
            new_top = jnp.maximum(top, jnp.max(scores, axis=0, keepdims=True))
            fade = jnp.exp(top - new_top)
            weights = jnp.exp(scores - new_top)
            top_s[one, :] = new_top
            sum_s[one, :] = sum_s[one, :] * fade + jnp.sum(weights, axis=0, keepdims=True)
            acc_s[pair] = acc_s[pair] * fade + tn(v_s[here, cols], weights.astype(bf16))

    lse_ref[...] = top_s[...] + jnp.log(sum_s[...])
    for pair in range(pairs):
        cols = slice(pair * PAIR, (pair + 1) * PAIR)
        mixed = acc_s[pair] / sum_s[pair : pair + 1, :]
        o_ref[:, cols] = unstack_heads(mixed.T).astype(bf16)


def backward_kernel(batch, hops, pieces, prev, first, skip, all_bounds, offsets, core_ref, *refs):
    bounds = [all_bounds[3 * batch + at] for at in range(3)]
    count = 2 * hops + 1
    x_refs = refs[:count]
    w_refs, refs = refs[count : count + pieces], refs[count + pieces :]
    bias_ref, segq_ref, segk_any, o_ref, lse_ref, do_ref = refs[:6]
    prev_refs, refs = refs[6 : 6 + prev], refs[6 + prev :]
    out_refs, refs = refs[:count], refs[count:]
    keep_ref, send_ref, segk_ref, seg_sem, *refs = refs
    seg_copy = pltpu.make_async_copy(segk_any.at[batch], segk_ref, seg_sem)
    seg_copy.start()
    x_s, p_s, own_s, w_ref, q_s, qq_s, gg_s, k_s, v_s, dk_s, dv_s, dw_s, stat_s, acc_s, db_s = refs[:15]
    x_sems, p_sems, o_sems, sems = refs[15:]
    block, full_width = x_refs[0].shape
    width = q_s.shape[1]
    tk = TK_BWD
    pairs = width // PAIR
    cols_all = slice(first * PAIR, first * PAIR + width)
    own_rows = slice(hops * block, (hops + 1) * block)
    others = [at for at in range(count) if at != hops]
    copies = start_columns(offsets, w_refs, w_ref, sems, full_width, first * PAIR, width)
    fetch_window(bounds, x_refs, x_s, x_sems)
    own_copy = pltpu.make_async_copy(prev_refs[hops if prev > 1 else 0], own_s, p_sems.at[hops])
    own_copy.start()

    def stage(at):
        return p_s.at[pl.ds(at * block, block), :]

    def prev_copy(at):
        return pltpu.make_async_copy(prev_refs[at], stage(at), p_sems.at[at])

    def out_copy(at):
        return pltpu.make_async_copy(own_s if at == hops else stage(at), out_refs[at], o_sems.at[at])

    for at in others:
        active = reached(bounds, at, count, block)
        if prev > 1:

            @pl.when(active)
            def _():
                prev_copy(at).start()

        else:

            @pl.when(jnp.logical_not(active))
            def _():
                p_s[at * block : (at + 1) * block, :] = jnp.zeros((block, full_width), bf16)
                out_copy(at).start()

    dk_s[...] = jnp.zeros(dk_s.shape, f32)
    dv_s[...] = jnp.zeros(dv_s.shape, f32)
    acc_s[...] = jnp.zeros(acc_s.shape, f32)
    for pair in range(pairs):
        cols = slice(pair * PAIR, (pair + 1) * PAIR)
        far = slice((first + pair) * PAIR, (first + pair + 1) * PAIR)
        theirs = slice((skip + pair) * PAIR, (skip + pair + 1) * PAIR)
        grads = stack_heads(do_ref[:, far])
        gg_s[:, cols] = grads
        mixed = o_ref[:, theirs].astype(f32)
        product = grads.astype(f32) * jnp.concatenate([mixed, mixed], axis=0)
        stat_s[pair : pair + 1, :] = jnp.sum(product.T, axis=0, keepdims=True)
    wait_all(copies)
    project_window(bounds, x_refs, x_s, x_sems, w_ref, bias_ref, cols_all, k_s, v_s, tk - ALIGN)
    project_queries(x_s[own_rows, :], w_ref, bias_ref, cols_all, q_s, qq_s)
    start, steps = tile_range(bounds, tk)
    seg_copy.wait()
    segq = segq_ref[batch, 0:1, :]
    segq = jnp.concatenate([segq, segq], axis=1)

    @pl.loop(0, steps)
    def _(at):
        here = pl.ds(pl.multiple_of(start + at * tk, ALIGN), tk)
        allowed = segk_ref[here, 0:1] == segq
        for pair in range(pairs):
            cols = slice(pair * PAIR, (pair + 1) * PAIR)
            keys = k_s[here, cols]
            queries = qq_s[:, cols]
            grads = gg_s[:, cols]
            scores = nt(keys, queries)
            scores = jnp.where(allowed, scores, masked_score)
            weights = jnp.exp(scores - lse_ref[skip + pair : skip + pair + 1, :])
            grad_weights = nt(v_s[here, cols], grads)
            grad_scores = (weights * (grad_weights - stat_s[pair : pair + 1, :])).astype(bf16)
            dv_s[here, cols] += nn(weights.astype(bf16), grads)
            dk_s[here, cols] += nn(grad_scores, queries)
            acc_s[pair] += tn(keys, grad_scores)

    for pair in range(pairs):
        cols = slice(pair * PAIR, (pair + 1) * PAIR)
        q_s[:, cols] = (unstack_heads(acc_s[pair].T) * scale).astype(bf16)
    dq = q_s[...]
    db_s[...] = jnp.zeros(db_s.shape, f32)
    db_s[0:1, cols_all] = jnp.sum(dq.astype(f32), axis=0, keepdims=True)

    def rows_of(at):
        rows = pl.ds(first_row(bounds, at, count, block), block)
        dk = dk_s[rows, :].astype(bf16)
        dv = dv_s[rows, :].astype(bf16)
        db_s[1:2, cols_all] += jnp.sum(dv.astype(f32), axis=0, keepdims=True)
        return [dk, dv]

    grads = jnp.concatenate([dq] + rows_of(hops), axis=1)
    own_copy.wait()
    own_s[...] += nt(grads, w_ref[...])
    out_copy(hops).start()
    dw_s[...] = tn(x_s[own_rows, :], grads)
    for at in others:

        @pl.when(reached(bounds, at, count, block))
        def _():
            rows = slice(at * block, (at + 1) * block)
            grads = jnp.concatenate(rows_of(at), axis=1)
            back = nt(grads, w_ref[:, width:])
            if prev > 1:
                prev_copy(at).wait()
                back = back + p_s[rows, :].astype(f32)
            p_s[rows, :] = back.astype(bf16)
            out_copy(at).start()
            x = x_s[pl.ds(first_row(bounds, at, count, block), block), :]
            dw_s[:, width:] += tn(x, grads)

    put_halves(core_ref[0], keep_ref, send_ref, slice(0, 3 * width), dw_s[...].astype(bf16))
    side = jnp.concatenate([db_s[...], jnp.zeros((120, full_width), f32)], axis=0).T
    put_halves(core_ref[0], keep_ref, send_ref, slice(3 * width, 3 * width + 128), side.astype(bf16))
    out_copy(hops).wait()
    for at in others:
        if prev > 1:

            @pl.when(reached(bounds, at, count, block))
            def _():
                out_copy(at).wait()

        else:
            out_copy(at).wait()


def whole():
    return pl.BlockSpec(memory_space=pltpu.VMEM)


def smem():
    return pl.BlockSpec(memory_space=pltpu.SMEM)


def raw():
    return pl.BlockSpec(memory_space=pl.ANY)


def attend_forward(span, mask, window, weight, biases):
    batch, bounds, segq, segk = mask
    offsets, pieces = weight
    first, pairs = span
    count = len(window)
    block, full_width = window[0].shape
    width = pairs * PAIR
    padded = count * block + TK_FWD - ALIGN
    return pl.pallas_call(
        functools.partial(forward_kernel, batch, count // 2, len(pieces), first),
        out_shape=(
            jax.ShapeDtypeStruct((block, width), bf16),
            jax.ShapeDtypeStruct((8, 2 * block), f32),
        ),
        in_specs=[smem()] * 2
        + [raw()] * (count + len(pieces))
        + [whole(), whole(), raw()],
        out_specs=(whole(), whole()),
        scratch_shapes=[
            pltpu.VMEM(segk.shape[1:], jnp.int32),
            pltpu.SemaphoreType.DMA,
            pltpu.VMEM((count * block, full_width), bf16),
            pltpu.VMEM((full_width, 3 * width), bf16),
            pltpu.VMEM((block, width), bf16),
            pltpu.VMEM((2 * block, width), bf16),
            pltpu.VMEM((padded, width), bf16),
            pltpu.VMEM((padded, width), bf16),
            pltpu.VMEM((8, 2 * block), f32),
            pltpu.VMEM((8, 2 * block), f32),
            pltpu.VMEM((pairs, PAIR, 2 * block), f32),
            pltpu.SemaphoreType.DMA((count,)),
            pltpu.SemaphoreType.DMA((count_pieces(pieces), 3)),
        ],
        compiler_params=pltpu.CompilerParams(vmem_limit_bytes=VMEM_LIMIT),
        cost_estimate=pl.CostEstimate(
            flops=2_500_000_000 * pairs, bytes_accessed=8_000_000, transcendentals=4_000_000
        ),
        name="attend_forward",
    )(bounds, offsets, *window, *pieces, biases, segq, segk)


def attend_backward(core, span, mask, window, weight, biases, attended, grad, before):
    batch, bounds, segq, segk = mask
    offsets, pieces = weight
    first, pairs = span
    count = len(window)
    block, full_width = window[0].shape
    width = pairs * PAIR
    hops = count // 2
    padded = count * block + TK_BWD - ALIGN
    per_part = full_width // PAIR // len(attended)
    mixed, lse = attended[first // per_part]
    at = first // per_part * per_part
    outs = [
        jax.ShapeDtypeStruct((block, full_width), f32 if at == hops else bf16) for at in range(count)
    ]
    return pl.pallas_call(
        functools.partial(backward_kernel, batch, hops, len(pieces), len(before), first, first - at),
        out_shape=(
            *outs,
            jax.ShapeDtypeStruct((2, full_width // 4, 3 * width + 128), bf16),
            jax.ShapeDtypeStruct((2, full_width // 4, 3 * width + 128), bf16),
        ),
        in_specs=[smem()] * 3
        + [raw()] * (count + len(pieces))
        + [whole(), whole(), raw()]
        + [whole()] * 3
        + [raw()] * len(before),
        out_specs=(raw(),) * count + (whole(),) * 2,
        input_output_aliases=(
            {9 + count + len(pieces) + at: at for at in range(count)} if len(before) > 1 else {}
        ),
        scratch_shapes=[
            pltpu.VMEM(segk.shape[1:], jnp.int32),
            pltpu.SemaphoreType.DMA,
            pltpu.VMEM((count * block, full_width), bf16),
            pltpu.VMEM((count * block, full_width), bf16),
            pltpu.VMEM((block, full_width), f32),
            pltpu.VMEM((full_width, 3 * width), bf16),
            pltpu.VMEM((block, width), bf16),
            pltpu.VMEM((2 * block, width), bf16),
            pltpu.VMEM((2 * block, width), bf16),
            pltpu.VMEM((padded, width), bf16),
            pltpu.VMEM((padded, width), bf16),
            pltpu.VMEM((padded, width), f32),
            pltpu.VMEM((padded, width), f32),
            pltpu.VMEM((full_width, 3 * width), f32),
            pltpu.VMEM((8, 2 * block), f32),
            pltpu.VMEM((pairs, PAIR, 2 * block), f32),
            pltpu.VMEM((8, full_width), f32),
            pltpu.SemaphoreType.DMA((count,)),
            pltpu.SemaphoreType.DMA((count,)),
            pltpu.SemaphoreType.DMA((count,)),
            pltpu.SemaphoreType.DMA((count_pieces(pieces), 3)),
        ],
        compiler_params=pltpu.CompilerParams(vmem_limit_bytes=VMEM_LIMIT),
        cost_estimate=pl.CostEstimate(
            flops=5_000_000_000 * pairs, bytes_accessed=20_000_000, transcendentals=4_000_000
        ),
        name="attend_backward",
    )(bounds, offsets, core, *window, *pieces, biases, segq, segk, mixed, lse, grad, *before)


def join(refs):
    if len(refs) == 1:
        return refs[0][...]
    return jnp.concatenate([ref[...] for ref in refs], axis=1)


def middle_kernel(
    counts, offsets, tokens_ref, cot_ref, vec_ref, upb_ref, *refs
):
    n_mixed, n_shared, n_down = counts
    mixed_refs, refs = refs[:n_mixed], refs[n_mixed:]
    out_own, up_own, refs = refs[0], refs[1], refs[2:]
    shared, down_p = split_pieces(refs[:n_shared]), split_pieces(refs[n_shared : n_shared + n_down])
    refs = refs[n_shared + n_down :]
    n_shared = len(shared)
    (
        result_ref, one_ref, mixed_ref, branch_ref, hidden_ref, inner_ref, act_ref, two_ref,
        small_ref, gupb_ref,
    ) = refs[:10]
    wo_s, up_s, down_s, slope_s, act_s, inner_s, leave_sems, sems = refs[10:]
    width = wo_s.shape[1]
    leaving = []
    out_copies, up_copies, down_copies = [], [], []

    def begin(copies, at, source, target):
        row = pl.multiple_of(offsets[at], ROW_STEP)
        copy = pltpu.make_async_copy(
            source, target.at[pl.ds(row, source.shape[0]), :], sems.at[at, len(copies) % 2]
        )
        copy.start()
        copies.append(copy)

    begin(out_copies, 0, out_own, wo_s)
    for at, piece in enumerate(shared):
        row = pl.multiple_of(offsets[2 + at], ROW_STEP)
        copy = pltpu.make_async_copy(
            piece.at[:, pl.ds(0, width)], wo_s.at[pl.ds(row, piece.shape[0]), :], sems.at[2 + at, 0]
        )
        copy.start()
        out_copies.append(copy)
    begin(up_copies, 1, up_own, up_s)
    for at, piece in enumerate(shared):
        row = pl.multiple_of(offsets[2 + at], ROW_STEP)
        copy = pltpu.make_async_copy(
            piece.at[:, pl.ds(width, up_s.shape[1])],
            up_s.at[pl.ds(row, piece.shape[0]), :],
            sems.at[2 + at, 1],
        )
        copy.start()
        up_copies.append(copy)
    for at, piece in enumerate(down_p):
        row = pl.multiple_of(offsets[2 + n_shared + at], ROW_STEP)
        copy = pltpu.make_async_copy(
            piece, down_s.at[pl.ds(row, piece.shape[0]), :], sems.at[2 + n_shared + at, 0]
        )
        copy.start()
        down_copies.append(copy)
    inner_width = up_s.shape[1]
    tile = inner_width // FF_TILES
    out_bias, norm_gain, norm_shift = vec_ref[0:1, :], vec_ref[1:2, :], vec_ref[2:3, :]
    down_bias, final_gain, final_shift = vec_ref[3:4, :], vec_ref[4:5, :], vec_ref[5:6, :]
    wait_all(out_copies)
    values = tokens_ref[...].astype(f32) + (nn(join(mixed_refs), wo_s[...]) + out_bias)
    centered = values - jnp.mean(values, axis=1, keepdims=True)
    inverse_one = lax.rsqrt(jnp.mean(centered * centered, axis=1, keepdims=True) + epsilon)
    normed_one = centered * inverse_one
    hidden = normed_one * norm_gain + norm_shift
    hidden_low = hidden.astype(bf16)
    hidden_ref[...] = hidden_low
    wait_all(up_copies)
    def up_tile(at):
        cols = slice(at * tile, (at + 1) * tile)
        return nn(hidden_low, up_s[:, cols]) + upb_ref[0:1, cols]

    branch_two = None
    inner = up_tile(0)
    wait_all(down_copies)
    for at in range(FF_TILES):
        cols = slice(at * tile, (at + 1) * tile)
        following = up_tile(at + 1) if at + 1 < FF_TILES else None
        normal = 0.5 * (1.0 + lax.erf(inner * 0.7071067811865476))
        density = jnp.exp(-0.5 * inner * inner) * 0.3989422804014327
        slope_s[:, cols] = normal + inner * density
        activated = (inner * normal).astype(bf16)
        act_s[:, cols] = activated
        leaving.append(pltpu.make_async_copy(act_s.at[:, cols], act_ref.at[:, cols], leave_sems.at[0, at]))
        leaving[-1].start()
        term = nn(activated, down_s[cols, :])
        branch_two = term if branch_two is None else branch_two + term
        inner = following
    values = hidden + (branch_two + down_bias)
    centered = values - jnp.mean(values, axis=1, keepdims=True)
    inverse_two = lax.rsqrt(jnp.mean(centered * centered, axis=1, keepdims=True) + epsilon)
    normed_two = centered * inverse_two
    result_ref[...] = (normed_two * final_gain + final_shift).astype(bf16)
    cot = cot_ref[...].astype(f32)
    small_ref[4:5, :] = jnp.sum(cot * normed_two, axis=0, keepdims=True)
    small_ref[5:6, :] = jnp.sum(cot, axis=0, keepdims=True)
    scaled = cot * final_gain
    first = jnp.mean(scaled, axis=1, keepdims=True)
    second = jnp.mean(scaled * normed_two, axis=1, keepdims=True)
    grad_two = inverse_two * (scaled - first - normed_two * second)
    grad_low = grad_two.astype(bf16)
    two_ref[...] = grad_low
    small_ref[3:4, :] = jnp.sum(grad_low.astype(f32), axis=0, keepdims=True)
    grad_hidden = grad_two
    gupb_ref[...] = jnp.zeros(gupb_ref.shape, f32)
    for at in range(FF_TILES):
        cols = slice(at * tile, (at + 1) * tile)
        grad_inner = (nt(grad_low, down_s[cols, :]) * slope_s[:, cols]).astype(bf16)
        inner_s[:, cols] = grad_inner
        leaving.append(pltpu.make_async_copy(inner_s.at[:, cols], inner_ref.at[:, cols], leave_sems.at[1, at]))
        leaving[-1].start()
        gupb_ref[0:1, cols] = jnp.sum(grad_inner.astype(f32), axis=0, keepdims=True)
        grad_hidden = grad_hidden + nt(grad_inner, up_s[:, cols])
    small_ref[1:2, :] = jnp.sum(grad_hidden * normed_one, axis=0, keepdims=True)
    small_ref[2:3, :] = jnp.sum(grad_hidden, axis=0, keepdims=True)
    scaled = grad_hidden * norm_gain
    first = jnp.mean(scaled, axis=1, keepdims=True)
    second = jnp.mean(scaled * normed_one, axis=1, keepdims=True)
    grad_one = inverse_one * (scaled - first - normed_one * second)
    one_ref[...] = grad_one
    grad_branch = grad_one.astype(bf16)
    branch_ref[...] = grad_branch
    small_ref[0:1, :] = jnp.sum(grad_branch.astype(f32), axis=0, keepdims=True)
    small_ref[6:8, :] = jnp.zeros((2, small_ref.shape[1]), f32)
    mixed_ref[...] = nt(grad_branch, wo_s[...]).astype(bf16)
    wait_all(leaving)


def middle(attended, tokens, cotangent, weights, vectors, up_bias):
    offsets, out_own, up_own, shared, down = weights
    counts = (len(attended), len(shared), len(down))
    pieces = [out_own, up_own, *shared, *down]
    block, width = tokens.shape
    inner_width = up_bias.shape[1]
    return pl.pallas_call(
        functools.partial(middle_kernel, counts),
        out_shape=(
            jax.ShapeDtypeStruct((block, width), bf16),
            jax.ShapeDtypeStruct((block, width), f32),
            jax.ShapeDtypeStruct((block, width), bf16),
            jax.ShapeDtypeStruct((block, width), bf16),
            jax.ShapeDtypeStruct((block, width), bf16),
            jax.ShapeDtypeStruct((block, inner_width), bf16),
            jax.ShapeDtypeStruct((block, inner_width), bf16),
            jax.ShapeDtypeStruct((block, width), bf16),
            jax.ShapeDtypeStruct((8, width), f32),
            jax.ShapeDtypeStruct((8, inner_width), f32),
        ),
        in_specs=[smem()] + [whole()] * (4 + len(attended)) + [raw()] * len(pieces),
        out_specs=(whole(),) * 5 + (raw(),) * 2 + (whole(),) * 3,
        scratch_shapes=[
            pltpu.VMEM((width, width), bf16),
            pltpu.VMEM((width, inner_width), bf16),
            pltpu.VMEM((inner_width, width), bf16),
            pltpu.VMEM((block, inner_width), f32),
            pltpu.VMEM((block, inner_width), bf16),
            pltpu.VMEM((block, inner_width), bf16),
            pltpu.SemaphoreType.DMA((2, FF_TILES)),
            pltpu.SemaphoreType.DMA((count_pieces(pieces), 2)),
        ],
        compiler_params=pltpu.CompilerParams(vmem_limit_bytes=VMEM_LIMIT),
        cost_estimate=pl.CostEstimate(flops=24_000_000_000, bytes_accessed=20_000_000, transcendentals=4_000_000),
        name="middle",
    )(offsets, tokens, cotangent, vectors, up_bias, *attended, *pieces)


def grad_down_kernel(micro, core_ref, *refs):
    act_refs, two_refs, side_ref = refs[:micro], refs[micro : 2 * micro], refs[-3]
    total = sum(tn(act[...], two[...]) for act, two in zip(act_refs, two_refs))
    rows, width = total.shape
    side = jnp.concatenate([side_ref[...], jnp.zeros((120, rows), f32)], axis=0).T

    def put(ref):
        ref[0, :, :width] = total.astype(bf16)
        ref[0, :, width:] = side.astype(bf16)

    @pl.when(pl.program_id(0) % 2 == 0)
    def _():
        put(refs[-1])

    @pl.when(pl.program_id(0) % 2 == 1)
    def _():
        put(refs[-2])


def put_halves(core, keep_ref, send_ref, cols, value):
    rows, width = value.shape
    halves = value.reshape(2, 2, rows // 4, width)

    @pl.when(core == 0)
    def _():
        keep_ref[:, :, cols] = halves[:, 0]
        send_ref[:, :, cols] = halves[:, 1]

    @pl.when(core == 1)
    def _():
        keep_ref[:, :, cols] = halves[:, 1]
        send_ref[:, :, cols] = halves[:, 0]


def weight_grad_down(core, activated, grad_low, side):
    micro = len(activated)
    block, inner_width = activated[0].shape
    width = grad_low[0].shape[1]
    tile = inner_width // 4

    def spot(at, core_ref):
        core = core_ref[0]
        return (0, 2 * (at // 2) + jnp.where(at % 2 == 0, 1 - core, core))

    half = jax.ShapeDtypeStruct((2, tile, width + 128), bf16)
    return pl.pallas_call(
        functools.partial(grad_down_kernel, micro),
        out_shape=(half, half),
        grid_spec=pltpu.PrefetchScalarGridSpec(
            num_scalar_prefetch=1,
            grid=(4,),
            in_specs=[pl.BlockSpec((block, tile), spot)] * micro
            + [pl.BlockSpec((block, width), lambda at, core_ref: (0, 0))] * micro
            + [pl.BlockSpec((8, tile), spot)],
            out_specs=[pl.BlockSpec((1, tile, width + 128), lambda at, core_ref: (at // 2, 0, 0))] * 2,
        ),
        compiler_params=pltpu.CompilerParams(vmem_limit_bytes=VMEM_LIMIT),
        cost_estimate=pl.CostEstimate(flops=5_400_000_000, bytes_accessed=14_000_000, transcendentals=0),
        name="weight_grad_down",
    )(core, *activated, *grad_low, side)


def grad_up_kernel(counts, core_ref, *refs):
    micro = len(counts)
    hidden, inner, branch = (refs[at * micro : (at + 1) * micro] for at in range(3))
    keep_ref, send_ref, refs = refs[-2], refs[-1], refs[3 * micro : -2]
    mixed = []
    for size in counts:
        mixed.append(refs[:size])
        refs = refs[size:]
    last = pl.num_programs(0) - 1
    core = core_ref[0]

    @pl.when(pl.program_id(0) < last)
    def _():
        total = sum(tn(one[...], two[...]) for one, two in zip(hidden, inner))
        put_halves(core, keep_ref, send_ref, slice(None), total.astype(bf16))

    @pl.when(pl.program_id(0) == last)
    def _():
        total = sum(tn(join(one), two[...]) for one, two in zip(mixed, branch))
        put_halves(core, keep_ref, send_ref, slice(None), total.astype(bf16))


def weight_grad_up(core, hidden_low, grad_inner, attended, grad_branch):
    micro = len(hidden_low)
    block, width = hidden_low[0].shape
    tiles = grad_inner[0].shape[1] // width
    fixed = [pl.BlockSpec((block, width), lambda at, core_ref: (0, 0))] * micro
    parts = [part for one in attended for part in one]
    half = jax.ShapeDtypeStruct((2, width // 4, (tiles + 1) * width), bf16)
    return pl.pallas_call(
        functools.partial(grad_up_kernel, tuple(len(one) for one in attended)),
        out_shape=(half, half),
        grid_spec=pltpu.PrefetchScalarGridSpec(
            num_scalar_prefetch=1,
            grid=(tiles + 1,),
            in_specs=fixed
            + [pl.BlockSpec((block, width), lambda at, core_ref: (0, jnp.minimum(at, tiles - 1)))] * micro
            + fixed
            + [pl.BlockSpec(part.shape, lambda at, core_ref: (0, 0)) for part in parts],
            out_specs=[pl.BlockSpec((2, width // 4, width), lambda at, core_ref: (0, 0, at))] * 2,
        ),
        compiler_params=pltpu.CompilerParams(vmem_limit_bytes=VMEM_LIMIT),
        cost_estimate=pl.CostEstimate(flops=6_800_000_000, bytes_accessed=16_000_000, transcendentals=0),
        name="weight_grad_up",
    )(core, *hidden_low, *grad_inner, *grad_branch, *parts)


def permute(value, axis, pairs):
    return lax.ppermute(value, axis, pairs)


def swap_pairs(size, distance):
    return [(at, at ^ distance) for at in range(size)]


def even_pairs(size):
    return [(at, at ^ 1) for at in range(size)]


def odd_pairs(size):
    return [(at, min(max(((at + 1) ^ 1) - 1, 0), size - 1)) for at in range(size)]


def pick(array, index, axis=0):
    return lax.dynamic_index_in_dim(array, index, axis, keepdims=False)


def ordered(first_here, mine, other, axis=0):
    first = jnp.where(first_here, mine, other)
    second = jnp.where(first_here, other, mine)
    return jnp.concatenate([first, second], axis=axis)


def two_level(mesh_shape):
    return mesh_shape["replica"] == 4 and mesh_shape["fsdp"] == 2 and mesh_shape["seq"] == 4


def sync(*values):
    return lax.optimization_barrier(values)


class Fetch:
    def __init__(self, fast):
        self.fast = fast
        self.here = lax.axis_index("fsdp")
        self.spot = 2 * lax.axis_index("x") + lax.axis_index("core") if fast else None

    def quarter(self, shard):
        if not self.fast:
            return shard
        size = shard.shape[0] // 4
        return lax.dynamic_slice_in_dim(shard, self.spot * size, size, 0)

    def far(self, quarter):
        if not self.fast:
            return [lax.all_gather(quarter, "fsdp", axis=0, tiled=True)]
        return [permute(quarter, "fsdp", swap_pairs(2, 1))]

    def across(self, held):
        if not self.fast:
            return held
        return held + [permute(held[0], "x", swap_pairs(2, 1))]

    def beside(self, held):
        if not self.fast:
            return held
        pair = jnp.stack(held)
        return [pair, permute(pair, "core", swap_pairs(2, 1))]

    def half(self, shard):
        if not self.fast:
            return shard
        size = shard.shape[0] // 2
        return lax.dynamic_slice_in_dim(shard, lax.axis_index("core") * size, size, 0)

    def half_beside(self, held):
        if not self.fast:
            return held
        return held + [permute(held[0], "core", swap_pairs(2, 1))]

    def offsets(self, rows):
        size = rows // 4
        there = (1 - self.here) * rows
        return [self.here * rows], [there + (self.spot ^ flip) * size for flip in (0, 2, 1, 3)]

    def one_weight(self, shard, held):
        if not self.fast:
            return jnp.zeros((1,), jnp.int32), held
        mine, others = self.offsets(shard.shape[0])
        return jnp.stack(mine + others).astype(jnp.int32), [shard] + held

    def middle_weights(self, out_shard, up_shard, down_shard, shared, down):
        if not self.fast:
            width = shared[0].shape[0]
            return (jnp.zeros((3,), jnp.int32), shared[0][:, :width], shared[0][:, width:], [], down)
        mine, others = self.offsets(out_shard.shape[0])
        rows = down_shard.shape[0]
        core = lax.axis_index("core")
        there = (1 - self.here) * rows
        rest = [self.here * rows, there + core * (rows // 2), there + (1 - core) * (rows // 2)]
        offsets = jnp.stack(mine + mine + others + rest).astype(jnp.int32)
        return offsets, out_shard, up_shard, shared, [down_shard] + down

    def with_vectors(self, quarter, shards):
        if not self.fast:
            return quarter
        return jnp.concatenate([quarter, jnp.concatenate(shards).reshape(-1, quarter.shape[1])], axis=0)

    def without_vectors(self, held, shards):
        if not self.fast:
            return held, [lax.all_gather(shard, "fsdp", axis=0, tiled=True) for shard in shards]
        moved = held[0]
        rows = sum(shard.shape[0] for shard in shards) // moved.shape[1]
        far = moved[moved.shape[0] - rows :].reshape(-1)
        full, at = [], 0
        for shard in shards:
            size = shard.shape[0]
            full.append(ordered(self.here == 0, shard, far[at : at + size]))
            at += size
        return [moved[: moved.shape[0] - rows]], full


def halved(part):
    return part.reshape(2, part.shape[0] // 2, part.shape[1])


def low_sum(parts):
    if len(parts) == 1:
        return parts[0]
    return sum(part.astype(f32) for part in parts).astype(bf16)


def add_low(left, right):
    return low_sum([left, right])


class Chain:
    def __init__(self, fast, *parts):
        self.fast = fast
        self.name = None
        self.pair = list(parts)
        self.path, self.depth = [], []

    def views(self):
        found = []
        for part, depth in zip(self.pair, self.depth):
            for name, index in self.path[depth:]:
                part = pick(halved(part) if name == "z1" else part, index)
            found.append(part)
        return found

    def restart(self, *pair):
        self.pair, self.path, self.depth = list(pair), [], [0] * len(pair)

    def settle(self):
        name, pair = self.name, self.pair
        if name == "z3":
            return ordered(lax.axis_index("seq") % 2 == 0, *pair)
        if name == "spread_x":
            return both_ways(lax.axis_index("x") == 0, *pair)
        if name == "spread_core":
            return both_ways(lax.axis_index("core") == 0, *pair)
        return low_sum(self.views())

    def go(self, name):
        if not self.fast:
            return
        if name == "core":
            keep = [part[0] for part in self.pair]
            send = low_sum([part[1] for part in self.pair])
            moved = permute(send, "core", swap_pairs(2, 1))
            self.name = name
            self.restart(*[one.reshape(2, 2, one.shape[1] // 2, one.shape[2]) for one in keep + [moved]])
            return
        if name in ("z2", "z3", "spread_x", "spread_core"):
            held = self.settle()
            axis = {"z2": "seq", "z3": "seq", "spread_x": "x", "spread_core": "core"}[name]
            pairs = {"z2": swap_pairs(4, 2), "z3": swap_pairs(4, 1)}.get(name, swap_pairs(2, 1))
            self.name = name
            self.restart(held, permute(held, axis, pairs))
            return
        axis = {"y": "fsdp", "x": "x", "z1": "seq"}[name]
        here = lax.axis_index(axis)
        parts = self.views()
        if name == "z1":
            here = here % 2
            parts = [halved(part) for part in parts]
        send = low_sum([pick(part, 1 - here) for part in parts])
        moved = permute(send, axis, swap_pairs(4 if axis == "seq" else 2, 1))
        self.path.append((name, here))
        self.pair.append(moved)
        self.depth.append(len(self.path))
        self.name = name

    def final(self):
        if not self.fast:
            keep, send = (sum(part[at].astype(f32) for part in self.pair) for at in (0, 1))
            parts = jnp.stack([keep, send], axis=1).astype(bf16)
            share = lax.psum_scatter(
                parts.reshape(-1, parts.shape[3]), "fsdp", scatter_dimension=0, tiled=True
            )
            return lax.psum(share, ("replica", "seq")).astype(f32)
        full = self.settle()
        return full.reshape(-1, full.shape[-1]).astype(f32)


def both_ways(first_here, mine, other):
    return jnp.stack([jnp.where(first_here, mine, other), jnp.where(first_here, other, mine)])


def settle_all(chains, *values):
    pairs, *values = sync([chain.pair for chain in chains], *values)
    for chain, pair in zip(chains, pairs):
        chain.pair = pair
    return values


def body(
    fast,
    tokens,
    segment_ids,
    joined_weight,
    query_bias,
    value_bias,
    out_weight,
    out_bias,
    norm_gain,
    norm_shift,
    up_weight,
    up_bias,
    down_weight,
    down_bias,
    final_gain,
    final_shift,
    cotangent,
):
    micro, block, width = tokens.shape[1:]
    length = segment_ids.shape[-1]
    size = lax.axis_size("seq")
    place = lax.axis_index("seq")
    hops = (length // 2 - 2) // block + 1
    assert size % 2 == 0 and hops in (1, 2)
    count = 2 * hops + 1
    inner_width = up_weight.shape[1]
    all_pairs = width // PAIR
    half_pairs = all_pairs // 2
    spans = [(0, half_pairs), (half_pairs, half_pairs)]
    fetch = Fetch(fast)

    def masks_of(ids):
        ends = ((0, 0), (hops * block, 0)), ((0, 0), (0, hops * block + TK_FWD - ALIGN))
        padded = jnp.pad(jnp.pad(ids, ends[0], constant_values=-1), ends[1], constant_values=1000)
        near = lax.dynamic_slice_in_dim(padded, place * block, count * block + TK_FWD - ALIGN, 1)
        rows = near[:, hops * block : (hops + 1) * block]
        low = jnp.sum(near < rows[:, :1], axis=1)
        high = jnp.sum(near <= rows[:, -1:], axis=1)
        bounds = jnp.stack([low, high, jnp.broadcast_to(1 - 2 * (place % 2), low.shape)], axis=1)
        segq = jnp.broadcast_to(rows[:, None, :], (micro, 8, block))
        segk = jnp.broadcast_to(near[:, :, None], near.shape + (128,))
        return bounds.astype(jnp.int32).reshape(-1), segq, segk

    def mask_at(batch):
        return (batch,) + tuple(masks)

    own = [tokens[0, batch] for batch in range(micro)]
    moves = [None] * micro
    small_shards = [
        query_bias,
        value_bias,
        out_bias,
        norm_gain,
        norm_shift,
        down_bias,
        final_gain,
        final_shift,
        up_bias,
    ]
    def hop_out(batch, step):
        if step == 0:
            one, two = own[batch], own[batch]
            moves[batch] = [one, permute(one, "seq", even_pairs(size)), permute(two, "seq", odd_pairs(size))]
        else:
            _, even, odd = moves[batch]
            moves[batch] = moves[batch] + [
                permute(even, "seq", odd_pairs(size)),
                permute(odd, "seq", even_pairs(size)),
            ]

    joined = fetch.far(fetch.with_vectors(fetch.quarter(joined_weight), small_shards))
    hop_out(0, 0)
    quarters = [
        jnp.concatenate([fetch.quarter(out_weight), fetch.quarter(up_weight)], axis=1),
        fetch.half(down_weight),
    ]
    shared = fetch.far(quarters[0])
    joined, moves[0], ids, quarters[1] = sync(joined, moves[0], segment_ids, quarters[1])
    joined, vectors = fetch.without_vectors(joined, small_shards)
    joined = fetch.across(joined)
    for step in range(1, hops):
        hop_out(0, step)
    joined, ids, vectors = sync(joined, ids, vectors)
    joined = fetch.beside(joined)
    masks = masks_of(ids[0])
    biases = jnp.pad(jnp.stack(vectors[:2]).astype(f32), ((0, 6), (0, 0)))
    rows_six = jnp.pad(jnp.stack(vectors[2:8]).astype(f32), ((0, 2), (0, 0)))
    up_row = jnp.pad(vectors[8].astype(f32)[None, :], ((0, 7), (0, 0)))
    shared, quarters[1] = sync(shared, quarters[1])
    shared = fetch.across(shared)
    down = fetch.far(quarters[1])
    moves[0], joined, own[1:], biases, rows_six, up_row, masks = sync(
        moves[0], joined, own[1:], biases, rows_six, up_row, masks
    )

    attended = [[] for _ in range(micro)]

    def window(batch):
        one, even, odd, *far = moves[batch]
        return [far[0], odd, one, even, far[1]] if far else [odd, one, even]

    windows = [window(0)] + [None] * (micro - 1)
    weight = fetch.one_weight(joined_weight, joined)

    if micro > 1:
        hop_out(1, 0)
    attended[0].append(tuple(attend_forward((0, all_pairs), mask_at(0), windows[0], weight, biases)))
    attended[0], shared, down, masks, windows[0], moves[1:2] = sync(
        attended[0], shared, down, masks, windows[0], moves[1:2]
    )
    shared = fetch.beside(shared)
    down = fetch.half_beside(down)
    attended[0], shared, down, own = sync(attended[0], shared, down, own)
    for step in range(1, hops if micro > 1 else 0):
        hop_out(1, step)
    middle_weights = fetch.middle_weights(out_weight, up_weight, down_weight, shared, down)

    middles = []
    for batch in range(micro):
        later = batch + 1
        if batch > 0:
            windows[batch] = window(batch)
            for step in range(1, hops if 1 < later < micro else 0):
                hop_out(later, step)
            attended[batch].append(
                tuple(attend_forward((0, all_pairs), mask_at(batch), windows[batch], weight, biases))
            )
            if later < micro:
                attended[batch], moves[later] = sync(attended[batch], moves[later])
        if later + 1 < micro:
            hop_out(later + 1, 0)
        middles.append(
            middle(
                [one[0] for one in attended[batch]],
                own[batch],
                cotangent[0, batch],
                middle_weights,
                rows_six,
                up_row,
            )
        )
        if later + 1 < micro:
            middles[-1], masks, moves[later : later + 2] = sync(middles[-1], masks, moves[later : later + 2])
        else:
            middles[-1], masks = sync(middles[-1], masks)

    core = lax.axis_index("core") if fast else jnp.zeros((), jnp.int32)
    core = core.astype(jnp.int32).reshape(1)
    outs = list(zip(*middles))
    small = sum(outs[8])
    grad_upb = sum(outs[9])
    half = width // 2
    gap = inner_width // 2 - half
    spread = jnp.pad(small[:6].reshape(6, 2, half), ((0, 0), (0, 0), (0, gap))).reshape(6, inner_width)
    side = jnp.concatenate([grad_upb[:1], spread, jnp.zeros((1, inner_width), f32)], axis=0)
    down = Chain(fast, weight_grad_down(core, outs[6], outs[7], side))
    up_ins = (outs[4], outs[5], [[part[0] for part in one] for one in attended], outs[3])
    (up_ins,) = settle_all([down], up_ins)
    down.go("core")
    up = Chain(fast, weight_grad_up(core, *up_ins))
    (masks,) = settle_all([down, up], list(masks))

    backs = [None] * micro
    coming = [None] * micro
    joined_sums = [[], []]
    last = micro - 1

    def run_back(which, batch, chains, moving=()):
        before = [outs[1][batch]] if which == 0 else backs[batch]
        *parts, keep, send = attend_backward(
            core, spans[which], mask_at(batch), windows[batch], weight, biases, attended[batch], outs[2][batch], before
        )
        moved = [coming[at] for at in moving]
        backs[batch], grad_joined, masks[:], moved = settle_all(chains, parts, (keep, send), list(masks), moved)
        for at, one in zip(moving, moved):
            coming[at] = one
        joined_sums[which].append(grad_joined)

    def total_of(which):
        return Chain(fast, *joined_sums[which])

    def hop_back(batch, step):
        parts = backs[batch]
        if step == 0 and hops > 1:
            coming[batch] = [
                permute(parts[hops + 2], "seq", even_pairs(size)),
                permute(parts[hops - 2], "seq", odd_pairs(size)),
            ]
            return
        odd, even = parts[hops - 1], parts[hops + 1]
        if hops > 1:
            odd, even = add_low(odd, coming[batch][0]), add_low(even, coming[batch][1])
        coming[batch] = [permute(odd, "seq", odd_pairs(size)), permute(even, "seq", even_pairs(size))]

    down.go("y")
    up.go("core")
    run_back(0, 0, [up, down])
    down.go("x")
    up.go("y")
    run_back(1, 0, [down])
    middle_steps = [
        ([(down, "z1")], [down, up]),
        ([(down, "z2"), (up, "x")], [down, up]),
        ([(down, "z3"), (up, "z1")], [down, up]),
        ([(down, "spread_x"), (up, "z2")], [down, up]),
    ]
    for batch in range(1, micro):
        for which in (0, 1):
            begin, end = middle_steps.pop(0) if middle_steps else ([], [])
            for chain, name in begin:
                chain.go(name)
            moving = []
            if which == 0:
                hop_back(batch - 1, 0)
                moving = [batch - 1]
            else:
                for step in range(1, hops):
                    hop_back(batch - 1, step)
                moving = [batch - 1]
            if batch == last and which == 1:
                joined_one = total_of(0)
                joined_one.go("core")
                end = end + [joined_one]
            run_back(which, batch, end, moving)

    joined_two = total_of(1)
    joined_two.go("core")
    joined_one.go("y")
    hop_back(last, 0)
    (backs,) = settle_all([joined_two], backs)
    joined_two.go("y")
    up.go("z3")
    down.go("spread_core")
    coming, backs = settle_all([joined_one, down], coming, backs)
    joined_one.go("x")
    for step in range(1, hops):
        hop_back(last, step)
    settle_all([joined_two, joined_one, up])
    joined_two.go("x")
    joined_one.go("z1")
    up.go("spread_x")
    (coming,) = settle_all([joined_two, joined_one], coming)
    joined_two.go("z1")
    joined_one.go("z2")
    settle_all([joined_two, joined_one, up])
    joined_two.go("z2")
    joined_one.go("z3")
    up.go("spread_core")
    settle_all([joined_two, joined_one])
    joined_two.go("z3")
    joined_one.go("spread_x")
    settle_all([joined_two, joined_one])
    joined_two.go("spread_x")
    joined_one.go("spread_core")
    settle_all([joined_two])
    joined_two.go("spread_core")

    final_down = down.final()
    final_up = up.final()
    final_up, final_out = final_up[:, :inner_width], final_up[:, inner_width:]
    final_a, final_b = joined_one.final(), joined_two.final()
    grad_tokens = []
    for batch in range(micro):
        total = backs[batch][hops] + sum(one.astype(f32) for one in coming[batch])
        grad_tokens.append(total.astype(bf16))
    low, high = spans[0][1] * PAIR, spans[1][1] * PAIR
    final_joined = jnp.concatenate(
        [
            part
            for at in range(3)
            for part in (final_a[:, at * low : (at + 1) * low], final_b[:, at * high : (at + 1) * high])
        ],
        axis=1,
    )
    bias_sums = final_a[:, 3 * low : 3 * low + 2] + final_b[:, 3 * high : 3 * high + 2]
    if fast:
        own_rows = width // lax.axis_size("fsdp")
        smalls = [final_down[:own_rows, width + 1 + at] for at in range(6)]
    else:
        smalls = [
            lax.psum_scatter(lax.psum(small[at], ("replica", "seq")), "fsdp", scatter_dimension=0, tiled=True)
            for at in range(6)
        ]
    return (
        jnp.stack(outs[0], axis=0)[None],
        jnp.stack(grad_tokens, axis=0)[None],
        final_joined,
        bias_sums[:, 0],
        bias_sums[:, 1],
        final_out,
        smalls[0],
        smalls[1],
        smalls[2],
        final_up,
        final_down[:, width],
        final_down[:, :width],
        smalls[3],
        smalls[4],
        smalls[5],
    )


def solution(mesh):
    fast = two_level(dict(mesh.shape))
    groups = ("replica", "fsdp")
    if fast:
        mesh = jax.sharding.Mesh(mesh.devices.reshape(2, 2, 2, 4), ("x", "core", "fsdp", "seq"))
        groups = ("x", "core", "fsdp")
    rows = P(groups, None, "seq", None)
    matrix, vector = P("fsdp", None), P("fsdp")
    in_specs = (
        rows,
        P(groups, None, None),
        matrix,
        vector,
        vector,
        matrix,
        vector,
        vector,
        vector,
        matrix,
        vector,
        matrix,
        vector,
        vector,
        vector,
        rows,
    )
    out_specs = (
        rows,
        rows,
        matrix,
        vector,
        vector,
        matrix,
        vector,
        vector,
        vector,
        matrix,
        vector,
        matrix,
        vector,
        vector,
        vector,
    )
    return jax.shard_map(
        functools.partial(body, fast),
        mesh=mesh,
        in_specs=in_specs,
        out_specs=out_specs,
        check_vma=False,
    )
```

```python
import functools
import jax
import jax.numpy as jnp
from jax import lax
from jax.experimental import pallas as pl
from jax.experimental.pallas import tpu as pltpu
from jax.sharding import PartitionSpec as P

HEADS = 12
HEAD_DIM = 64
PAIR = 2 * HEAD_DIM
epsilon = 1e-05
masked_score = -1e30
scale = HEAD_DIM ** (-0.5)
TK_FWD = 256
TK_BWD = 256
ALIGN = 128
ROW_STEP = 16
VMEM_LIMIT = 62 * 1024 * 1024
FF_TILES = 4
f32 = jnp.float32
bf16 = jnp.bfloat16


def nt(left, right):
    return lax.dot_general(left, right, (((1,), (1,)), ((), ())), preferred_element_type=f32)


def tn(left, right):
    return lax.dot_general(left, right, (((0,), (0,)), ((), ())), preferred_element_type=f32)


def nn(left, right):
    return lax.dot_general(left, right, (((1,), (0,)), ((), ())), preferred_element_type=f32)


def stack_heads(pair):
    lane = lax.broadcasted_iota(jnp.int32, pair.shape, 1)
    zero = jnp.zeros_like(pair)
    return jnp.concatenate(
        [jnp.where(lane < HEAD_DIM, pair, zero), jnp.where(lane < HEAD_DIM, zero, pair)], axis=0
    )


def unstack_heads(rows):
    half = rows.shape[0] // 2
    lane = lax.broadcasted_iota(jnp.int32, (half, rows.shape[1]), 1)
    return jnp.where(lane < HEAD_DIM, rows[:half], rows[half:])


def split_pieces(refs):
    pieces = []
    for ref in refs:
        if len(ref.shape) == 2:
            pieces.append(ref)
        else:
            pieces.extend(ref.at[at] for at in range(ref.shape[0]))
    return pieces


def count_pieces(arrays):
    return sum(1 if len(one.shape) == 2 else one.shape[0] for one in arrays)


def start_columns(offsets, piece_refs, full_s, sems, width, at_col, size_col):
    copies = []
    for at, piece in enumerate(split_pieces(piece_refs)):
        size = piece.shape[0]
        row = pl.multiple_of(offsets[at], ROW_STEP)
        for part in range(3):
            copy = pltpu.make_async_copy(
                piece.at[:, pl.ds(part * width + at_col, size_col)],
                full_s.at[pl.ds(row, size), pl.ds(part * size_col, size_col)],
                sems.at[at, part],
            )
            copy.start()
            copies.append(copy)
    return copies


def wait_all(copies):
    for copy in copies:
        copy.wait()


def first_row(bounds, at, count, block):
    middle = count // 2
    return pl.multiple_of((middle + bounds[2] * (at - middle)) * block, ALIGN)


def reached(bounds, at, count, block):
    row = first_row(bounds, at, count, block)
    return (bounds[1] > row) & (bounds[0] < row + block)


def block_copy(bounds, x_refs, x_s, sems, at):
    block = x_refs[at].shape[0]
    row = first_row(bounds, at, len(x_refs), block)
    return pltpu.make_async_copy(x_refs[at], x_s.at[pl.ds(row, block), :], sems.at[at])


def fetch_window(bounds, x_refs, x_s, sems):
    for at in range(len(x_refs)):

        @pl.when(reached(bounds, at, len(x_refs), x_refs[at].shape[0]))
        def _():
            block_copy(bounds, x_refs, x_s, sems, at).start()


def project_window(bounds, x_refs, x_s, sems, w_ref, bias_ref, cols, k_s, v_s, tail):
    block = x_refs[0].shape[0]
    width = k_s.shape[1]
    for at in range(len(x_refs)):
        rows = pl.ds(first_row(bounds, at, len(x_refs), block), block)
        active = reached(bounds, at, len(x_refs), block)

        @pl.when(active)
        def _():
            block_copy(bounds, x_refs, x_s, sems, at).wait()
            x = x_s[rows, :]
            both = nn(x, w_ref[:, width:])
            k_s[rows, :] = both[:, :width].astype(bf16)
            v_s[rows, :] = (both[:, width:] + bias_ref[1:2, cols]).astype(bf16)

        @pl.when(jnp.logical_not(active))
        def _():
            k_s[rows, :] = jnp.zeros((block, width), bf16)
            v_s[rows, :] = jnp.zeros((block, width), bf16)

    end = len(x_refs) * block
    k_s[end:, :] = jnp.zeros((tail, width), bf16)
    v_s[end:, :] = jnp.zeros((tail, width), bf16)


def tile_range(bounds, tk):
    low = bounds[0]
    high = bounds[1]
    start = (low // ALIGN) * ALIGN
    return start, (high - start + tk - 1) // tk


def project_queries(x, w_ref, bias_ref, cols, q_s, qq_s):
    width = q_s.shape[1]
    q = nn(x, w_ref[:, :width]) + bias_ref[0:1, cols]
    q_s[...] = q.astype(bf16) * jnp.asarray(scale, bf16)
    for pair in range(width // PAIR):
        here = slice(pair * PAIR, (pair + 1) * PAIR)
        qq_s[:, here] = stack_heads(q_s[:, here])


def forward_kernel(batch, hops, pieces, first, all_bounds, offsets, *refs):
    bounds = [all_bounds[3 * batch + at] for at in range(3)]
    count = 2 * hops + 1
    x_refs = refs[:count]
    w_refs, refs = refs[count : count + pieces], refs[count + pieces :]
    bias_ref, segq_ref, segk_any, o_ref, lse_ref = refs[:5]
    segk_ref, seg_sem, x_s, w_ref, q_s, qq_s, k_s, v_s, top_s, sum_s, acc_s, x_sems, sems = refs[5:]
    seg_copy = pltpu.make_async_copy(segk_any.at[batch], segk_ref, seg_sem)
    seg_copy.start()
    block, full_width = x_refs[0].shape
    width = o_ref.shape[1]
    own_rows = slice(hops * block, (hops + 1) * block)
    tk = TK_FWD
    pairs = width // PAIR
    cols_all = slice(first * PAIR, first * PAIR + width)
    copies = start_columns(offsets, w_refs, w_ref, sems, full_width, first * PAIR, width)
    fetch_window(bounds, x_refs, x_s, x_sems)
    wait_all(copies)
    project_window(bounds, x_refs, x_s, x_sems, w_ref, bias_ref, cols_all, k_s, v_s, tk - ALIGN)
    project_queries(x_s[own_rows, :], w_ref, bias_ref, cols_all, q_s, qq_s)
    start, steps = tile_range(bounds, tk)
    seg_copy.wait()
    segq = segq_ref[batch, 0:1, :]
    segq = jnp.concatenate([segq, segq], axis=1)
    top_s[...] = jnp.full(top_s.shape, masked_score, f32)
    sum_s[...] = jnp.ones(sum_s.shape, f32)
    sum_s[:pairs, :] = jnp.zeros((pairs, sum_s.shape[1]), f32)
    acc_s[...] = jnp.zeros(acc_s.shape, f32)

    @pl.loop(0, steps)
    def _(at):
        here = pl.ds(pl.multiple_of(start + at * tk, ALIGN), tk)
        allowed = segk_ref[here, 0:1] == segq
        for pair in range(pairs):
            cols = slice(pair * PAIR, (pair + 1) * PAIR)
            one = slice(pair, pair + 1)
            scores = nt(k_s[here, cols], qq_s[:, cols])
            scores = jnp.where(allowed, scores, masked_score)
            top = top_s[one, :]
            new_top = jnp.maximum(top, jnp.max(scores, axis=0, keepdims=True))
            fade = jnp.exp(top - new_top)
            weights = jnp.exp(scores - new_top)
            top_s[one, :] = new_top
            sum_s[one, :] = sum_s[one, :] * fade + jnp.sum(weights, axis=0, keepdims=True)
            acc_s[pair] = acc_s[pair] * fade + tn(v_s[here, cols], weights.astype(bf16))

    lse_ref[...] = top_s[...] + jnp.log(sum_s[...])
    for pair in range(pairs):
        cols = slice(pair * PAIR, (pair + 1) * PAIR)
        mixed = acc_s[pair] / sum_s[pair : pair + 1, :]
        o_ref[:, cols] = unstack_heads(mixed.T).astype(bf16)


def backward_kernel(batch, hops, pieces, prev, first, skip, groups, all_bounds, offsets, core_ref, *refs):
    bounds = [all_bounds[3 * batch + at] for at in range(3)]
    count = 2 * hops + 1
    x_refs = refs[:count]
    w_refs, refs = refs[count : count + pieces], refs[count + pieces :]
    bias_ref, segq_ref, segk_any, o_ref, lse_ref, do_ref = refs[:6]
    prev_refs, refs = refs[6 : 6 + prev], refs[6 + prev :]
    out_refs, refs = refs[:count], refs[count:]
    halves, refs = refs[: 2 * groups], refs[2 * groups :]
    segk_ref, seg_sem, *refs = refs
    seg_copy = pltpu.make_async_copy(segk_any.at[batch], segk_ref, seg_sem)
    seg_copy.start()
    x_s, p_s, own_s, w_ref, q_s, qq_s, gg_s, k_s, v_s, dk_s, dv_s, dw_s, stat_s, acc_s, db_s = refs[:15]
    x_sems, p_sems, o_sems, sems = refs[15:]
    block, full_width = x_refs[0].shape
    width = q_s.shape[1]
    tk = TK_BWD
    pairs = width // PAIR
    cols_all = slice(first * PAIR, first * PAIR + width)
    own_rows = slice(hops * block, (hops + 1) * block)
    others = [at for at in range(count) if at != hops]
    copies = start_columns(offsets, w_refs, w_ref, sems, full_width, first * PAIR, width)
    fetch_window(bounds, x_refs, x_s, x_sems)
    own_copy = pltpu.make_async_copy(prev_refs[hops if prev > 1 else 0], own_s, p_sems.at[hops])
    own_copy.start()

    def stage(at):
        return p_s.at[pl.ds(at * block, block), :]

    def prev_copy(at):
        return pltpu.make_async_copy(prev_refs[at], stage(at), p_sems.at[at])

    def out_copy(at):
        return pltpu.make_async_copy(own_s if at == hops else stage(at), out_refs[at], o_sems.at[at])

    for at in others:
        active = reached(bounds, at, count, block)
        if prev > 1:

            @pl.when(active)
            def _():
                prev_copy(at).start()

        else:

            @pl.when(jnp.logical_not(active))
            def _():
                p_s[at * block : (at + 1) * block, :] = jnp.zeros((block, full_width), bf16)
                out_copy(at).start()

    dk_s[...] = jnp.zeros(dk_s.shape, f32)
    dv_s[...] = jnp.zeros(dv_s.shape, f32)
    acc_s[...] = jnp.zeros(acc_s.shape, f32)
    for pair in range(pairs):
        cols = slice(pair * PAIR, (pair + 1) * PAIR)
        far = slice((first + pair) * PAIR, (first + pair + 1) * PAIR)
        theirs = slice((skip + pair) * PAIR, (skip + pair + 1) * PAIR)
        grads = stack_heads(do_ref[:, far])
        gg_s[:, cols] = grads
        mixed = o_ref[:, theirs].astype(f32)
        product = grads.astype(f32) * jnp.concatenate([mixed, mixed], axis=0)
        stat_s[pair : pair + 1, :] = jnp.sum(product.T, axis=0, keepdims=True)
    wait_all(copies)
    project_window(bounds, x_refs, x_s, x_sems, w_ref, bias_ref, cols_all, k_s, v_s, tk - ALIGN)
    project_queries(x_s[own_rows, :], w_ref, bias_ref, cols_all, q_s, qq_s)
    start, steps = tile_range(bounds, tk)
    seg_copy.wait()
    segq = segq_ref[batch, 0:1, :]
    segq = jnp.concatenate([segq, segq], axis=1)

    @pl.loop(0, steps)
    def _(at):
        here = pl.ds(pl.multiple_of(start + at * tk, ALIGN), tk)
        allowed = segk_ref[here, 0:1] == segq
        for pair in range(pairs):
            cols = slice(pair * PAIR, (pair + 1) * PAIR)
            keys = k_s[here, cols]
            queries = qq_s[:, cols]
            grads = gg_s[:, cols]
            scores = nt(keys, queries)
            scores = jnp.where(allowed, scores, masked_score)
            weights = jnp.exp(scores - lse_ref[skip + pair : skip + pair + 1, :])
            grad_weights = nt(v_s[here, cols], grads)
            grad_scores = (weights * (grad_weights - stat_s[pair : pair + 1, :])).astype(bf16)
            dv_s[here, cols] += nn(weights.astype(bf16), grads)
            dk_s[here, cols] += nn(grad_scores, queries)
            acc_s[pair] += tn(keys, grad_scores)

    for pair in range(pairs):
        cols = slice(pair * PAIR, (pair + 1) * PAIR)
        q_s[:, cols] = (unstack_heads(acc_s[pair].T) * scale).astype(bf16)
    dq = q_s[...]
    db_s[...] = jnp.zeros(db_s.shape, f32)
    db_s[0:1, cols_all] = jnp.sum(dq.astype(f32), axis=0, keepdims=True)

    def rows_of(at):
        rows = pl.ds(first_row(bounds, at, count, block), block)
        dk = dk_s[rows, :].astype(bf16)
        dv = dv_s[rows, :].astype(bf16)
        db_s[1:2, cols_all] += jnp.sum(dv.astype(f32), axis=0, keepdims=True)
        return [dk, dv]

    grads = jnp.concatenate([dq] + rows_of(hops), axis=1)
    own_copy.wait()
    own_s[...] += nt(grads, w_ref[...])
    out_copy(hops).start()
    dw_s[...] = tn(x_s[own_rows, :], grads)
    for at in others:

        @pl.when(reached(bounds, at, count, block))
        def _():
            rows = slice(at * block, (at + 1) * block)
            grads = jnp.concatenate(rows_of(at), axis=1)
            back = nt(grads, w_ref[:, width:])
            if prev > 1:
                prev_copy(at).wait()
                back = back + p_s[rows, :].astype(f32)
            p_s[rows, :] = back.astype(bf16)
            out_copy(at).start()
            x = x_s[pl.ds(first_row(bounds, at, count, block), block), :]
            dw_s[:, width:] += tn(x, grads)

    side = jnp.concatenate([db_s[...], jnp.zeros((120, full_width), f32)], axis=0).T.astype(bf16)
    size = width // groups
    for group in range(groups):
        keep_ref, send_ref = halves[2 * group], halves[2 * group + 1]
        for part in range(3):
            at_col = part * width + group * size
            put_halves(
                core_ref[0],
                keep_ref,
                send_ref,
                slice(part * size, (part + 1) * size),
                dw_s[:, at_col : at_col + size].astype(bf16),
            )
        put_halves(
            core_ref[0],
            keep_ref,
            send_ref,
            slice(3 * size, 3 * size + 128),
            side if group == 0 else jnp.zeros_like(side),
        )
    out_copy(hops).wait()
    for at in others:
        if prev > 1:

            @pl.when(reached(bounds, at, count, block))
            def _():
                out_copy(at).wait()

        else:
            out_copy(at).wait()


def whole():
    return pl.BlockSpec(memory_space=pltpu.VMEM)


def smem():
    return pl.BlockSpec(memory_space=pltpu.SMEM)


def raw():
    return pl.BlockSpec(memory_space=pl.ANY)


def attend_forward(span, mask, window, weight, biases):
    batch, bounds, segq, segk = mask
    offsets, pieces = weight
    first, pairs = span
    count = len(window)
    block, full_width = window[0].shape
    width = pairs * PAIR
    padded = count * block + TK_FWD - ALIGN
    return pl.pallas_call(
        functools.partial(forward_kernel, batch, count // 2, len(pieces), first),
        out_shape=(
            jax.ShapeDtypeStruct((block, width), bf16),
            jax.ShapeDtypeStruct((8, 2 * block), f32),
        ),
        in_specs=[smem()] * 2
        + [raw()] * (count + len(pieces))
        + [whole(), whole(), raw()],
        out_specs=(whole(), whole()),
        scratch_shapes=[
            pltpu.VMEM(segk.shape[1:], jnp.int32),
            pltpu.SemaphoreType.DMA,
            pltpu.VMEM((count * block, full_width), bf16),
            pltpu.VMEM((full_width, 3 * width), bf16),
            pltpu.VMEM((block, width), bf16),
            pltpu.VMEM((2 * block, width), bf16),
            pltpu.VMEM((padded, width), bf16),
            pltpu.VMEM((padded, width), bf16),
            pltpu.VMEM((8, 2 * block), f32),
            pltpu.VMEM((8, 2 * block), f32),
            pltpu.VMEM((pairs, PAIR, 2 * block), f32),
            pltpu.SemaphoreType.DMA((count,)),
            pltpu.SemaphoreType.DMA((count_pieces(pieces), 3)),
        ],
        compiler_params=pltpu.CompilerParams(vmem_limit_bytes=VMEM_LIMIT),
        cost_estimate=pl.CostEstimate(
            flops=2_500_000_000 * pairs, bytes_accessed=8_000_000, transcendentals=4_000_000
        ),
        name="attend_forward",
    )(bounds, offsets, *window, *pieces, biases, segq, segk)


def attend_backward(core, span, groups, mask, window, weight, biases, attended, grad, before):
    batch, bounds, segq, segk = mask
    offsets, pieces = weight
    first, pairs = span
    count = len(window)
    block, full_width = window[0].shape
    width = pairs * PAIR
    hops = count // 2
    padded = count * block + TK_BWD - ALIGN
    per_part = full_width // PAIR // len(attended)
    mixed, lse = attended[first // per_part]
    at = first // per_part * per_part
    outs = [
        jax.ShapeDtypeStruct((block, full_width), f32 if at == hops else bf16) for at in range(count)
    ]
    return pl.pallas_call(
        functools.partial(
            backward_kernel, batch, hops, len(pieces), len(before), first, first - at, groups
        ),
        out_shape=(
            *outs,
            *[jax.ShapeDtypeStruct((2, full_width // 4, 3 * width // groups + 128), bf16)] * (2 * groups),
        ),
        in_specs=[smem()] * 3
        + [raw()] * (count + len(pieces))
        + [whole(), whole(), raw()]
        + [whole()] * 3
        + [raw()] * len(before),
        out_specs=(raw(),) * count + (whole(),) * (2 * groups),
        input_output_aliases=(
            {9 + count + len(pieces) + at: at for at in range(count)} if len(before) > 1 else {}
        ),
        scratch_shapes=[
            pltpu.VMEM(segk.shape[1:], jnp.int32),
            pltpu.SemaphoreType.DMA,
            pltpu.VMEM((count * block, full_width), bf16),
            pltpu.VMEM((count * block, full_width), bf16),
            pltpu.VMEM((block, full_width), f32),
            pltpu.VMEM((full_width, 3 * width), bf16),
            pltpu.VMEM((block, width), bf16),
            pltpu.VMEM((2 * block, width), bf16),
            pltpu.VMEM((2 * block, width), bf16),
            pltpu.VMEM((padded, width), bf16),
            pltpu.VMEM((padded, width), bf16),
            pltpu.VMEM((padded, width), f32),
            pltpu.VMEM((padded, width), f32),
            pltpu.VMEM((full_width, 3 * width), f32),
            pltpu.VMEM((8, 2 * block), f32),
            pltpu.VMEM((pairs, PAIR, 2 * block), f32),
            pltpu.VMEM((8, full_width), f32),
            pltpu.SemaphoreType.DMA((count,)),
            pltpu.SemaphoreType.DMA((count,)),
            pltpu.SemaphoreType.DMA((count,)),
            pltpu.SemaphoreType.DMA((count_pieces(pieces), 3)),
        ],
        compiler_params=pltpu.CompilerParams(vmem_limit_bytes=VMEM_LIMIT),
        cost_estimate=pl.CostEstimate(
            flops=5_000_000_000 * pairs, bytes_accessed=20_000_000, transcendentals=4_000_000
        ),
        name="attend_backward",
    )(bounds, offsets, core, *window, *pieces, biases, segq, segk, mixed, lse, grad, *before)


def join(refs):
    if len(refs) == 1:
        return refs[0][...]
    return jnp.concatenate([ref[...] for ref in refs], axis=1)


def middle_kernel(
    counts, offsets, tokens_ref, cot_ref, vec_ref, upb_ref, *refs
):
    n_mixed, n_shared, n_down = counts
    mixed_refs, refs = refs[:n_mixed], refs[n_mixed:]
    out_own, up_own, refs = refs[0], refs[1], refs[2:]
    shared, down_p = split_pieces(refs[:n_shared]), split_pieces(refs[n_shared : n_shared + n_down])
    refs = refs[n_shared + n_down :]
    n_shared = len(shared)
    (
        result_ref, one_ref, mixed_ref, branch_ref, hidden_ref, inner_ref, act_ref, two_ref,
        small_ref, gupb_ref,
    ) = refs[:10]
    wo_s, up_s, down_s, slope_s, act_s, inner_s, leave_sems, sems = refs[10:]
    width = wo_s.shape[1]
    leaving = []
    out_copies, up_copies, down_copies = [], [], []

    def begin(copies, at, source, target):
        row = pl.multiple_of(offsets[at], ROW_STEP)
        copy = pltpu.make_async_copy(
            source, target.at[pl.ds(row, source.shape[0]), :], sems.at[at, len(copies) % 2]
        )
        copy.start()
        copies.append(copy)

    begin(out_copies, 0, out_own, wo_s)
    for at, piece in enumerate(shared):
        row = pl.multiple_of(offsets[2 + at], ROW_STEP)
        copy = pltpu.make_async_copy(
            piece.at[:, pl.ds(0, width)], wo_s.at[pl.ds(row, piece.shape[0]), :], sems.at[2 + at, 0]
        )
        copy.start()
        out_copies.append(copy)
    begin(up_copies, 1, up_own, up_s)
    for at, piece in enumerate(shared):
        row = pl.multiple_of(offsets[2 + at], ROW_STEP)
        copy = pltpu.make_async_copy(
            piece.at[:, pl.ds(width, up_s.shape[1])],
            up_s.at[pl.ds(row, piece.shape[0]), :],
            sems.at[2 + at, 1],
        )
        copy.start()
        up_copies.append(copy)
    for at, piece in enumerate(down_p):
        row = pl.multiple_of(offsets[2 + n_shared + at], ROW_STEP)
        copy = pltpu.make_async_copy(
            piece, down_s.at[pl.ds(row, piece.shape[0]), :], sems.at[2 + n_shared + at, 0]
        )
        copy.start()
        down_copies.append(copy)
    inner_width = up_s.shape[1]
    tile = inner_width // FF_TILES
    out_bias, norm_gain, norm_shift = vec_ref[0:1, :], vec_ref[1:2, :], vec_ref[2:3, :]
    down_bias, final_gain, final_shift = vec_ref[3:4, :], vec_ref[4:5, :], vec_ref[5:6, :]
    wait_all(out_copies)
    values = tokens_ref[...].astype(f32) + (nn(join(mixed_refs), wo_s[...]) + out_bias)
    centered = values - jnp.mean(values, axis=1, keepdims=True)
    inverse_one = lax.rsqrt(jnp.mean(centered * centered, axis=1, keepdims=True) + epsilon)
    normed_one = centered * inverse_one
    hidden = normed_one * norm_gain + norm_shift
    hidden_low = hidden.astype(bf16)
    hidden_ref[...] = hidden_low
    wait_all(up_copies)
    def up_tile(at):
        cols = slice(at * tile, (at + 1) * tile)
        return nn(hidden_low, up_s[:, cols]) + upb_ref[0:1, cols]

    branch_two = None
    inner = up_tile(0)
    wait_all(down_copies)
    for at in range(FF_TILES):
        cols = slice(at * tile, (at + 1) * tile)
        following = up_tile(at + 1) if at + 1 < FF_TILES else None
        normal = 0.5 * (1.0 + lax.erf(inner * 0.7071067811865476))
        density = jnp.exp(-0.5 * inner * inner) * 0.3989422804014327
        slope_s[:, cols] = normal + inner * density
        activated = (inner * normal).astype(bf16)
        act_s[:, cols] = activated
        leaving.append(pltpu.make_async_copy(act_s.at[:, cols], act_ref.at[:, cols], leave_sems.at[0, at]))
        leaving[-1].start()
        term = nn(activated, down_s[cols, :])
        branch_two = term if branch_two is None else branch_two + term
        inner = following
    values = hidden + (branch_two + down_bias)
    centered = values - jnp.mean(values, axis=1, keepdims=True)
    inverse_two = lax.rsqrt(jnp.mean(centered * centered, axis=1, keepdims=True) + epsilon)
    normed_two = centered * inverse_two
    result_ref[...] = (normed_two * final_gain + final_shift).astype(bf16)
    cot = cot_ref[...].astype(f32)
    small_ref[4:5, :] = jnp.sum(cot * normed_two, axis=0, keepdims=True)
    small_ref[5:6, :] = jnp.sum(cot, axis=0, keepdims=True)
    scaled = cot * final_gain
    first = jnp.mean(scaled, axis=1, keepdims=True)
    second = jnp.mean(scaled * normed_two, axis=1, keepdims=True)
    grad_two = inverse_two * (scaled - first - normed_two * second)
    grad_low = grad_two.astype(bf16)
    two_ref[...] = grad_low
    small_ref[3:4, :] = jnp.sum(grad_low.astype(f32), axis=0, keepdims=True)
    grad_hidden = grad_two
    gupb_ref[...] = jnp.zeros(gupb_ref.shape, f32)
    for at in range(FF_TILES):
        cols = slice(at * tile, (at + 1) * tile)
        grad_inner = (nt(grad_low, down_s[cols, :]) * slope_s[:, cols]).astype(bf16)
        inner_s[:, cols] = grad_inner
        leaving.append(pltpu.make_async_copy(inner_s.at[:, cols], inner_ref.at[:, cols], leave_sems.at[1, at]))
        leaving[-1].start()
        gupb_ref[0:1, cols] = jnp.sum(grad_inner.astype(f32), axis=0, keepdims=True)
        grad_hidden = grad_hidden + nt(grad_inner, up_s[:, cols])
    small_ref[1:2, :] = jnp.sum(grad_hidden * normed_one, axis=0, keepdims=True)
    small_ref[2:3, :] = jnp.sum(grad_hidden, axis=0, keepdims=True)
    scaled = grad_hidden * norm_gain
    first = jnp.mean(scaled, axis=1, keepdims=True)
    second = jnp.mean(scaled * normed_one, axis=1, keepdims=True)
    grad_one = inverse_one * (scaled - first - normed_one * second)
    one_ref[...] = grad_one
    grad_branch = grad_one.astype(bf16)
    branch_ref[...] = grad_branch
    small_ref[0:1, :] = jnp.sum(grad_branch.astype(f32), axis=0, keepdims=True)
    small_ref[6:8, :] = jnp.zeros((2, small_ref.shape[1]), f32)
    mixed_ref[...] = nt(grad_branch, wo_s[...]).astype(bf16)
    wait_all(leaving)


def middle(attended, tokens, cotangent, weights, vectors, up_bias):
    offsets, out_own, up_own, shared, down = weights
    counts = (len(attended), len(shared), len(down))
    pieces = [out_own, up_own, *shared, *down]
    block, width = tokens.shape
    inner_width = up_bias.shape[1]
    return pl.pallas_call(
        functools.partial(middle_kernel, counts),
        out_shape=(
            jax.ShapeDtypeStruct((block, width), bf16),
            jax.ShapeDtypeStruct((block, width), f32),
            jax.ShapeDtypeStruct((block, width), bf16),
            jax.ShapeDtypeStruct((block, width), bf16),
            jax.ShapeDtypeStruct((block, width), bf16),
            jax.ShapeDtypeStruct((block, inner_width), bf16),
            jax.ShapeDtypeStruct((block, inner_width), bf16),
            jax.ShapeDtypeStruct((block, width), bf16),
            jax.ShapeDtypeStruct((8, width), f32),
            jax.ShapeDtypeStruct((8, inner_width), f32),
        ),
        in_specs=[smem()] + [whole()] * (4 + len(attended)) + [raw()] * len(pieces),
        out_specs=(whole(),) * 5 + (raw(),) * 2 + (whole(),) * 3,
        scratch_shapes=[
            pltpu.VMEM((width, width), bf16),
            pltpu.VMEM((width, inner_width), bf16),
            pltpu.VMEM((inner_width, width), bf16),
            pltpu.VMEM((block, inner_width), f32),
            pltpu.VMEM((block, inner_width), bf16),
            pltpu.VMEM((block, inner_width), bf16),
            pltpu.SemaphoreType.DMA((2, FF_TILES)),
            pltpu.SemaphoreType.DMA((count_pieces(pieces), 2)),
        ],
        compiler_params=pltpu.CompilerParams(vmem_limit_bytes=VMEM_LIMIT),
        cost_estimate=pl.CostEstimate(flops=24_000_000_000, bytes_accessed=20_000_000, transcendentals=4_000_000),
        name="middle",
    )(offsets, tokens, cotangent, vectors, up_bias, *attended, *pieces)


def grad_down_kernel(micro, core_ref, *refs):
    act_refs, two_refs, side_ref = refs[:micro], refs[micro : 2 * micro], refs[-3]
    total = sum(tn(act[...], two[...]) for act, two in zip(act_refs, two_refs))
    rows, width = total.shape
    side = jnp.concatenate([side_ref[...], jnp.zeros((120, rows), f32)], axis=0).T

    def put(ref):
        ref[0, :, :width] = total.astype(bf16)
        ref[0, :, width:] = side.astype(bf16)

    @pl.when(pl.program_id(0) % 2 == 0)
    def _():
        put(refs[-1])

    @pl.when(pl.program_id(0) % 2 == 1)
    def _():
        put(refs[-2])


def put_halves(core, keep_ref, send_ref, cols, value):
    rows, width = value.shape
    halves = value.reshape(2, 2, rows // 4, width)

    @pl.when(core == 0)
    def _():
        keep_ref[:, :, cols] = halves[:, 0]
        send_ref[:, :, cols] = halves[:, 1]

    @pl.when(core == 1)
    def _():
        keep_ref[:, :, cols] = halves[:, 1]
        send_ref[:, :, cols] = halves[:, 0]


def weight_grad_down(core, activated, grad_low, side):
    micro = len(activated)
    block, inner_width = activated[0].shape
    width = grad_low[0].shape[1]
    tile = inner_width // 4

    def spot(at, core_ref):
        core = core_ref[0]
        return (0, 2 * (at // 2) + jnp.where(at % 2 == 0, 1 - core, core))

    half = jax.ShapeDtypeStruct((2, tile, width + 128), bf16)
    return pl.pallas_call(
        functools.partial(grad_down_kernel, micro),
        out_shape=(half, half),
        grid_spec=pltpu.PrefetchScalarGridSpec(
            num_scalar_prefetch=1,
            grid=(4,),
            in_specs=[pl.BlockSpec((block, tile), spot)] * micro
            + [pl.BlockSpec((block, width), lambda at, core_ref: (0, 0))] * micro
            + [pl.BlockSpec((8, tile), spot)],
            out_specs=[pl.BlockSpec((1, tile, width + 128), lambda at, core_ref: (at // 2, 0, 0))] * 2,
        ),
        compiler_params=pltpu.CompilerParams(vmem_limit_bytes=VMEM_LIMIT),
        cost_estimate=pl.CostEstimate(flops=5_400_000_000, bytes_accessed=14_000_000, transcendentals=0),
        name="weight_grad_down",
    )(core, *activated, *grad_low, side)


def grad_up_kernel(counts, core_ref, *refs):
    micro = len(counts)
    hidden, inner, branch = (refs[at * micro : (at + 1) * micro] for at in range(3))
    keep_ref, send_ref, refs = refs[-2], refs[-1], refs[3 * micro : -2]
    mixed = []
    for size in counts:
        mixed.append(refs[:size])
        refs = refs[size:]
    last = pl.num_programs(0) - 1
    core = core_ref[0]

    @pl.when(pl.program_id(0) < last)
    def _():
        total = sum(tn(one[...], two[...]) for one, two in zip(hidden, inner))
        put_halves(core, keep_ref, send_ref, slice(None), total.astype(bf16))

    @pl.when(pl.program_id(0) == last)
    def _():
        total = sum(tn(join(one), two[...]) for one, two in zip(mixed, branch))
        put_halves(core, keep_ref, send_ref, slice(None), total.astype(bf16))


def weight_grad_up(core, hidden_low, grad_inner, attended, grad_branch):
    micro = len(hidden_low)
    block, width = hidden_low[0].shape
    tiles = grad_inner[0].shape[1] // width
    fixed = [pl.BlockSpec((block, width), lambda at, core_ref: (0, 0))] * micro
    parts = [part for one in attended for part in one]
    half = jax.ShapeDtypeStruct((2, width // 4, (tiles + 1) * width), bf16)
    return pl.pallas_call(
        functools.partial(grad_up_kernel, tuple(len(one) for one in attended)),
        out_shape=(half, half),
        grid_spec=pltpu.PrefetchScalarGridSpec(
            num_scalar_prefetch=1,
            grid=(tiles + 1,),
            in_specs=fixed
            + [pl.BlockSpec((block, width), lambda at, core_ref: (0, jnp.minimum(at, tiles - 1)))] * micro
            + fixed
            + [pl.BlockSpec(part.shape, lambda at, core_ref: (0, 0)) for part in parts],
            out_specs=[pl.BlockSpec((2, width // 4, width), lambda at, core_ref: (0, 0, at))] * 2,
        ),
        compiler_params=pltpu.CompilerParams(vmem_limit_bytes=VMEM_LIMIT),
        cost_estimate=pl.CostEstimate(flops=6_800_000_000, bytes_accessed=16_000_000, transcendentals=0),
        name="weight_grad_up",
    )(core, *hidden_low, *grad_inner, *grad_branch, *parts)


def permute(value, axis, pairs):
    return lax.ppermute(value, axis, pairs)


def swap_pairs(size, distance):
    return [(at, at ^ distance) for at in range(size)]


def even_pairs(size):
    return [(at, at ^ 1) for at in range(size)]


def odd_pairs(size):
    return [(at, min(max(((at + 1) ^ 1) - 1, 0), size - 1)) for at in range(size)]


def pick(array, index, axis=0):
    return lax.dynamic_index_in_dim(array, index, axis, keepdims=False)


def ordered(first_here, mine, other, axis=0):
    first = jnp.where(first_here, mine, other)
    second = jnp.where(first_here, other, mine)
    return jnp.concatenate([first, second], axis=axis)


def two_level(mesh_shape):
    return mesh_shape["replica"] == 4 and mesh_shape["fsdp"] == 2 and mesh_shape["seq"] == 4


def sync(*values):
    return lax.optimization_barrier(values)


class Fetch:
    def __init__(self, fast):
        self.fast = fast
        self.here = lax.axis_index("fsdp")
        self.spot = 2 * lax.axis_index("x") + lax.axis_index("core") if fast else None

    def quarter(self, shard):
        if not self.fast:
            return shard
        size = shard.shape[0] // 4
        return lax.dynamic_slice_in_dim(shard, self.spot * size, size, 0)

    def far(self, quarter):
        if not self.fast:
            return [lax.all_gather(quarter, "fsdp", axis=0, tiled=True)]
        return [permute(quarter, "fsdp", swap_pairs(2, 1))]

    def across(self, held):
        if not self.fast:
            return held
        return held + [permute(held[0], "x", swap_pairs(2, 1))]

    def beside(self, held):
        if not self.fast:
            return held
        pair = jnp.stack(held)
        return [pair, permute(pair, "core", swap_pairs(2, 1))]

    def half(self, shard):
        if not self.fast:
            return shard
        size = shard.shape[0] // 2
        return lax.dynamic_slice_in_dim(shard, lax.axis_index("core") * size, size, 0)

    def half_beside(self, held):
        if not self.fast:
            return held
        return held + [permute(held[0], "core", swap_pairs(2, 1))]

    def offsets(self, rows):
        size = rows // 4
        there = (1 - self.here) * rows
        return [self.here * rows], [there + (self.spot ^ flip) * size for flip in (0, 2, 1, 3)]

    def one_weight(self, shard, held):
        if not self.fast:
            return jnp.zeros((1,), jnp.int32), held
        mine, others = self.offsets(shard.shape[0])
        return jnp.stack(mine + others).astype(jnp.int32), [shard] + held

    def middle_weights(self, out_shard, up_shard, down_shard, shared, down):
        if not self.fast:
            width = shared[0].shape[0]
            return (jnp.zeros((3,), jnp.int32), shared[0][:, :width], shared[0][:, width:], [], down)
        mine, others = self.offsets(out_shard.shape[0])
        rows = down_shard.shape[0]
        core = lax.axis_index("core")
        there = (1 - self.here) * rows
        rest = [self.here * rows, there + core * (rows // 2), there + (1 - core) * (rows // 2)]
        offsets = jnp.stack(mine + mine + others + rest).astype(jnp.int32)
        return offsets, out_shard, up_shard, shared, [down_shard] + down

    def with_vectors(self, quarter, shards):
        if not self.fast:
            return quarter
        return jnp.concatenate([quarter, jnp.concatenate(shards).reshape(-1, quarter.shape[1])], axis=0)

    def without_vectors(self, held, shards):
        if not self.fast:
            return held, [lax.all_gather(shard, "fsdp", axis=0, tiled=True) for shard in shards]
        moved = held[0]
        rows = sum(shard.shape[0] for shard in shards) // moved.shape[1]
        far = moved[moved.shape[0] - rows :].reshape(-1)
        full, at = [], 0
        for shard in shards:
            size = shard.shape[0]
            full.append(ordered(self.here == 0, shard, far[at : at + size]))
            at += size
        return [moved[: moved.shape[0] - rows]], full


def halved(part):
    return part.reshape(2, part.shape[0] // 2, part.shape[1])


def low_sum(parts):
    if len(parts) == 1:
        return parts[0]
    return sum(part.astype(f32) for part in parts).astype(bf16)


def add_low(left, right):
    return low_sum([left, right])


class Chain:
    def __init__(self, fast, *parts):
        self.fast = fast
        self.name = None
        self.pair = list(parts)
        self.path, self.depth = [], []

    def views(self):
        found = []
        for part, depth in zip(self.pair, self.depth):
            for name, index in self.path[depth:]:
                part = pick(halved(part) if name == "z1" else part, index)
            found.append(part)
        return found

    def restart(self, *pair):
        self.pair, self.path, self.depth = list(pair), [], [0] * len(pair)

    def settle(self):
        name, pair = self.name, self.pair
        if name == "z3":
            return ordered(lax.axis_index("seq") % 2 == 0, *pair)
        if name == "spread_x":
            return both_ways(lax.axis_index("x") == 0, *pair)
        if name == "spread_core":
            return both_ways(lax.axis_index("core") == 0, *pair)
        return low_sum(self.views())

    def go(self, name):
        if not self.fast:
            return
        if name == "core":
            keep = [part[0] for part in self.pair]
            send = low_sum([part[1] for part in self.pair])
            moved = permute(send, "core", swap_pairs(2, 1))
            self.name = name
            self.restart(*[one.reshape(2, 2, one.shape[1] // 2, one.shape[2]) for one in keep + [moved]])
            return
        if name in ("z2", "z3", "spread_x", "spread_core"):
            held = self.settle()
            axis = {"z2": "seq", "z3": "seq", "spread_x": "x", "spread_core": "core"}[name]
            pairs = {"z2": swap_pairs(4, 2), "z3": swap_pairs(4, 1)}.get(name, swap_pairs(2, 1))
            self.name = name
            self.restart(held, permute(held, axis, pairs))
            return
        axis = {"y": "fsdp", "x": "x", "z1": "seq"}[name]
        here = lax.axis_index(axis)
        parts = self.views()
        if name == "z1":
            here = here % 2
            parts = [halved(part) for part in parts]
        send = low_sum([pick(part, 1 - here) for part in parts])
        moved = permute(send, axis, swap_pairs(4 if axis == "seq" else 2, 1))
        self.path.append((name, here))
        self.pair.append(moved)
        self.depth.append(len(self.path))
        self.name = name

    def final(self):
        if not self.fast:
            keep, send = (sum(part[at].astype(f32) for part in self.pair) for at in (0, 1))
            parts = jnp.stack([keep, send], axis=1).astype(bf16)
            share = lax.psum_scatter(
                parts.reshape(-1, parts.shape[3]), "fsdp", scatter_dimension=0, tiled=True
            )
            return lax.psum(share, ("replica", "seq")).astype(f32)
        full = self.settle()
        return full.reshape(-1, full.shape[-1]).astype(f32)


def both_ways(first_here, mine, other):
    return jnp.stack([jnp.where(first_here, mine, other), jnp.where(first_here, other, mine)])


def settle_all(chains, *values):
    pairs, *values = sync([chain.pair for chain in chains], *values)
    for chain, pair in zip(chains, pairs):
        chain.pair = pair
    return values


def body(
    fast,
    tokens,
    segment_ids,
    joined_weight,
    query_bias,
    value_bias,
    out_weight,
    out_bias,
    norm_gain,
    norm_shift,
    up_weight,
    up_bias,
    down_weight,
    down_bias,
    final_gain,
    final_shift,
    cotangent,
):
    micro, block, width = tokens.shape[1:]
    length = segment_ids.shape[-1]
    size = lax.axis_size("seq")
    place = lax.axis_index("seq")
    hops = (length // 2 - 2) // block + 1
    assert size % 2 == 0 and hops in (1, 2)
    count = 2 * hops + 1
    inner_width = up_weight.shape[1]
    all_pairs = width // PAIR
    half_pairs = all_pairs // 2
    spans = [(0, half_pairs), (half_pairs, half_pairs)]
    fetch = Fetch(fast)

    def masks_of(ids):
        ends = ((0, 0), (hops * block, 0)), ((0, 0), (0, hops * block + TK_FWD - ALIGN))
        padded = jnp.pad(jnp.pad(ids, ends[0], constant_values=-1), ends[1], constant_values=1000)
        near = lax.dynamic_slice_in_dim(padded, place * block, count * block + TK_FWD - ALIGN, 1)
        rows = near[:, hops * block : (hops + 1) * block]
        low = jnp.sum(near < rows[:, :1], axis=1)
        high = jnp.sum(near <= rows[:, -1:], axis=1)
        bounds = jnp.stack([low, high, jnp.broadcast_to(1 - 2 * (place % 2), low.shape)], axis=1)
        segq = jnp.broadcast_to(rows[:, None, :], (micro, 8, block))
        segk = jnp.broadcast_to(near[:, :, None], near.shape + (128,))
        return bounds.astype(jnp.int32).reshape(-1), segq, segk

    def mask_at(batch):
        return (batch,) + tuple(masks)

    own = [tokens[0, batch] for batch in range(micro)]
    moves = [None] * micro
    small_shards = [
        query_bias,
        value_bias,
        out_bias,
        norm_gain,
        norm_shift,
        down_bias,
        final_gain,
        final_shift,
        up_bias,
    ]
    def hop_out(batch, step):
        if step == 0:
            one, two = own[batch], own[batch]
            moves[batch] = [one, permute(one, "seq", even_pairs(size)), permute(two, "seq", odd_pairs(size))]
        else:
            _, even, odd = moves[batch]
            moves[batch] = moves[batch] + [
                permute(even, "seq", odd_pairs(size)),
                permute(odd, "seq", even_pairs(size)),
            ]

    joined = fetch.far(fetch.with_vectors(fetch.quarter(joined_weight), small_shards))
    hop_out(0, 0)
    quarters = [
        jnp.concatenate([fetch.quarter(out_weight), fetch.quarter(up_weight)], axis=1),
        fetch.half(down_weight),
    ]
    shared = fetch.far(quarters[0])
    joined, moves[0], ids, quarters[1] = sync(joined, moves[0], segment_ids, quarters[1])
    joined, vectors = fetch.without_vectors(joined, small_shards)
    joined = fetch.across(joined)
    for step in range(1, hops):
        hop_out(0, step)
    joined, ids, vectors = sync(joined, ids, vectors)
    joined = fetch.beside(joined)
    masks = masks_of(ids[0])
    biases = jnp.pad(jnp.stack(vectors[:2]).astype(f32), ((0, 6), (0, 0)))
    rows_six = jnp.pad(jnp.stack(vectors[2:8]).astype(f32), ((0, 2), (0, 0)))
    up_row = jnp.pad(vectors[8].astype(f32)[None, :], ((0, 7), (0, 0)))
    shared, quarters[1] = sync(shared, quarters[1])
    shared = fetch.across(shared)
    down = fetch.far(quarters[1])
    moves[0], joined, own[1:], biases, rows_six, up_row, masks = sync(
        moves[0], joined, own[1:], biases, rows_six, up_row, masks
    )

    attended = [[] for _ in range(micro)]

    def window(batch):
        one, even, odd, *far = moves[batch]
        return [far[0], odd, one, even, far[1]] if far else [odd, one, even]

    windows = [window(0)] + [None] * (micro - 1)
    weight = fetch.one_weight(joined_weight, joined)

    if micro > 1:
        hop_out(1, 0)
    attended[0].append(tuple(attend_forward((0, all_pairs), mask_at(0), windows[0], weight, biases)))
    attended[0], shared, down, masks, windows[0], moves[1:2] = sync(
        attended[0], shared, down, masks, windows[0], moves[1:2]
    )
    shared = fetch.beside(shared)
    down = fetch.half_beside(down)
    attended[0], shared, down, own = sync(attended[0], shared, down, own)
    for step in range(1, hops if micro > 1 else 0):
        hop_out(1, step)
    middle_weights = fetch.middle_weights(out_weight, up_weight, down_weight, shared, down)

    middles = []
    for batch in range(micro):
        later = batch + 1
        if batch > 0:
            windows[batch] = window(batch)
            for step in range(1, hops if 1 < later < micro else 0):
                hop_out(later, step)
            attended[batch].append(
                tuple(attend_forward((0, all_pairs), mask_at(batch), windows[batch], weight, biases))
            )
            if later < micro:
                attended[batch], moves[later] = sync(attended[batch], moves[later])
        if later + 1 < micro:
            hop_out(later + 1, 0)
        middles.append(
            middle(
                [one[0] for one in attended[batch]],
                own[batch],
                cotangent[0, batch],
                middle_weights,
                rows_six,
                up_row,
            )
        )
        if later + 1 < micro:
            middles[-1], masks, moves[later : later + 2] = sync(middles[-1], masks, moves[later : later + 2])
        else:
            middles[-1], masks = sync(middles[-1], masks)

    core = lax.axis_index("core") if fast else jnp.zeros((), jnp.int32)
    core = core.astype(jnp.int32).reshape(1)
    outs = list(zip(*middles))
    small = sum(outs[8])
    grad_upb = sum(outs[9])
    half = width // 2
    gap = inner_width // 2 - half
    spread = jnp.pad(small[:6].reshape(6, 2, half), ((0, 0), (0, 0), (0, gap))).reshape(6, inner_width)
    side = jnp.concatenate([grad_upb[:1], spread, jnp.zeros((1, inner_width), f32)], axis=0)
    down = Chain(fast, weight_grad_down(core, outs[6], outs[7], side))
    up_ins = (outs[4], outs[5], [[part[0] for part in one] for one in attended], outs[3])
    (up_ins,) = settle_all([down], up_ins)
    down.go("core")
    up = Chain(fast, weight_grad_up(core, *up_ins))
    (masks,) = settle_all([down, up], list(masks))

    backs = [None] * micro
    coming = [None] * micro
    joined_sums = [[], []]
    last = micro - 1

    def run_back(which, batch, chains, moving=()):
        span, groups = ((0, all_pairs), 2) if which is None else (spans[which], 1)
        before = backs[batch] if which == 1 else [outs[1][batch]]
        results = attend_backward(
            core, span, groups, mask_at(batch), windows[batch], weight, biases, attended[batch],
            outs[2][batch], before
        )
        parts, halves = list(results[:count]), list(results[count:])
        moved = [coming[at] for at in moving]
        backs[batch], halves, masks[:], moved = settle_all(chains, parts, halves, list(masks), moved)
        for at, one in zip(moving, moved):
            coming[at] = one
        for at in range(groups):
            joined_sums[which or at].append(halves[2 * at : 2 * at + 2])

    def total_of(which):
        return Chain(fast, *joined_sums[which])

    def hop_back(batch, step):
        parts = backs[batch]
        if step == 0 and hops > 1:
            coming[batch] = [
                permute(parts[hops + 2], "seq", even_pairs(size)),
                permute(parts[hops - 2], "seq", odd_pairs(size)),
            ]
            return
        odd, even = parts[hops - 1], parts[hops + 1]
        if hops > 1:
            odd, even = add_low(odd, coming[batch][0]), add_low(even, coming[batch][1])
        coming[batch] = [permute(odd, "seq", odd_pairs(size)), permute(even, "seq", even_pairs(size))]

    down.go("y")
    up.go("core")
    run_back(None, 0, [up, down])
    down.go("x")
    up.go("y")
    middle_steps = [
        ([], [down]),
        ([(down, "z1")], [down, up]),
        ([(down, "z2"), (up, "x")], [down, up]),
        ([(down, "z3"), (up, "z1")], [down, up]),
    ]
    for batch in range(1, micro):
        for which in (0, 1):
            begin, end = middle_steps.pop(0) if middle_steps else ([], [])
            for chain, name in begin:
                chain.go(name)
            if which == 0:
                hop_back(batch - 1, 0)
            else:
                for step in range(1, hops):
                    hop_back(batch - 1, step)
            if batch == last and which == 1:
                joined_one = total_of(0)
                joined_one.go("core")
                end = end + [joined_one]
            run_back(which, batch, end, [batch - 1])

    joined_two = total_of(1)
    joined_two.go("core")
    joined_one.go("y")
    hop_back(last, 0)
    down.go("spread_x")
    (backs,) = settle_all([joined_two], backs)
    joined_two.go("y")
    coming, backs = settle_all([joined_one], coming, backs)
    joined_one.go("x")
    for step in range(1, hops):
        hop_back(last, step)
    settle_all([joined_two, joined_one, down])
    joined_two.go("x")
    joined_one.go("z1")
    up.go("z2")
    down.go("spread_core")
    (coming,) = settle_all([joined_two, joined_one], coming)
    joined_two.go("z1")
    joined_one.go("z2")
    settle_all([joined_two, joined_one, up])
    joined_two.go("z2")
    joined_one.go("z3")
    up.go("z3")
    settle_all([joined_two, joined_one, up])
    joined_two.go("z3")
    joined_one.go("spread_x")
    up.go("spread_x")
    settle_all([joined_two, joined_one])
    joined_two.go("spread_x")
    joined_one.go("spread_core")
    settle_all([joined_two, up])
    up.go("spread_core")
    joined_two.go("spread_core")

    final_down = down.final()
    final_up = up.final()
    final_up, final_out = final_up[:, :inner_width], final_up[:, inner_width:]
    final_a, final_b = joined_one.final(), joined_two.final()
    grad_tokens = []
    for batch in range(micro):
        total = backs[batch][hops] + sum(one.astype(f32) for one in coming[batch])
        grad_tokens.append(total.astype(bf16))
    low, high = spans[0][1] * PAIR, spans[1][1] * PAIR
    final_joined = jnp.concatenate(
        [
            part
            for at in range(3)
            for part in (final_a[:, at * low : (at + 1) * low], final_b[:, at * high : (at + 1) * high])
        ],
        axis=1,
    )
    bias_sums = final_a[:, 3 * low : 3 * low + 2] + final_b[:, 3 * high : 3 * high + 2]
    if fast:
        own_rows = width // lax.axis_size("fsdp")
        smalls = [final_down[:own_rows, width + 1 + at] for at in range(6)]
    else:
        smalls = [
            lax.psum_scatter(lax.psum(small[at], ("replica", "seq")), "fsdp", scatter_dimension=0, tiled=True)
            for at in range(6)
        ]
    return (
        jnp.stack(outs[0], axis=0)[None],
        jnp.stack(grad_tokens, axis=0)[None],
        final_joined,
        bias_sums[:, 0],
        bias_sums[:, 1],
        final_out,
        smalls[0],
        smalls[1],
        smalls[2],
        final_up,
        final_down[:, width],
        final_down[:, :width],
        smalls[3],
        smalls[4],
        smalls[5],
    )


def solution(mesh):
    fast = two_level(dict(mesh.shape))
    groups = ("replica", "fsdp")
    if fast:
        mesh = jax.sharding.Mesh(mesh.devices.reshape(2, 2, 2, 4), ("x", "core", "fsdp", "seq"))
        groups = ("x", "core", "fsdp")
    rows = P(groups, None, "seq", None)
    matrix, vector = P("fsdp", None), P("fsdp")
    in_specs = (
        rows,
        P(groups, None, None),
        matrix,
        vector,
        vector,
        matrix,
        vector,
        vector,
        vector,
        matrix,
        vector,
        matrix,
        vector,
        vector,
        vector,
        rows,
    )
    out_specs = (
        rows,
        rows,
        matrix,
        vector,
        vector,
        matrix,
        vector,
        vector,
        vector,
        matrix,
        vector,
        matrix,
        vector,
        vector,
        vector,
    )
    return jax.shard_map(
        functools.partial(body, fast),
        mesh=mesh,
        in_specs=in_specs,
        out_specs=out_specs,
        check_vma=False,
    )
```

```python
import functools
import jax
import jax.numpy as jnp
from jax import lax
from jax.experimental import pallas as pl
from jax.experimental.pallas import tpu as pltpu
from jax.sharding import PartitionSpec as P

HEADS = 12
HEAD_DIM = 64
PAIR = 2 * HEAD_DIM
epsilon = 1e-05
masked_score = -1e30
scale = HEAD_DIM ** (-0.5)
TK_FWD = 256
TK_BWD = 256
ALIGN = 128
ROW_STEP = 16
VMEM_LIMIT = 62 * 1024 * 1024
FF_TILES = 4
f32 = jnp.float32
bf16 = jnp.bfloat16


def nt(left, right):
    return lax.dot_general(left, right, (((1,), (1,)), ((), ())), preferred_element_type=f32)


def tn(left, right):
    return lax.dot_general(left, right, (((0,), (0,)), ((), ())), preferred_element_type=f32)


def nn(left, right):
    return lax.dot_general(left, right, (((1,), (0,)), ((), ())), preferred_element_type=f32)


def stack_heads(pair):
    lane = lax.broadcasted_iota(jnp.int32, pair.shape, 1)
    zero = jnp.zeros_like(pair)
    return jnp.concatenate(
        [jnp.where(lane < HEAD_DIM, pair, zero), jnp.where(lane < HEAD_DIM, zero, pair)], axis=0
    )


def unstack_heads(rows):
    half = rows.shape[0] // 2
    lane = lax.broadcasted_iota(jnp.int32, (half, rows.shape[1]), 1)
    return jnp.where(lane < HEAD_DIM, rows[:half], rows[half:])


def split_pieces(refs):
    pieces = []
    for ref in refs:
        if len(ref.shape) == 2:
            pieces.append(ref)
        else:
            pieces.extend(ref.at[at] for at in range(ref.shape[0]))
    return pieces


def count_pieces(arrays):
    return sum(1 if len(one.shape) == 2 else one.shape[0] for one in arrays)


def start_columns(offsets, piece_refs, full_s, sems, width, at_col, size_col):
    copies = []
    for at, piece in enumerate(split_pieces(piece_refs)):
        size = piece.shape[0]
        row = pl.multiple_of(offsets[at], ROW_STEP)
        for part in range(3):
            copy = pltpu.make_async_copy(
                piece.at[:, pl.ds(part * width + at_col, size_col)],
                full_s.at[pl.ds(row, size), pl.ds(part * size_col, size_col)],
                sems.at[at, part],
            )
            copy.start()
            copies.append(copy)
    return copies


def wait_all(copies):
    for copy in copies:
        copy.wait()


def first_row(bounds, at, count, block):
    middle = count // 2
    return pl.multiple_of((middle + bounds[2] * (at - middle)) * block, ALIGN)


def reached(bounds, at, count, block):
    row = first_row(bounds, at, count, block)
    return (bounds[1] > row) & (bounds[0] < row + block)


def block_copy(bounds, x_refs, x_s, sems, at):
    block = x_refs[at].shape[0]
    row = first_row(bounds, at, len(x_refs), block)
    return pltpu.make_async_copy(x_refs[at], x_s.at[pl.ds(row, block), :], sems.at[at])


def fetch_window(bounds, x_refs, x_s, sems):
    for at in range(len(x_refs)):

        @pl.when(reached(bounds, at, len(x_refs), x_refs[at].shape[0]))
        def _():
            block_copy(bounds, x_refs, x_s, sems, at).start()


def project_window(bounds, x_refs, x_s, sems, w_ref, bias_ref, cols, k_s, v_s, tail):
    block = x_refs[0].shape[0]
    width = k_s.shape[1]
    for at in range(len(x_refs)):
        rows = pl.ds(first_row(bounds, at, len(x_refs), block), block)
        active = reached(bounds, at, len(x_refs), block)

        @pl.when(active)
        def _():
            block_copy(bounds, x_refs, x_s, sems, at).wait()
            x = x_s[rows, :]
            both = nn(x, w_ref[:, width:])
            k_s[rows, :] = both[:, :width].astype(bf16)
            v_s[rows, :] = (both[:, width:] + bias_ref[1:2, cols]).astype(bf16)

        @pl.when(jnp.logical_not(active))
        def _():
            k_s[rows, :] = jnp.zeros((block, width), bf16)
            v_s[rows, :] = jnp.zeros((block, width), bf16)

    end = len(x_refs) * block
    k_s[end:, :] = jnp.zeros((tail, width), bf16)
    v_s[end:, :] = jnp.zeros((tail, width), bf16)


def tile_range(bounds, tk):
    low = bounds[0]
    high = bounds[1]
    start = (low // ALIGN) * ALIGN
    return start, (high - start + tk - 1) // tk


def project_queries(x, w_ref, bias_ref, cols, q_s, qq_s):
    width = q_s.shape[1]
    q = nn(x, w_ref[:, :width]) + bias_ref[0:1, cols]
    q_s[...] = q.astype(bf16) * jnp.asarray(scale, bf16)
    for pair in range(width // PAIR):
        here = slice(pair * PAIR, (pair + 1) * PAIR)
        qq_s[:, here] = stack_heads(q_s[:, here])


def forward_kernel(batch, hops, pieces, first, all_bounds, offsets, *refs):
    bounds = [all_bounds[3 * batch + at] for at in range(3)]
    count = 2 * hops + 1
    x_refs = refs[:count]
    w_refs, refs = refs[count : count + pieces], refs[count + pieces :]
    bias_ref, segq_ref, segk_any, o_ref, lse_ref = refs[:5]
    segk_ref, seg_sem, x_s, w_ref, q_s, qq_s, k_s, v_s, top_s, sum_s, acc_s, x_sems, sems = refs[5:]
    seg_copy = pltpu.make_async_copy(segk_any.at[batch], segk_ref, seg_sem)
    seg_copy.start()
    block, full_width = x_refs[0].shape
    width = o_ref.shape[1]
    own_rows = slice(hops * block, (hops + 1) * block)
    tk = TK_FWD
    pairs = width // PAIR
    cols_all = slice(first * PAIR, first * PAIR + width)
    copies = start_columns(offsets, w_refs, w_ref, sems, full_width, first * PAIR, width)
    fetch_window(bounds, x_refs, x_s, x_sems)
    wait_all(copies)
    project_window(bounds, x_refs, x_s, x_sems, w_ref, bias_ref, cols_all, k_s, v_s, tk - ALIGN)
    project_queries(x_s[own_rows, :], w_ref, bias_ref, cols_all, q_s, qq_s)
    start, steps = tile_range(bounds, tk)
    seg_copy.wait()
    segq = segq_ref[batch, 0:1, :]
    segq = jnp.concatenate([segq, segq], axis=1)
    top_s[...] = jnp.full(top_s.shape, masked_score, f32)
    sum_s[...] = jnp.ones(sum_s.shape, f32)
    sum_s[:pairs, :] = jnp.zeros((pairs, sum_s.shape[1]), f32)
    acc_s[...] = jnp.zeros(acc_s.shape, f32)

    @pl.loop(0, steps)
    def _(at):
        here = pl.ds(pl.multiple_of(start + at * tk, ALIGN), tk)
        allowed = segk_ref[here, 0:1] == segq
        for pair in range(pairs):
            cols = slice(pair * PAIR, (pair + 1) * PAIR)
            one = slice(pair, pair + 1)
            scores = nt(k_s[here, cols], qq_s[:, cols])
            scores = jnp.where(allowed, scores, masked_score)
            top = top_s[one, :]
            new_top = jnp.maximum(top, jnp.max(scores, axis=0, keepdims=True))
            fade = jnp.exp(top - new_top)
            weights = jnp.exp(scores - new_top)
            top_s[one, :] = new_top
            sum_s[one, :] = sum_s[one, :] * fade + jnp.sum(weights, axis=0, keepdims=True)
            acc_s[pair] = acc_s[pair] * fade + tn(v_s[here, cols], weights.astype(bf16))

    lse_ref[...] = top_s[...] + jnp.log(sum_s[...])
    for pair in range(pairs):
        cols = slice(pair * PAIR, (pair + 1) * PAIR)
        mixed = acc_s[pair] / sum_s[pair : pair + 1, :]
        o_ref[:, cols] = unstack_heads(mixed.T).astype(bf16)


def backward_kernel(batch, hops, pieces, prev, first, skip, all_bounds, offsets, core_ref, *refs):
    bounds = [all_bounds[3 * batch + at] for at in range(3)]
    count = 2 * hops + 1
    x_refs = refs[:count]
    w_refs, refs = refs[count : count + pieces], refs[count + pieces :]
    bias_ref, segq_ref, segk_any, o_ref, lse_ref, do_ref = refs[:6]
    prev_refs, refs = refs[6 : 6 + prev], refs[6 + prev :]
    out_refs, refs = refs[:count], refs[count:]
    keep_ref, send_ref, segk_ref, seg_sem, *refs = refs
    seg_copy = pltpu.make_async_copy(segk_any.at[batch], segk_ref, seg_sem)
    seg_copy.start()
    x_s, p_s, own_s, w_ref, q_s, qq_s, gg_s, k_s, v_s, dk_s, dv_s, dw_s, stat_s, acc_s, db_s = refs[:15]
    x_sems, p_sems, o_sems, sems = refs[15:]
    block, full_width = x_refs[0].shape
    width = q_s.shape[1]
    tk = TK_BWD
    pairs = width // PAIR
    cols_all = slice(first * PAIR, first * PAIR + width)
    own_rows = slice(hops * block, (hops + 1) * block)
    others = [at for at in range(count) if at != hops]
    copies = start_columns(offsets, w_refs, w_ref, sems, full_width, first * PAIR, width)
    fetch_window(bounds, x_refs, x_s, x_sems)
    own_copy = pltpu.make_async_copy(prev_refs[hops if prev > 1 else 0], own_s, p_sems.at[hops])
    own_copy.start()

    def stage(at):
        return p_s.at[pl.ds(at * block, block), :]

    def prev_copy(at):
        return pltpu.make_async_copy(prev_refs[at], stage(at), p_sems.at[at])

    def out_copy(at):
        return pltpu.make_async_copy(own_s if at == hops else stage(at), out_refs[at], o_sems.at[at])

    for at in others:
        active = reached(bounds, at, count, block)
        if prev > 1:

            @pl.when(active)
            def _():
                prev_copy(at).start()

        else:

            @pl.when(jnp.logical_not(active))
            def _():
                p_s[at * block : (at + 1) * block, :] = jnp.zeros((block, full_width), bf16)
                out_copy(at).start()

    dk_s[...] = jnp.zeros(dk_s.shape, f32)
    dv_s[...] = jnp.zeros(dv_s.shape, f32)
    acc_s[...] = jnp.zeros(acc_s.shape, f32)
    for pair in range(pairs):
        cols = slice(pair * PAIR, (pair + 1) * PAIR)
        far = slice((first + pair) * PAIR, (first + pair + 1) * PAIR)
        theirs = slice((skip + pair) * PAIR, (skip + pair + 1) * PAIR)
        grads = stack_heads(do_ref[:, far])
        gg_s[:, cols] = grads
        mixed = o_ref[:, theirs].astype(f32)
        product = grads.astype(f32) * jnp.concatenate([mixed, mixed], axis=0)
        stat_s[pair : pair + 1, :] = jnp.sum(product.T, axis=0, keepdims=True)
    wait_all(copies)
    project_window(bounds, x_refs, x_s, x_sems, w_ref, bias_ref, cols_all, k_s, v_s, tk - ALIGN)
    project_queries(x_s[own_rows, :], w_ref, bias_ref, cols_all, q_s, qq_s)
    start, steps = tile_range(bounds, tk)
    seg_copy.wait()
    segq = segq_ref[batch, 0:1, :]
    segq = jnp.concatenate([segq, segq], axis=1)

    @pl.loop(0, steps)
    def _(at):
        here = pl.ds(pl.multiple_of(start + at * tk, ALIGN), tk)
        allowed = segk_ref[here, 0:1] == segq
        for pair in range(pairs):
            cols = slice(pair * PAIR, (pair + 1) * PAIR)
            keys = k_s[here, cols]
            queries = qq_s[:, cols]
            grads = gg_s[:, cols]
            scores = nt(keys, queries)
            scores = jnp.where(allowed, scores, masked_score)
            weights = jnp.exp(scores - lse_ref[skip + pair : skip + pair + 1, :])
            grad_weights = nt(v_s[here, cols], grads)
            grad_scores = (weights * (grad_weights - stat_s[pair : pair + 1, :])).astype(bf16)
            dv_s[here, cols] += nn(weights.astype(bf16), grads)
            dk_s[here, cols] += nn(grad_scores, queries)
            acc_s[pair] += tn(keys, grad_scores)

    for pair in range(pairs):
        cols = slice(pair * PAIR, (pair + 1) * PAIR)
        q_s[:, cols] = (unstack_heads(acc_s[pair].T) * scale).astype(bf16)
    dq = q_s[...]
    db_s[...] = jnp.zeros(db_s.shape, f32)
    db_s[0:1, cols_all] = jnp.sum(dq.astype(f32), axis=0, keepdims=True)

    def rows_of(at):
        rows = pl.ds(first_row(bounds, at, count, block), block)
        dk = dk_s[rows, :].astype(bf16)
        dv = dv_s[rows, :].astype(bf16)
        db_s[1:2, cols_all] += jnp.sum(dv.astype(f32), axis=0, keepdims=True)
        return [dk, dv]

    grads = jnp.concatenate([dq] + rows_of(hops), axis=1)
    own_copy.wait()
    own_s[...] += nt(grads, w_ref[...])
    out_copy(hops).start()
    dw_s[...] = tn(x_s[own_rows, :], grads)
    for at in others:

        @pl.when(reached(bounds, at, count, block))
        def _():
            rows = slice(at * block, (at + 1) * block)
            grads = jnp.concatenate(rows_of(at), axis=1)
            back = nt(grads, w_ref[:, width:])
            if prev > 1:
                prev_copy(at).wait()
                back = back + p_s[rows, :].astype(f32)
            p_s[rows, :] = back.astype(bf16)
            out_copy(at).start()
            x = x_s[pl.ds(first_row(bounds, at, count, block), block), :]
            dw_s[:, width:] += tn(x, grads)

    put_halves(core_ref[0], keep_ref, send_ref, slice(0, 3 * width), dw_s[...].astype(bf16))
    side = jnp.concatenate([db_s[...], jnp.zeros((120, full_width), f32)], axis=0).T
    put_halves(core_ref[0], keep_ref, send_ref, slice(3 * width, 3 * width + 128), side.astype(bf16))
    out_copy(hops).wait()
    for at in others:
        if prev > 1:

            @pl.when(reached(bounds, at, count, block))
            def _():
                out_copy(at).wait()

        else:
            out_copy(at).wait()


def whole():
    return pl.BlockSpec(memory_space=pltpu.VMEM)


def smem():
    return pl.BlockSpec(memory_space=pltpu.SMEM)


def raw():
    return pl.BlockSpec(memory_space=pl.ANY)


def attend_forward(span, mask, window, weight, biases):
    batch, bounds, segq, segk = mask
    offsets, pieces = weight
    first, pairs = span
    count = len(window)
    block, full_width = window[0].shape
    width = pairs * PAIR
    padded = count * block + TK_FWD - ALIGN
    return pl.pallas_call(
        functools.partial(forward_kernel, batch, count // 2, len(pieces), first),
        out_shape=(
            jax.ShapeDtypeStruct((block, width), bf16),
            jax.ShapeDtypeStruct((8, 2 * block), f32),
        ),
        in_specs=[smem()] * 2
        + [raw()] * (count + len(pieces))
        + [whole(), whole(), raw()],
        out_specs=(whole(), whole()),
        scratch_shapes=[
            pltpu.VMEM(segk.shape[1:], jnp.int32),
            pltpu.SemaphoreType.DMA,
            pltpu.VMEM((count * block, full_width), bf16),
            pltpu.VMEM((full_width, 3 * width), bf16),
            pltpu.VMEM((block, width), bf16),
            pltpu.VMEM((2 * block, width), bf16),
            pltpu.VMEM((padded, width), bf16),
            pltpu.VMEM((padded, width), bf16),
            pltpu.VMEM((8, 2 * block), f32),
            pltpu.VMEM((8, 2 * block), f32),
            pltpu.VMEM((pairs, PAIR, 2 * block), f32),
            pltpu.SemaphoreType.DMA((count,)),
            pltpu.SemaphoreType.DMA((count_pieces(pieces), 3)),
        ],
        compiler_params=pltpu.CompilerParams(vmem_limit_bytes=VMEM_LIMIT),
        cost_estimate=pl.CostEstimate(
            flops=2_500_000_000 * pairs, bytes_accessed=8_000_000, transcendentals=4_000_000
        ),
        name="attend_forward",
    )(bounds, offsets, *window, *pieces, biases, segq, segk)


def attend_backward(core, span, mask, window, weight, biases, attended, grad, before):
    batch, bounds, segq, segk = mask
    offsets, pieces = weight
    first, pairs = span
    count = len(window)
    block, full_width = window[0].shape
    width = pairs * PAIR
    hops = count // 2
    padded = count * block + TK_BWD - ALIGN
    per_part = full_width // PAIR // len(attended)
    mixed, lse = attended[first // per_part]
    at = first // per_part * per_part
    outs = [
        jax.ShapeDtypeStruct((block, full_width), f32 if at == hops else bf16) for at in range(count)
    ]
    return pl.pallas_call(
        functools.partial(backward_kernel, batch, hops, len(pieces), len(before), first, first - at),
        out_shape=(
            *outs,
            jax.ShapeDtypeStruct((2, full_width // 4, 3 * width + 128), bf16),
            jax.ShapeDtypeStruct((2, full_width // 4, 3 * width + 128), bf16),
        ),
        in_specs=[smem()] * 3
        + [raw()] * (count + len(pieces))
        + [whole(), whole(), raw()]
        + [whole()] * 3
        + [raw()] * len(before),
        out_specs=(raw(),) * count + (whole(),) * 2,
        input_output_aliases=(
            {9 + count + len(pieces) + at: at for at in range(count)} if len(before) > 1 else {}
        ),
        scratch_shapes=[
            pltpu.VMEM(segk.shape[1:], jnp.int32),
            pltpu.SemaphoreType.DMA,
            pltpu.VMEM((count * block, full_width), bf16),
            pltpu.VMEM((count * block, full_width), bf16),
            pltpu.VMEM((block, full_width), f32),
            pltpu.VMEM((full_width, 3 * width), bf16),
            pltpu.VMEM((block, width), bf16),
            pltpu.VMEM((2 * block, width), bf16),
            pltpu.VMEM((2 * block, width), bf16),
            pltpu.VMEM((padded, width), bf16),
            pltpu.VMEM((padded, width), bf16),
            pltpu.VMEM((padded, width), f32),
            pltpu.VMEM((padded, width), f32),
            pltpu.VMEM((full_width, 3 * width), f32),
            pltpu.VMEM((8, 2 * block), f32),
            pltpu.VMEM((pairs, PAIR, 2 * block), f32),
            pltpu.VMEM((8, full_width), f32),
            pltpu.SemaphoreType.DMA((count,)),
            pltpu.SemaphoreType.DMA((count,)),
            pltpu.SemaphoreType.DMA((count,)),
            pltpu.SemaphoreType.DMA((count_pieces(pieces), 3)),
        ],
        compiler_params=pltpu.CompilerParams(vmem_limit_bytes=VMEM_LIMIT),
        cost_estimate=pl.CostEstimate(
            flops=5_000_000_000 * pairs, bytes_accessed=20_000_000, transcendentals=4_000_000
        ),
        name="attend_backward",
    )(bounds, offsets, core, *window, *pieces, biases, segq, segk, mixed, lse, grad, *before)


def join(refs):
    if len(refs) == 1:
        return refs[0][...]
    return jnp.concatenate([ref[...] for ref in refs], axis=1)


def middle_kernel(
    counts, offsets, tokens_ref, cot_ref, vec_ref, upb_ref, *refs
):
    n_mixed, n_shared, n_down = counts
    mixed_refs, refs = refs[:n_mixed], refs[n_mixed:]
    out_own, up_own, refs = refs[0], refs[1], refs[2:]
    shared, down_p = split_pieces(refs[:n_shared]), split_pieces(refs[n_shared : n_shared + n_down])
    refs = refs[n_shared + n_down :]
    n_shared = len(shared)
    (
        result_ref, one_ref, mixed_ref, branch_ref, hidden_ref, inner_ref, act_ref, two_ref,
        small_ref, gupb_ref,
    ) = refs[:10]
    wo_s, up_s, down_s, slope_s, act_s, inner_s, leave_sems, sems = refs[10:]
    width = wo_s.shape[1]
    leaving = []
    out_copies, up_copies, down_copies = [], [], []

    def begin(copies, at, source, target):
        row = pl.multiple_of(offsets[at], ROW_STEP)
        copy = pltpu.make_async_copy(
            source, target.at[pl.ds(row, source.shape[0]), :], sems.at[at, len(copies) % 2]
        )
        copy.start()
        copies.append(copy)

    begin(out_copies, 0, out_own, wo_s)
    for at, piece in enumerate(shared):
        row = pl.multiple_of(offsets[2 + at], ROW_STEP)
        copy = pltpu.make_async_copy(
            piece.at[:, pl.ds(0, width)], wo_s.at[pl.ds(row, piece.shape[0]), :], sems.at[2 + at, 0]
        )
        copy.start()
        out_copies.append(copy)
    begin(up_copies, 1, up_own, up_s)
    for at, piece in enumerate(shared):
        row = pl.multiple_of(offsets[2 + at], ROW_STEP)
        copy = pltpu.make_async_copy(
            piece.at[:, pl.ds(width, up_s.shape[1])],
            up_s.at[pl.ds(row, piece.shape[0]), :],
            sems.at[2 + at, 1],
        )
        copy.start()
        up_copies.append(copy)
    for at, piece in enumerate(down_p):
        row = pl.multiple_of(offsets[2 + n_shared + at], ROW_STEP)
        copy = pltpu.make_async_copy(
            piece, down_s.at[pl.ds(row, piece.shape[0]), :], sems.at[2 + n_shared + at, 0]
        )
        copy.start()
        down_copies.append(copy)
    inner_width = up_s.shape[1]
    tile = inner_width // FF_TILES
    out_bias, norm_gain, norm_shift = vec_ref[0:1, :], vec_ref[1:2, :], vec_ref[2:3, :]
    down_bias, final_gain, final_shift = vec_ref[3:4, :], vec_ref[4:5, :], vec_ref[5:6, :]
    wait_all(out_copies)
    values = tokens_ref[...].astype(f32) + (nn(join(mixed_refs), wo_s[...]) + out_bias)
    centered = values - jnp.mean(values, axis=1, keepdims=True)
    inverse_one = lax.rsqrt(jnp.mean(centered * centered, axis=1, keepdims=True) + epsilon)
    normed_one = centered * inverse_one
    hidden = normed_one * norm_gain + norm_shift
    hidden_low = hidden.astype(bf16)
    hidden_ref[...] = hidden_low
    wait_all(up_copies)
    def up_tile(at):
        cols = slice(at * tile, (at + 1) * tile)
        return nn(hidden_low, up_s[:, cols]) + upb_ref[0:1, cols]

    branch_two = None
    inner = up_tile(0)
    wait_all(down_copies)
    for at in range(FF_TILES):
        cols = slice(at * tile, (at + 1) * tile)
        normal = 0.5 * (1.0 + lax.erf(inner * 0.7071067811865476))
        density = jnp.exp(-0.5 * inner * inner) * 0.3989422804014327
        slope_s[:, cols] = normal + inner * density
        activated = (inner * normal).astype(bf16)
        act_s[:, cols] = activated
        leaving.append(pltpu.make_async_copy(act_s.at[:, cols], act_ref.at[:, cols], leave_sems.at[0, at]))
        leaving[-1].start()
        term = nn(activated, down_s[cols, :])
        branch_two = term if branch_two is None else branch_two + term
        if at + 1 < FF_TILES:
            inner = up_tile(at + 1)
    values = hidden + (branch_two + down_bias)
    centered = values - jnp.mean(values, axis=1, keepdims=True)
    inverse_two = lax.rsqrt(jnp.mean(centered * centered, axis=1, keepdims=True) + epsilon)
    normed_two = centered * inverse_two
    result_ref[...] = (normed_two * final_gain + final_shift).astype(bf16)
    cot = cot_ref[...].astype(f32)
    small_ref[4:5, :] = jnp.sum(cot * normed_two, axis=0, keepdims=True)
    small_ref[5:6, :] = jnp.sum(cot, axis=0, keepdims=True)
    scaled = cot * final_gain
    first = jnp.mean(scaled, axis=1, keepdims=True)
    second = jnp.mean(scaled * normed_two, axis=1, keepdims=True)
    grad_two = inverse_two * (scaled - first - normed_two * second)
    grad_low = grad_two.astype(bf16)
    two_ref[...] = grad_low
    small_ref[3:4, :] = jnp.sum(grad_low.astype(f32), axis=0, keepdims=True)
    grad_hidden = grad_two
    gupb_ref[...] = jnp.zeros(gupb_ref.shape, f32)
    for at in range(FF_TILES):
        cols = slice(at * tile, (at + 1) * tile)
        grad_inner = (nt(grad_low, down_s[cols, :]) * slope_s[:, cols]).astype(bf16)
        inner_s[:, cols] = grad_inner
        leaving.append(pltpu.make_async_copy(inner_s.at[:, cols], inner_ref.at[:, cols], leave_sems.at[1, at]))
        leaving[-1].start()
        gupb_ref[0:1, cols] = jnp.sum(grad_inner.astype(f32), axis=0, keepdims=True)
        grad_hidden = grad_hidden + nt(grad_inner, up_s[:, cols])
    small_ref[1:2, :] = jnp.sum(grad_hidden * normed_one, axis=0, keepdims=True)
    small_ref[2:3, :] = jnp.sum(grad_hidden, axis=0, keepdims=True)
    scaled = grad_hidden * norm_gain
    first = jnp.mean(scaled, axis=1, keepdims=True)
    second = jnp.mean(scaled * normed_one, axis=1, keepdims=True)
    grad_one = inverse_one * (scaled - first - normed_one * second)
    one_ref[...] = grad_one
    grad_branch = grad_one.astype(bf16)
    branch_ref[...] = grad_branch
    small_ref[0:1, :] = jnp.sum(grad_branch.astype(f32), axis=0, keepdims=True)
    small_ref[6:8, :] = jnp.zeros((2, small_ref.shape[1]), f32)
    mixed_ref[...] = nt(grad_branch, wo_s[...]).astype(bf16)
    wait_all(leaving)


def middle(attended, tokens, cotangent, weights, vectors, up_bias):
    offsets, out_own, up_own, shared, down = weights
    counts = (len(attended), len(shared), len(down))
    pieces = [out_own, up_own, *shared, *down]
    block, width = tokens.shape
    inner_width = up_bias.shape[1]
    return pl.pallas_call(
        functools.partial(middle_kernel, counts),
        out_shape=(
            jax.ShapeDtypeStruct((block, width), bf16),
            jax.ShapeDtypeStruct((block, width), f32),
            jax.ShapeDtypeStruct((block, width), bf16),
            jax.ShapeDtypeStruct((block, width), bf16),
            jax.ShapeDtypeStruct((block, width), bf16),
            jax.ShapeDtypeStruct((block, inner_width), bf16),
            jax.ShapeDtypeStruct((block, inner_width), bf16),
            jax.ShapeDtypeStruct((block, width), bf16),
            jax.ShapeDtypeStruct((8, width), f32),
            jax.ShapeDtypeStruct((8, inner_width), f32),
        ),
        in_specs=[smem()] + [whole()] * (4 + len(attended)) + [raw()] * len(pieces),
        out_specs=(whole(),) * 5 + (raw(),) * 2 + (whole(),) * 3,
        scratch_shapes=[
            pltpu.VMEM((width, width), bf16),
            pltpu.VMEM((width, inner_width), bf16),
            pltpu.VMEM((inner_width, width), bf16),
            pltpu.VMEM((block, inner_width), f32),
            pltpu.VMEM((block, inner_width), bf16),
            pltpu.VMEM((block, inner_width), bf16),
            pltpu.SemaphoreType.DMA((2, FF_TILES)),
            pltpu.SemaphoreType.DMA((count_pieces(pieces), 2)),
        ],
        compiler_params=pltpu.CompilerParams(vmem_limit_bytes=VMEM_LIMIT),
        cost_estimate=pl.CostEstimate(flops=24_000_000_000, bytes_accessed=20_000_000, transcendentals=4_000_000),
        name="middle",
    )(offsets, tokens, cotangent, vectors, up_bias, *attended, *pieces)


def grad_down_kernel(micro, core_ref, *refs):
    act_refs, two_refs, side_ref = refs[:micro], refs[micro : 2 * micro], refs[-3]
    total = sum(tn(act[...], two[...]) for act, two in zip(act_refs, two_refs))
    rows, width = total.shape
    side = jnp.concatenate([side_ref[...], jnp.zeros((120, rows), f32)], axis=0).T

    def put(ref):
        ref[0, :, :width] = total.astype(bf16)
        ref[0, :, width:] = side.astype(bf16)

    @pl.when(pl.program_id(0) % 2 == 0)
    def _():
        put(refs[-1])

    @pl.when(pl.program_id(0) % 2 == 1)
    def _():
        put(refs[-2])


def put_halves(core, keep_ref, send_ref, cols, value):
    rows, width = value.shape
    halves = value.reshape(2, 2, rows // 4, width)

    @pl.when(core == 0)
    def _():
        keep_ref[:, :, cols] = halves[:, 0]
        send_ref[:, :, cols] = halves[:, 1]

    @pl.when(core == 1)
    def _():
        keep_ref[:, :, cols] = halves[:, 1]
        send_ref[:, :, cols] = halves[:, 0]


def weight_grad_down(core, activated, grad_low, side):
    micro = len(activated)
    block, inner_width = activated[0].shape
    width = grad_low[0].shape[1]
    tile = inner_width // 4

    def spot(at, core_ref):
        core = core_ref[0]
        return (0, 2 * (at // 2) + jnp.where(at % 2 == 0, 1 - core, core))

    half = jax.ShapeDtypeStruct((2, tile, width + 128), bf16)
    return pl.pallas_call(
        functools.partial(grad_down_kernel, micro),
        out_shape=(half, half),
        grid_spec=pltpu.PrefetchScalarGridSpec(
            num_scalar_prefetch=1,
            grid=(4,),
            in_specs=[pl.BlockSpec((block, tile), spot)] * micro
            + [pl.BlockSpec((block, width), lambda at, core_ref: (0, 0))] * micro
            + [pl.BlockSpec((8, tile), spot)],
            out_specs=[pl.BlockSpec((1, tile, width + 128), lambda at, core_ref: (at // 2, 0, 0))] * 2,
        ),
        compiler_params=pltpu.CompilerParams(vmem_limit_bytes=VMEM_LIMIT),
        cost_estimate=pl.CostEstimate(flops=5_400_000_000, bytes_accessed=14_000_000, transcendentals=0),
        name="weight_grad_down",
    )(core, *activated, *grad_low, side)


def grad_up_kernel(counts, core_ref, *refs):
    micro = len(counts)
    hidden, inner, branch = (refs[at * micro : (at + 1) * micro] for at in range(3))
    keep_ref, send_ref, refs = refs[-2], refs[-1], refs[3 * micro : -2]
    mixed = []
    for size in counts:
        mixed.append(refs[:size])
        refs = refs[size:]
    last = pl.num_programs(0) - 1
    core = core_ref[0]

    @pl.when(pl.program_id(0) < last)
    def _():
        total = sum(tn(one[...], two[...]) for one, two in zip(hidden, inner))
        put_halves(core, keep_ref, send_ref, slice(None), total.astype(bf16))

    @pl.when(pl.program_id(0) == last)
    def _():
        total = sum(tn(join(one), two[...]) for one, two in zip(mixed, branch))
        put_halves(core, keep_ref, send_ref, slice(None), total.astype(bf16))


def weight_grad_up(core, hidden_low, grad_inner, attended, grad_branch):
    micro = len(hidden_low)
    block, width = hidden_low[0].shape
    tiles = grad_inner[0].shape[1] // width
    fixed = [pl.BlockSpec((block, width), lambda at, core_ref: (0, 0))] * micro
    parts = [part for one in attended for part in one]
    half = jax.ShapeDtypeStruct((2, width // 4, (tiles + 1) * width), bf16)
    return pl.pallas_call(
        functools.partial(grad_up_kernel, tuple(len(one) for one in attended)),
        out_shape=(half, half),
        grid_spec=pltpu.PrefetchScalarGridSpec(
            num_scalar_prefetch=1,
            grid=(tiles + 1,),
            in_specs=fixed
            + [pl.BlockSpec((block, width), lambda at, core_ref: (0, jnp.minimum(at, tiles - 1)))] * micro
            + fixed
            + [pl.BlockSpec(part.shape, lambda at, core_ref: (0, 0)) for part in parts],
            out_specs=[pl.BlockSpec((2, width // 4, width), lambda at, core_ref: (0, 0, at))] * 2,
        ),
        compiler_params=pltpu.CompilerParams(vmem_limit_bytes=VMEM_LIMIT),
        cost_estimate=pl.CostEstimate(flops=6_800_000_000, bytes_accessed=16_000_000, transcendentals=0),
        name="weight_grad_up",
    )(core, *hidden_low, *grad_inner, *grad_branch, *parts)


def permute(value, axis, pairs):
    return lax.ppermute(value, axis, pairs)


def swap_pairs(size, distance):
    return [(at, at ^ distance) for at in range(size)]


def even_pairs(size):
    return [(at, at ^ 1) for at in range(size)]


def odd_pairs(size):
    return [(at, min(max(((at + 1) ^ 1) - 1, 0), size - 1)) for at in range(size)]


def pick(array, index, axis=0):
    return lax.dynamic_index_in_dim(array, index, axis, keepdims=False)


def ordered(first_here, mine, other, axis=0):
    first = jnp.where(first_here, mine, other)
    second = jnp.where(first_here, other, mine)
    return jnp.concatenate([first, second], axis=axis)


def two_level(mesh_shape):
    return mesh_shape["replica"] == 4 and mesh_shape["fsdp"] == 2 and mesh_shape["seq"] == 4


def sync(*values):
    return lax.optimization_barrier(values)


class Fetch:
    def __init__(self, fast):
        self.fast = fast
        self.here = lax.axis_index("fsdp")
        self.spot = 2 * lax.axis_index("x") + lax.axis_index("core") if fast else None

    def quarter(self, shard):
        if not self.fast:
            return shard
        size = shard.shape[0] // 4
        return lax.dynamic_slice_in_dim(shard, self.spot * size, size, 0)

    def far(self, quarter):
        if not self.fast:
            return [lax.all_gather(quarter, "fsdp", axis=0, tiled=True)]
        return [permute(quarter, "fsdp", swap_pairs(2, 1))]

    def across(self, held):
        if not self.fast:
            return held
        return held + [permute(held[0], "x", swap_pairs(2, 1))]

    def beside(self, held):
        if not self.fast:
            return held
        pair = jnp.stack(held)
        return [pair, permute(pair, "core", swap_pairs(2, 1))]

    def half(self, shard):
        if not self.fast:
            return shard
        size = shard.shape[0] // 2
        return lax.dynamic_slice_in_dim(shard, lax.axis_index("core") * size, size, 0)

    def half_beside(self, held):
        if not self.fast:
            return held
        return held + [permute(held[0], "core", swap_pairs(2, 1))]

    def offsets(self, rows):
        size = rows // 4
        there = (1 - self.here) * rows
        return [self.here * rows], [there + (self.spot ^ flip) * size for flip in (0, 2, 1, 3)]

    def one_weight(self, shard, held):
        if not self.fast:
            return jnp.zeros((1,), jnp.int32), held
        mine, others = self.offsets(shard.shape[0])
        return jnp.stack(mine + others).astype(jnp.int32), [shard] + held

    def middle_weights(self, out_shard, up_shard, down_shard, shared, down):
        if not self.fast:
            width = shared[0].shape[0]
            return (jnp.zeros((3,), jnp.int32), shared[0][:, :width], shared[0][:, width:], [], down)
        mine, others = self.offsets(out_shard.shape[0])
        rows = down_shard.shape[0]
        core = lax.axis_index("core")
        there = (1 - self.here) * rows
        rest = [self.here * rows, there + core * (rows // 2), there + (1 - core) * (rows // 2)]
        offsets = jnp.stack(mine + mine + others + rest).astype(jnp.int32)
        return offsets, out_shard, up_shard, shared, [down_shard] + down

    def with_vectors(self, quarter, shards):
        if not self.fast:
            return quarter
        return jnp.concatenate([quarter, jnp.concatenate(shards).reshape(-1, quarter.shape[1])], axis=0)

    def without_vectors(self, held, shards):
        if not self.fast:
            return held, [lax.all_gather(shard, "fsdp", axis=0, tiled=True) for shard in shards]
        moved = held[0]
        rows = sum(shard.shape[0] for shard in shards) // moved.shape[1]
        far = moved[moved.shape[0] - rows :].reshape(-1)
        full, at = [], 0
        for shard in shards:
            size = shard.shape[0]
            full.append(ordered(self.here == 0, shard, far[at : at + size]))
            at += size
        return [moved[: moved.shape[0] - rows]], full


def halved(part):
    return part.reshape(2, part.shape[0] // 2, part.shape[1])


def low_sum(parts):
    if len(parts) == 1:
        return parts[0]
    return sum(part.astype(f32) for part in parts).astype(bf16)


def add_low(left, right):
    return low_sum([left, right])


class Chain:
    def __init__(self, fast, *parts):
        self.fast = fast
        self.name = None
        self.pair = list(parts)
        self.path, self.depth = [], []

    def views(self):
        found = []
        for part, depth in zip(self.pair, self.depth):
            for name, index in self.path[depth:]:
                part = pick(halved(part) if name == "z1" else part, index)
            found.append(part)
        return found

    def restart(self, *pair):
        self.pair, self.path, self.depth = list(pair), [], [0] * len(pair)

    def settle(self):
        name, pair = self.name, self.pair
        if name == "z3":
            return ordered(lax.axis_index("seq") % 2 == 0, *pair)
        if name == "spread_x":
            return both_ways(lax.axis_index("x") == 0, *pair)
        if name == "spread_core":
            return both_ways(lax.axis_index("core") == 0, *pair)
        return low_sum(self.views())

    def go(self, name):
        if not self.fast:
            return
        if name == "core":
            keep = [part[0] for part in self.pair]
            send = low_sum([part[1] for part in self.pair])
            moved = permute(send, "core", swap_pairs(2, 1))
            self.name = name
            self.restart(*[one.reshape(2, 2, one.shape[1] // 2, one.shape[2]) for one in keep + [moved]])
            return
        if name in ("z2", "z3", "spread_x", "spread_core"):
            held = self.settle()
            axis = {"z2": "seq", "z3": "seq", "spread_x": "x", "spread_core": "core"}[name]
            pairs = {"z2": swap_pairs(4, 2), "z3": swap_pairs(4, 1)}.get(name, swap_pairs(2, 1))
            self.name = name
            self.restart(held, permute(held, axis, pairs))
            return
        axis = {"y": "fsdp", "x": "x", "z1": "seq"}[name]
        here = lax.axis_index(axis)
        parts = self.views()
        if name == "z1":
            here = here % 2
            parts = [halved(part) for part in parts]
        send = low_sum([pick(part, 1 - here) for part in parts])
        moved = permute(send, axis, swap_pairs(4 if axis == "seq" else 2, 1))
        self.path.append((name, here))
        self.pair.append(moved)
        self.depth.append(len(self.path))
        self.name = name

    def final(self):
        if not self.fast:
            keep, send = (sum(part[at].astype(f32) for part in self.pair) for at in (0, 1))
            parts = jnp.stack([keep, send], axis=1).astype(bf16)
            share = lax.psum_scatter(
                parts.reshape(-1, parts.shape[3]), "fsdp", scatter_dimension=0, tiled=True
            )
            return lax.psum(share, ("replica", "seq")).astype(f32)
        full = self.settle()
        return full.reshape(-1, full.shape[-1]).astype(f32)


def both_ways(first_here, mine, other):
    return jnp.stack([jnp.where(first_here, mine, other), jnp.where(first_here, other, mine)])


def settle_all(chains, *values):
    pairs, *values = sync([chain.pair for chain in chains], *values)
    for chain, pair in zip(chains, pairs):
        chain.pair = pair
    return values


def body(
    fast,
    tokens,
    segment_ids,
    joined_weight,
    query_bias,
    value_bias,
    out_weight,
    out_bias,
    norm_gain,
    norm_shift,
    up_weight,
    up_bias,
    down_weight,
    down_bias,
    final_gain,
    final_shift,
    cotangent,
):
    micro, block, width = tokens.shape[1:]
    length = segment_ids.shape[-1]
    size = lax.axis_size("seq")
    place = lax.axis_index("seq")
    hops = (length // 2 - 2) // block + 1
    assert size % 2 == 0 and hops in (1, 2)
    count = 2 * hops + 1
    inner_width = up_weight.shape[1]
    all_pairs = width // PAIR
    half_pairs = all_pairs // 2
    spans = [(0, half_pairs), (half_pairs, half_pairs)]
    fetch = Fetch(fast)

    def masks_of(ids):
        ends = ((0, 0), (hops * block, 0)), ((0, 0), (0, hops * block + TK_FWD - ALIGN))
        padded = jnp.pad(jnp.pad(ids, ends[0], constant_values=-1), ends[1], constant_values=1000)
        near = lax.dynamic_slice_in_dim(padded, place * block, count * block + TK_FWD - ALIGN, 1)
        rows = near[:, hops * block : (hops + 1) * block]
        low = jnp.sum(near < rows[:, :1], axis=1)
        high = jnp.sum(near <= rows[:, -1:], axis=1)
        bounds = jnp.stack([low, high, jnp.broadcast_to(1 - 2 * (place % 2), low.shape)], axis=1)
        segq = jnp.broadcast_to(rows[:, None, :], (micro, 8, block))
        segk = jnp.broadcast_to(near[:, :, None], near.shape + (128,))
        return bounds.astype(jnp.int32).reshape(-1), segq, segk

    def mask_at(batch):
        return (batch,) + tuple(masks)

    own = [tokens[0, batch] for batch in range(micro)]
    moves = [None] * micro
    small_shards = [
        query_bias,
        value_bias,
        out_bias,
        norm_gain,
        norm_shift,
        down_bias,
        final_gain,
        final_shift,
        up_bias,
    ]
    def hop_out(batch, step):
        if step == 0:
            one, two = own[batch], own[batch]
            moves[batch] = [one, permute(one, "seq", even_pairs(size)), permute(two, "seq", odd_pairs(size))]
        else:
            _, even, odd = moves[batch]
            moves[batch] = moves[batch] + [
                permute(even, "seq", odd_pairs(size)),
                permute(odd, "seq", even_pairs(size)),
            ]

    joined = fetch.far(fetch.with_vectors(fetch.quarter(joined_weight), small_shards))
    hop_out(0, 0)
    quarters = [
        jnp.concatenate([fetch.quarter(out_weight), fetch.quarter(up_weight)], axis=1),
        fetch.half(down_weight),
    ]
    shared = fetch.far(quarters[0])
    joined, moves[0], ids, quarters[1] = sync(joined, moves[0], segment_ids, quarters[1])
    joined, vectors = fetch.without_vectors(joined, small_shards)
    joined = fetch.across(joined)
    for step in range(1, hops):
        hop_out(0, step)
    joined, ids, vectors = sync(joined, ids, vectors)
    joined = fetch.beside(joined)
    masks = masks_of(ids[0])
    biases = jnp.pad(jnp.stack(vectors[:2]).astype(f32), ((0, 6), (0, 0)))
    rows_six = jnp.pad(jnp.stack(vectors[2:8]).astype(f32), ((0, 2), (0, 0)))
    up_row = jnp.pad(vectors[8].astype(f32)[None, :], ((0, 7), (0, 0)))
    shared, quarters[1] = sync(shared, quarters[1])
    shared = fetch.across(shared)
    down = fetch.far(quarters[1])
    moves[0], joined, own[1:], biases, rows_six, up_row, masks = sync(
        moves[0], joined, own[1:], biases, rows_six, up_row, masks
    )

    attended = [[] for _ in range(micro)]

    def window(batch):
        one, even, odd, *far = moves[batch]
        return [far[0], odd, one, even, far[1]] if far else [odd, one, even]

    windows = [window(0)] + [None] * (micro - 1)
    weight = fetch.one_weight(joined_weight, joined)

    if micro > 1:
        hop_out(1, 0)
    attended[0].append(tuple(attend_forward((0, all_pairs), mask_at(0), windows[0], weight, biases)))
    attended[0], shared, down, masks, windows[0], moves[1:2] = sync(
        attended[0], shared, down, masks, windows[0], moves[1:2]
    )
    shared = fetch.beside(shared)
    down = fetch.half_beside(down)
    attended[0], shared, down, own = sync(attended[0], shared, down, own)
    for step in range(1, hops if micro > 1 else 0):
        hop_out(1, step)
    middle_weights = fetch.middle_weights(out_weight, up_weight, down_weight, shared, down)

    middles = []
    for batch in range(micro):
        later = batch + 1
        if batch > 0:
            windows[batch] = window(batch)
            if later < micro:
                hop_out(later, 0)
            attended[batch].append(
                tuple(attend_forward((0, all_pairs), mask_at(batch), windows[batch], weight, biases))
            )
            if later < micro:
                attended[batch], moves[later] = sync(attended[batch], moves[later])
        if batch > 0 and later < micro:
            for step in range(1, hops):
                hop_out(later, step)
        middles.append(
            middle(
                [one[0] for one in attended[batch]],
                own[batch],
                cotangent[0, batch],
                middle_weights,
                rows_six,
                up_row,
            )
        )
        if later < micro:
            middles[-1], masks, moves[later] = sync(middles[-1], masks, moves[later])
        else:
            middles[-1], masks = sync(middles[-1], masks)

    core = lax.axis_index("core") if fast else jnp.zeros((), jnp.int32)
    core = core.astype(jnp.int32).reshape(1)
    outs = list(zip(*middles))
    small = sum(outs[8])
    grad_upb = sum(outs[9])
    half = width // 2
    gap = inner_width // 2 - half
    spread = jnp.pad(small[:6].reshape(6, 2, half), ((0, 0), (0, 0), (0, gap))).reshape(6, inner_width)
    side = jnp.concatenate([grad_upb[:1], spread, jnp.zeros((1, inner_width), f32)], axis=0)
    down = Chain(fast, weight_grad_down(core, outs[6], outs[7], side))
    up_ins = (outs[4], outs[5], [[part[0] for part in one] for one in attended], outs[3])
    (up_ins,) = settle_all([down], up_ins)
    down.go("core")
    up = Chain(fast, weight_grad_up(core, *up_ins))
    (masks,) = settle_all([down, up], list(masks))

    backs = [None] * micro
    coming = [None] * micro
    joined_sums = [[], []]
    last = micro - 1

    def run_back(which, batch, chains, moving=()):
        before = [outs[1][batch]] if which == 0 else backs[batch]
        *parts, keep, send = attend_backward(
            core, spans[which], mask_at(batch), windows[batch], weight, biases, attended[batch], outs[2][batch], before
        )
        moved = [coming[at] for at in moving]
        backs[batch], grad_joined, masks[:], moved = settle_all(chains, parts, (keep, send), list(masks), moved)
        for at, one in zip(moving, moved):
            coming[at] = one
        joined_sums[which].append(grad_joined)

    def total_of(which):
        return Chain(fast, *joined_sums[which])

    def hop_back(batch, step):
        parts = backs[batch]
        if step == 0 and hops > 1:
            coming[batch] = [
                permute(parts[hops + 2], "seq", even_pairs(size)),
                permute(parts[hops - 2], "seq", odd_pairs(size)),
            ]
            return
        odd, even = parts[hops - 1], parts[hops + 1]
        if hops > 1:
            odd, even = add_low(odd, coming[batch][0]), add_low(even, coming[batch][1])
        coming[batch] = [permute(odd, "seq", odd_pairs(size)), permute(even, "seq", even_pairs(size))]

    down.go("y")
    up.go("core")
    run_back(0, 0, [up, down])
    down.go("x")
    up.go("y")
    run_back(1, 0, [down])
    middle_steps = [
        ([(down, "z1")], [down, up]),
        ([(down, "z2"), (up, "x")], [down, up]),
        ([(down, "z3"), (up, "z1")], [down, up]),
        ([(down, "spread_x"), (up, "z2")], [down, up]),
    ]
    for batch in range(1, micro):
        for which in (0, 1):
            begin, end = middle_steps.pop(0) if middle_steps else ([], [])
            for chain, name in begin:
                chain.go(name)
            moving = []
            if which == 0:
                hop_back(batch - 1, 0)
                moving = [batch - 1]
            else:
                for step in range(1, hops):
                    hop_back(batch - 1, step)
                moving = [batch - 1]
            if batch == last and which == 1:
                joined_one = total_of(0)
                joined_one.go("core")
                end = end + [joined_one]
            run_back(which, batch, end, moving)

    joined_two = total_of(1)
    joined_two.go("core")
    joined_one.go("y")
    hop_back(last, 0)
    (backs,) = settle_all([joined_two], backs)
    joined_two.go("y")
    up.go("z3")
    down.go("spread_core")
    coming, backs = settle_all([joined_one, down], coming, backs)
    joined_one.go("x")
    for step in range(1, hops):
        hop_back(last, step)
    settle_all([joined_two, joined_one, up])
    joined_two.go("x")
    joined_one.go("z1")
    up.go("spread_x")
    (coming,) = settle_all([joined_two, joined_one], coming)
    joined_two.go("z1")
    joined_one.go("z2")
    settle_all([joined_two, joined_one, up])
    joined_two.go("z2")
    joined_one.go("z3")
    up.go("spread_core")
    settle_all([joined_two, joined_one])
    joined_two.go("z3")
    joined_one.go("spread_x")
    settle_all([joined_two, joined_one])
    joined_two.go("spread_x")
    joined_one.go("spread_core")
    settle_all([joined_two])
    joined_two.go("spread_core")

    final_down = down.final()
    final_up = up.final()
    final_up, final_out = final_up[:, :inner_width], final_up[:, inner_width:]
    final_a, final_b = joined_one.final(), joined_two.final()
    grad_tokens = []
    for batch in range(micro):
        total = backs[batch][hops] + sum(one.astype(f32) for one in coming[batch])
        grad_tokens.append(total.astype(bf16))
    low, high = spans[0][1] * PAIR, spans[1][1] * PAIR
    final_joined = jnp.concatenate(
        [
            part
            for at in range(3)
            for part in (final_a[:, at * low : (at + 1) * low], final_b[:, at * high : (at + 1) * high])
        ],
        axis=1,
    )
    bias_sums = final_a[:, 3 * low : 3 * low + 2] + final_b[:, 3 * high : 3 * high + 2]
    if fast:
        own_rows = width // lax.axis_size("fsdp")
        smalls = [final_down[:own_rows, width + 1 + at] for at in range(6)]
    else:
        smalls = [
            lax.psum_scatter(lax.psum(small[at], ("replica", "seq")), "fsdp", scatter_dimension=0, tiled=True)
            for at in range(6)
        ]
    return (
        jnp.stack(outs[0], axis=0)[None],
        jnp.stack(grad_tokens, axis=0)[None],
        final_joined,
        bias_sums[:, 0],
        bias_sums[:, 1],
        final_out,
        smalls[0],
        smalls[1],
        smalls[2],
        final_up,
        final_down[:, width],
        final_down[:, :width],
        smalls[3],
        smalls[4],
        smalls[5],
    )


def solution(mesh):
    fast = two_level(dict(mesh.shape))
    groups = ("replica", "fsdp")
    if fast:
        mesh = jax.sharding.Mesh(mesh.devices.reshape(2, 2, 2, 4), ("x", "core", "fsdp", "seq"))
        groups = ("x", "core", "fsdp")
    rows = P(groups, None, "seq", None)
    matrix, vector = P("fsdp", None), P("fsdp")
    in_specs = (
        rows,
        P(groups, None, None),
        matrix,
        vector,
        vector,
        matrix,
        vector,
        vector,
        vector,
        matrix,
        vector,
        matrix,
        vector,
        vector,
        vector,
        rows,
    )
    out_specs = (
        rows,
        rows,
        matrix,
        vector,
        vector,
        matrix,
        vector,
        vector,
        vector,
        matrix,
        vector,
        matrix,
        vector,
        vector,
        vector,
    )
    return jax.shard_map(
        functools.partial(body, fast),
        mesh=mesh,
        in_specs=in_specs,
        out_specs=out_specs,
        check_vma=False,
    )
```

```python
import functools
import jax
import jax.numpy as jnp
from jax import lax
from jax.experimental import pallas as pl
from jax.experimental.pallas import tpu as pltpu
from jax.sharding import PartitionSpec as P

HEADS = 12
HEAD_DIM = 64
PAIR = 2 * HEAD_DIM
epsilon = 1e-05
masked_score = -1e30
scale = HEAD_DIM ** (-0.5)
TK_FWD = 384
TK_BWD = 384
ALIGN = 128
ROW_STEP = 16
VMEM_LIMIT = 62 * 1024 * 1024
FF_TILES = 4
f32 = jnp.float32
bf16 = jnp.bfloat16


def nt(left, right):
    return lax.dot_general(left, right, (((1,), (1,)), ((), ())), preferred_element_type=f32)


def tn(left, right):
    return lax.dot_general(left, right, (((0,), (0,)), ((), ())), preferred_element_type=f32)


def nn(left, right):
    return lax.dot_general(left, right, (((1,), (0,)), ((), ())), preferred_element_type=f32)


def stack_heads(pair):
    lane = lax.broadcasted_iota(jnp.int32, pair.shape, 1)
    zero = jnp.zeros_like(pair)
    return jnp.concatenate(
        [jnp.where(lane < HEAD_DIM, pair, zero), jnp.where(lane < HEAD_DIM, zero, pair)], axis=0
    )


def unstack_heads(rows):
    half = rows.shape[0] // 2
    lane = lax.broadcasted_iota(jnp.int32, (half, rows.shape[1]), 1)
    return jnp.where(lane < HEAD_DIM, rows[:half], rows[half:])


def split_pieces(refs):
    pieces = []
    for ref in refs:
        if len(ref.shape) == 2:
            pieces.append(ref)
        else:
            pieces.extend(ref.at[at] for at in range(ref.shape[0]))
    return pieces


def count_pieces(arrays):
    return sum(1 if len(one.shape) == 2 else one.shape[0] for one in arrays)


def start_columns(offsets, piece_refs, full_s, sems, width, at_col, size_col):
    copies = []
    for at, piece in enumerate(split_pieces(piece_refs)):
        size = piece.shape[0]
        row = pl.multiple_of(offsets[at], ROW_STEP)
        for part in range(3):
            copy = pltpu.make_async_copy(
                piece.at[:, pl.ds(part * width + at_col, size_col)],
                full_s.at[pl.ds(row, size), pl.ds(part * size_col, size_col)],
                sems.at[at, part],
            )
            copy.start()
            copies.append(copy)
    return copies


def wait_all(copies):
    for copy in copies:
        copy.wait()


def first_row(bounds, at, count, block):
    middle = count // 2
    return pl.multiple_of((middle + bounds[2] * (at - middle)) * block, ALIGN)


def reached(bounds, at, count, block):
    row = first_row(bounds, at, count, block)
    return (bounds[1] > row) & (bounds[0] < row + block)


def block_copy(bounds, x_refs, x_s, sems, at):
    block = x_refs[at].shape[0]
    row = first_row(bounds, at, len(x_refs), block)
    return pltpu.make_async_copy(x_refs[at], x_s.at[pl.ds(row, block), :], sems.at[at])


def fetch_window(bounds, x_refs, x_s, sems):
    for at in range(len(x_refs)):

        @pl.when(reached(bounds, at, len(x_refs), x_refs[at].shape[0]))
        def _():
            block_copy(bounds, x_refs, x_s, sems, at).start()


def project_window(bounds, x_refs, x_s, sems, w_ref, bias_ref, cols, k_s, v_s, tail):
    block = x_refs[0].shape[0]
    width = k_s.shape[1]
    for at in range(len(x_refs)):
        rows = pl.ds(first_row(bounds, at, len(x_refs), block), block)
        active = reached(bounds, at, len(x_refs), block)

        @pl.when(active)
        def _():
            block_copy(bounds, x_refs, x_s, sems, at).wait()
            x = x_s[rows, :]
            both = nn(x, w_ref[:, width:])
            k_s[rows, :] = both[:, :width].astype(bf16)
            v_s[rows, :] = (both[:, width:] + bias_ref[1:2, cols]).astype(bf16)

        @pl.when(jnp.logical_not(active))
        def _():
            k_s[rows, :] = jnp.zeros((block, width), bf16)
            v_s[rows, :] = jnp.zeros((block, width), bf16)

    end = len(x_refs) * block
    k_s[end:, :] = jnp.zeros((tail, width), bf16)
    v_s[end:, :] = jnp.zeros((tail, width), bf16)


def tile_range(bounds, tk):
    low = bounds[0]
    high = bounds[1]
    start = (low // ALIGN) * ALIGN
    return start, (high - start + tk - 1) // tk


def project_queries(x, w_ref, bias_ref, cols, q_s, qq_s):
    width = q_s.shape[1]
    q = nn(x, w_ref[:, :width]) + bias_ref[0:1, cols]
    q_s[...] = q.astype(bf16) * jnp.asarray(scale, bf16)
    for pair in range(width // PAIR):
        here = slice(pair * PAIR, (pair + 1) * PAIR)
        qq_s[:, here] = stack_heads(q_s[:, here])


def forward_kernel(batch, hops, pieces, first, all_bounds, offsets, *refs):
    bounds = [all_bounds[3 * batch + at] for at in range(3)]
    count = 2 * hops + 1
    x_refs = refs[:count]
    w_refs, refs = refs[count : count + pieces], refs[count + pieces :]
    bias_ref, segq_ref, segk_any, o_ref, lse_ref = refs[:5]
    segk_ref, seg_sem, x_s, w_ref, q_s, qq_s, k_s, v_s, top_s, sum_s, acc_s, x_sems, sems = refs[5:]
    seg_copy = pltpu.make_async_copy(segk_any.at[batch], segk_ref, seg_sem)
    seg_copy.start()
    block, full_width = x_refs[0].shape
    width = o_ref.shape[1]
    own_rows = slice(hops * block, (hops + 1) * block)
    tk = TK_FWD
    pairs = width // PAIR
    cols_all = slice(first * PAIR, first * PAIR + width)
    copies = start_columns(offsets, w_refs, w_ref, sems, full_width, first * PAIR, width)
    fetch_window(bounds, x_refs, x_s, x_sems)
    wait_all(copies)
    project_window(bounds, x_refs, x_s, x_sems, w_ref, bias_ref, cols_all, k_s, v_s, tk - ALIGN)
    project_queries(x_s[own_rows, :], w_ref, bias_ref, cols_all, q_s, qq_s)
    start, steps = tile_range(bounds, tk)
    seg_copy.wait()
    segq = segq_ref[batch, 0:1, :]
    segq = jnp.concatenate([segq, segq], axis=1)
    top_s[...] = jnp.full(top_s.shape, masked_score, f32)
    sum_s[...] = jnp.ones(sum_s.shape, f32)
    sum_s[:pairs, :] = jnp.zeros((pairs, sum_s.shape[1]), f32)
    acc_s[...] = jnp.zeros(acc_s.shape, f32)

    @pl.loop(0, steps)
    def _(at):
        here = pl.ds(pl.multiple_of(start + at * tk, ALIGN), tk)
        allowed = segk_ref[here, 0:1] == segq
        for pair in range(pairs):
            cols = slice(pair * PAIR, (pair + 1) * PAIR)
            one = slice(pair, pair + 1)
            scores = nt(k_s[here, cols], qq_s[:, cols])
            scores = jnp.where(allowed, scores, masked_score)
            top = top_s[one, :]
            new_top = jnp.maximum(top, jnp.max(scores, axis=0, keepdims=True))
            fade = jnp.exp(top - new_top)
            weights = jnp.exp(scores - new_top)
            top_s[one, :] = new_top
            sum_s[one, :] = sum_s[one, :] * fade + jnp.sum(weights, axis=0, keepdims=True)
            acc_s[pair] = acc_s[pair] * fade + tn(v_s[here, cols], weights.astype(bf16))

    lse_ref[...] = top_s[...] + jnp.log(sum_s[...])
    for pair in range(pairs):
        cols = slice(pair * PAIR, (pair + 1) * PAIR)
        mixed = acc_s[pair] / sum_s[pair : pair + 1, :]
        o_ref[:, cols] = unstack_heads(mixed.T).astype(bf16)


def backward_kernel(batch, hops, pieces, prev, first, skip, all_bounds, offsets, core_ref, *refs):
    bounds = [all_bounds[3 * batch + at] for at in range(3)]
    count = 2 * hops + 1
    x_refs = refs[:count]
    w_refs, refs = refs[count : count + pieces], refs[count + pieces :]
    bias_ref, segq_ref, segk_any, o_ref, lse_ref, do_ref = refs[:6]
    prev_refs, refs = refs[6 : 6 + prev], refs[6 + prev :]
    out_refs, refs = refs[:count], refs[count:]
    keep_ref, send_ref, segk_ref, seg_sem, *refs = refs
    seg_copy = pltpu.make_async_copy(segk_any.at[batch], segk_ref, seg_sem)
    seg_copy.start()
    x_s, p_s, own_s, w_ref, q_s, qq_s, gg_s, k_s, v_s, dk_s, dv_s, dw_s, stat_s, acc_s, db_s = refs[:15]
    x_sems, p_sems, o_sems, sems = refs[15:]
    block, full_width = x_refs[0].shape
    width = q_s.shape[1]
    tk = TK_BWD
    pairs = width // PAIR
    cols_all = slice(first * PAIR, first * PAIR + width)
    own_rows = slice(hops * block, (hops + 1) * block)
    others = [at for at in range(count) if at != hops]
    copies = start_columns(offsets, w_refs, w_ref, sems, full_width, first * PAIR, width)
    fetch_window(bounds, x_refs, x_s, x_sems)
    own_copy = pltpu.make_async_copy(prev_refs[hops if prev > 1 else 0], own_s, p_sems.at[hops])
    own_copy.start()

    def stage(at):
        return p_s.at[pl.ds(at * block, block), :]

    def prev_copy(at):
        return pltpu.make_async_copy(prev_refs[at], stage(at), p_sems.at[at])

    def out_copy(at):
        return pltpu.make_async_copy(own_s if at == hops else stage(at), out_refs[at], o_sems.at[at])

    for at in others:
        active = reached(bounds, at, count, block)
        if prev > 1:

            @pl.when(active)
            def _():
                prev_copy(at).start()

        else:

            @pl.when(jnp.logical_not(active))
            def _():
                p_s[at * block : (at + 1) * block, :] = jnp.zeros((block, full_width), bf16)
                out_copy(at).start()

    dk_s[...] = jnp.zeros(dk_s.shape, f32)
    dv_s[...] = jnp.zeros(dv_s.shape, f32)
    acc_s[...] = jnp.zeros(acc_s.shape, f32)
    for pair in range(pairs):
        cols = slice(pair * PAIR, (pair + 1) * PAIR)
        far = slice((first + pair) * PAIR, (first + pair + 1) * PAIR)
        theirs = slice((skip + pair) * PAIR, (skip + pair + 1) * PAIR)
        grads = stack_heads(do_ref[:, far])
        gg_s[:, cols] = grads
        mixed = o_ref[:, theirs].astype(f32)
        product = grads.astype(f32) * jnp.concatenate([mixed, mixed], axis=0)
        stat_s[pair : pair + 1, :] = jnp.sum(product.T, axis=0, keepdims=True)
    wait_all(copies)
    project_window(bounds, x_refs, x_s, x_sems, w_ref, bias_ref, cols_all, k_s, v_s, tk - ALIGN)
    project_queries(x_s[own_rows, :], w_ref, bias_ref, cols_all, q_s, qq_s)
    start, steps = tile_range(bounds, tk)
    seg_copy.wait()
    segq = segq_ref[batch, 0:1, :]
    segq = jnp.concatenate([segq, segq], axis=1)

    @pl.loop(0, steps)
    def _(at):
        here = pl.ds(pl.multiple_of(start + at * tk, ALIGN), tk)
        allowed = segk_ref[here, 0:1] == segq
        for pair in range(pairs):
            cols = slice(pair * PAIR, (pair + 1) * PAIR)
            keys = k_s[here, cols]
            queries = qq_s[:, cols]
            grads = gg_s[:, cols]
            scores = nt(keys, queries)
            scores = jnp.where(allowed, scores, masked_score)
            weights = jnp.exp(scores - lse_ref[skip + pair : skip + pair + 1, :])
            grad_weights = nt(v_s[here, cols], grads)
            grad_scores = (weights * (grad_weights - stat_s[pair : pair + 1, :])).astype(bf16)
            dv_s[here, cols] += nn(weights.astype(bf16), grads)
            dk_s[here, cols] += nn(grad_scores, queries)
            acc_s[pair] += tn(keys, grad_scores)

    for pair in range(pairs):
        cols = slice(pair * PAIR, (pair + 1) * PAIR)
        q_s[:, cols] = (unstack_heads(acc_s[pair].T) * scale).astype(bf16)
    dq = q_s[...]
    db_s[...] = jnp.zeros(db_s.shape, f32)
    db_s[0:1, cols_all] = jnp.sum(dq.astype(f32), axis=0, keepdims=True)

    def rows_of(at):
        rows = pl.ds(first_row(bounds, at, count, block), block)
        dk = dk_s[rows, :].astype(bf16)
        dv = dv_s[rows, :].astype(bf16)
        db_s[1:2, cols_all] += jnp.sum(dv.astype(f32), axis=0, keepdims=True)
        return [dk, dv]

    grads = jnp.concatenate([dq] + rows_of(hops), axis=1)
    own_copy.wait()
    own_s[...] += nt(grads, w_ref[...])
    out_copy(hops).start()
    dw_s[...] = tn(x_s[own_rows, :], grads)
    for at in others:

        @pl.when(reached(bounds, at, count, block))
        def _():
            rows = slice(at * block, (at + 1) * block)
            grads = jnp.concatenate(rows_of(at), axis=1)
            back = nt(grads, w_ref[:, width:])
            if prev > 1:
                prev_copy(at).wait()
                back = back + p_s[rows, :].astype(f32)
            p_s[rows, :] = back.astype(bf16)
            out_copy(at).start()
            x = x_s[pl.ds(first_row(bounds, at, count, block), block), :]
            dw_s[:, width:] += tn(x, grads)

    put_halves(core_ref[0], keep_ref, send_ref, slice(0, 3 * width), dw_s[...].astype(bf16))
    side = jnp.concatenate([db_s[...], jnp.zeros((120, full_width), f32)], axis=0).T
    put_halves(core_ref[0], keep_ref, send_ref, slice(3 * width, 3 * width + 128), side.astype(bf16))
    out_copy(hops).wait()
    for at in others:
        if prev > 1:

            @pl.when(reached(bounds, at, count, block))
            def _():
                out_copy(at).wait()

        else:
            out_copy(at).wait()


def whole():
    return pl.BlockSpec(memory_space=pltpu.VMEM)


def smem():
    return pl.BlockSpec(memory_space=pltpu.SMEM)


def raw():
    return pl.BlockSpec(memory_space=pl.ANY)


def attend_forward(span, mask, window, weight, biases):
    batch, bounds, segq, segk = mask
    offsets, pieces = weight
    first, pairs = span
    count = len(window)
    block, full_width = window[0].shape
    width = pairs * PAIR
    padded = count * block + TK_FWD - ALIGN
    return pl.pallas_call(
        functools.partial(forward_kernel, batch, count // 2, len(pieces), first),
        out_shape=(
            jax.ShapeDtypeStruct((block, width), bf16),
            jax.ShapeDtypeStruct((8, 2 * block), f32),
        ),
        in_specs=[smem()] * 2
        + [raw()] * (count + len(pieces))
        + [whole(), whole(), raw()],
        out_specs=(whole(), whole()),
        scratch_shapes=[
            pltpu.VMEM(segk.shape[1:], jnp.int32),
            pltpu.SemaphoreType.DMA,
            pltpu.VMEM((count * block, full_width), bf16),
            pltpu.VMEM((full_width, 3 * width), bf16),
            pltpu.VMEM((block, width), bf16),
            pltpu.VMEM((2 * block, width), bf16),
            pltpu.VMEM((padded, width), bf16),
            pltpu.VMEM((padded, width), bf16),
            pltpu.VMEM((8, 2 * block), f32),
            pltpu.VMEM((8, 2 * block), f32),
            pltpu.VMEM((pairs, PAIR, 2 * block), f32),
            pltpu.SemaphoreType.DMA((count,)),
            pltpu.SemaphoreType.DMA((count_pieces(pieces), 3)),
        ],
        compiler_params=pltpu.CompilerParams(vmem_limit_bytes=VMEM_LIMIT),
        cost_estimate=pl.CostEstimate(
            flops=2_500_000_000 * pairs, bytes_accessed=8_000_000, transcendentals=4_000_000
        ),
        name="attend_forward",
    )(bounds, offsets, *window, *pieces, biases, segq, segk)


def attend_backward(core, span, mask, window, weight, biases, attended, grad, before):
    batch, bounds, segq, segk = mask
    offsets, pieces = weight
    first, pairs = span
    count = len(window)
    block, full_width = window[0].shape
    width = pairs * PAIR
    hops = count // 2
    padded = count * block + TK_BWD - ALIGN
    per_part = full_width // PAIR // len(attended)
    mixed, lse = attended[first // per_part]
    at = first // per_part * per_part
    outs = [
        jax.ShapeDtypeStruct((block, full_width), f32 if at == hops else bf16) for at in range(count)
    ]
    return pl.pallas_call(
        functools.partial(backward_kernel, batch, hops, len(pieces), len(before), first, first - at),
        out_shape=(
            *outs,
            jax.ShapeDtypeStruct((2, full_width // 4, 3 * width + 128), bf16),
            jax.ShapeDtypeStruct((2, full_width // 4, 3 * width + 128), bf16),
        ),
        in_specs=[smem()] * 3
        + [raw()] * (count + len(pieces))
        + [whole(), whole(), raw()]
        + [whole()] * 3
        + [raw()] * len(before),
        out_specs=(raw(),) * count + (whole(),) * 2,
        input_output_aliases=(
            {9 + count + len(pieces) + at: at for at in range(count)} if len(before) > 1 else {}
        ),
        scratch_shapes=[
            pltpu.VMEM(segk.shape[1:], jnp.int32),
            pltpu.SemaphoreType.DMA,
            pltpu.VMEM((count * block, full_width), bf16),
            pltpu.VMEM((count * block, full_width), bf16),
            pltpu.VMEM((block, full_width), f32),
            pltpu.VMEM((full_width, 3 * width), bf16),
            pltpu.VMEM((block, width), bf16),
            pltpu.VMEM((2 * block, width), bf16),
            pltpu.VMEM((2 * block, width), bf16),
            pltpu.VMEM((padded, width), bf16),
            pltpu.VMEM((padded, width), bf16),
            pltpu.VMEM((padded, width), f32),
            pltpu.VMEM((padded, width), f32),
            pltpu.VMEM((full_width, 3 * width), f32),
            pltpu.VMEM((8, 2 * block), f32),
            pltpu.VMEM((pairs, PAIR, 2 * block), f32),
            pltpu.VMEM((8, full_width), f32),
            pltpu.SemaphoreType.DMA((count,)),
            pltpu.SemaphoreType.DMA((count,)),
            pltpu.SemaphoreType.DMA((count,)),
            pltpu.SemaphoreType.DMA((count_pieces(pieces), 3)),
        ],
        compiler_params=pltpu.CompilerParams(vmem_limit_bytes=VMEM_LIMIT),
        cost_estimate=pl.CostEstimate(
            flops=5_000_000_000 * pairs, bytes_accessed=20_000_000, transcendentals=4_000_000
        ),
        name="attend_backward",
    )(bounds, offsets, core, *window, *pieces, biases, segq, segk, mixed, lse, grad, *before)


def join(refs):
    if len(refs) == 1:
        return refs[0][...]
    return jnp.concatenate([ref[...] for ref in refs], axis=1)


def middle_kernel(
    counts, offsets, tokens_ref, cot_ref, vec_ref, upb_ref, *refs
):
    n_mixed, n_shared, n_down = counts
    mixed_refs, refs = refs[:n_mixed], refs[n_mixed:]
    out_own, up_own, refs = refs[0], refs[1], refs[2:]
    shared, down_p = split_pieces(refs[:n_shared]), split_pieces(refs[n_shared : n_shared + n_down])
    refs = refs[n_shared + n_down :]
    n_shared = len(shared)
    (
        result_ref, one_ref, mixed_ref, branch_ref, hidden_ref, inner_ref, act_ref, two_ref,
        small_ref, gupb_ref,
    ) = refs[:10]
    wo_s, up_s, down_s, slope_s, act_s, inner_s, leave_sems, sems = refs[10:]
    width = wo_s.shape[1]
    leaving = []
    out_copies, up_copies, down_copies = [], [], []

    def begin(copies, at, source, target):
        row = pl.multiple_of(offsets[at], ROW_STEP)
        copy = pltpu.make_async_copy(
            source, target.at[pl.ds(row, source.shape[0]), :], sems.at[at, len(copies) % 2]
        )
        copy.start()
        copies.append(copy)

    begin(out_copies, 0, out_own, wo_s)
    for at, piece in enumerate(shared):
        row = pl.multiple_of(offsets[2 + at], ROW_STEP)
        copy = pltpu.make_async_copy(
            piece.at[:, pl.ds(0, width)], wo_s.at[pl.ds(row, piece.shape[0]), :], sems.at[2 + at, 0]
        )
        copy.start()
        out_copies.append(copy)
    begin(up_copies, 1, up_own, up_s)
    for at, piece in enumerate(shared):
        row = pl.multiple_of(offsets[2 + at], ROW_STEP)
        copy = pltpu.make_async_copy(
            piece.at[:, pl.ds(width, up_s.shape[1])],
            up_s.at[pl.ds(row, piece.shape[0]), :],
            sems.at[2 + at, 1],
        )
        copy.start()
        up_copies.append(copy)
    for at, piece in enumerate(down_p):
        row = pl.multiple_of(offsets[2 + n_shared + at], ROW_STEP)
        copy = pltpu.make_async_copy(
            piece, down_s.at[pl.ds(row, piece.shape[0]), :], sems.at[2 + n_shared + at, 0]
        )
        copy.start()
        down_copies.append(copy)
    inner_width = up_s.shape[1]
    tile = inner_width // FF_TILES
    out_bias, norm_gain, norm_shift = vec_ref[0:1, :], vec_ref[1:2, :], vec_ref[2:3, :]
    down_bias, final_gain, final_shift = vec_ref[3:4, :], vec_ref[4:5, :], vec_ref[5:6, :]
    wait_all(out_copies)
    values = tokens_ref[...].astype(f32) + (nn(join(mixed_refs), wo_s[...]) + out_bias)
    centered = values - jnp.mean(values, axis=1, keepdims=True)
    inverse_one = lax.rsqrt(jnp.mean(centered * centered, axis=1, keepdims=True) + epsilon)
    normed_one = centered * inverse_one
    hidden = normed_one * norm_gain + norm_shift
    hidden_low = hidden.astype(bf16)
    hidden_ref[...] = hidden_low
    wait_all(up_copies)
    def up_tile(at):
        cols = slice(at * tile, (at + 1) * tile)
        return nn(hidden_low, up_s[:, cols]) + upb_ref[0:1, cols]

    branch_two = None
    inner = up_tile(0)
    wait_all(down_copies)
    for at in range(FF_TILES):
        cols = slice(at * tile, (at + 1) * tile)
        normal = 0.5 * (1.0 + lax.erf(inner * 0.7071067811865476))
        density = jnp.exp(-0.5 * inner * inner) * 0.3989422804014327
        slope_s[:, cols] = normal + inner * density
        activated = (inner * normal).astype(bf16)
        act_s[:, cols] = activated
        leaving.append(pltpu.make_async_copy(act_s.at[:, cols], act_ref.at[:, cols], leave_sems.at[0, at]))
        leaving[-1].start()
        term = nn(activated, down_s[cols, :])
        branch_two = term if branch_two is None else branch_two + term
        if at + 1 < FF_TILES:
            inner = up_tile(at + 1)
    values = hidden + (branch_two + down_bias)
    centered = values - jnp.mean(values, axis=1, keepdims=True)
    inverse_two = lax.rsqrt(jnp.mean(centered * centered, axis=1, keepdims=True) + epsilon)
    normed_two = centered * inverse_two
    result_ref[...] = (normed_two * final_gain + final_shift).astype(bf16)
    cot = cot_ref[...].astype(f32)
    small_ref[4:5, :] = jnp.sum(cot * normed_two, axis=0, keepdims=True)
    small_ref[5:6, :] = jnp.sum(cot, axis=0, keepdims=True)
    scaled = cot * final_gain
    first = jnp.mean(scaled, axis=1, keepdims=True)
    second = jnp.mean(scaled * normed_two, axis=1, keepdims=True)
    grad_two = inverse_two * (scaled - first - normed_two * second)
    grad_low = grad_two.astype(bf16)
    two_ref[...] = grad_low
    small_ref[3:4, :] = jnp.sum(grad_low.astype(f32), axis=0, keepdims=True)
    grad_hidden = grad_two
    gupb_ref[...] = jnp.zeros(gupb_ref.shape, f32)
    for at in range(FF_TILES):
        cols = slice(at * tile, (at + 1) * tile)
        grad_inner = (nt(grad_low, down_s[cols, :]) * slope_s[:, cols]).astype(bf16)
        inner_s[:, cols] = grad_inner
        leaving.append(pltpu.make_async_copy(inner_s.at[:, cols], inner_ref.at[:, cols], leave_sems.at[1, at]))
        leaving[-1].start()
        gupb_ref[0:1, cols] = jnp.sum(grad_inner.astype(f32), axis=0, keepdims=True)
        grad_hidden = grad_hidden + nt(grad_inner, up_s[:, cols])
    small_ref[1:2, :] = jnp.sum(grad_hidden * normed_one, axis=0, keepdims=True)
    small_ref[2:3, :] = jnp.sum(grad_hidden, axis=0, keepdims=True)
    scaled = grad_hidden * norm_gain
    first = jnp.mean(scaled, axis=1, keepdims=True)
    second = jnp.mean(scaled * normed_one, axis=1, keepdims=True)
    grad_one = inverse_one * (scaled - first - normed_one * second)
    one_ref[...] = grad_one
    grad_branch = grad_one.astype(bf16)
    branch_ref[...] = grad_branch
    small_ref[0:1, :] = jnp.sum(grad_branch.astype(f32), axis=0, keepdims=True)
    small_ref[6:8, :] = jnp.zeros((2, small_ref.shape[1]), f32)
    mixed_ref[...] = nt(grad_branch, wo_s[...]).astype(bf16)
    wait_all(leaving)


def middle(attended, tokens, cotangent, weights, vectors, up_bias):
    offsets, out_own, up_own, shared, down = weights
    counts = (len(attended), len(shared), len(down))
    pieces = [out_own, up_own, *shared, *down]
    block, width = tokens.shape
    inner_width = up_bias.shape[1]
    return pl.pallas_call(
        functools.partial(middle_kernel, counts),
        out_shape=(
            jax.ShapeDtypeStruct((block, width), bf16),
            jax.ShapeDtypeStruct((block, width), f32),
            jax.ShapeDtypeStruct((block, width), bf16),
            jax.ShapeDtypeStruct((block, width), bf16),
            jax.ShapeDtypeStruct((block, width), bf16),
            jax.ShapeDtypeStruct((block, inner_width), bf16),
            jax.ShapeDtypeStruct((block, inner_width), bf16),
            jax.ShapeDtypeStruct((block, width), bf16),
            jax.ShapeDtypeStruct((8, width), f32),
            jax.ShapeDtypeStruct((8, inner_width), f32),
        ),
        in_specs=[smem()] + [whole()] * (4 + len(attended)) + [raw()] * len(pieces),
        out_specs=(whole(),) * 5 + (raw(),) * 2 + (whole(),) * 3,
        scratch_shapes=[
            pltpu.VMEM((width, width), bf16),
            pltpu.VMEM((width, inner_width), bf16),
            pltpu.VMEM((inner_width, width), bf16),
            pltpu.VMEM((block, inner_width), f32),
            pltpu.VMEM((block, inner_width), bf16),
            pltpu.VMEM((block, inner_width), bf16),
            pltpu.SemaphoreType.DMA((2, FF_TILES)),
            pltpu.SemaphoreType.DMA((count_pieces(pieces), 2)),
        ],
        compiler_params=pltpu.CompilerParams(vmem_limit_bytes=VMEM_LIMIT),
        cost_estimate=pl.CostEstimate(flops=24_000_000_000, bytes_accessed=20_000_000, transcendentals=4_000_000),
        name="middle",
    )(offsets, tokens, cotangent, vectors, up_bias, *attended, *pieces)


def grad_down_kernel(micro, core_ref, *refs):
    act_refs, two_refs, side_ref = refs[:micro], refs[micro : 2 * micro], refs[-3]
    total = sum(tn(act[...], two[...]) for act, two in zip(act_refs, two_refs))
    rows, width = total.shape
    side = jnp.concatenate([side_ref[...], jnp.zeros((120, rows), f32)], axis=0).T

    def put(ref):
        ref[0, :, :width] = total.astype(bf16)
        ref[0, :, width:] = side.astype(bf16)

    @pl.when(pl.program_id(0) % 2 == 0)
    def _():
        put(refs[-1])

    @pl.when(pl.program_id(0) % 2 == 1)
    def _():
        put(refs[-2])


def put_halves(core, keep_ref, send_ref, cols, value):
    rows, width = value.shape
    halves = value.reshape(2, 2, rows // 4, width)

    @pl.when(core == 0)
    def _():
        keep_ref[:, :, cols] = halves[:, 0]
        send_ref[:, :, cols] = halves[:, 1]

    @pl.when(core == 1)
    def _():
        keep_ref[:, :, cols] = halves[:, 1]
        send_ref[:, :, cols] = halves[:, 0]


def weight_grad_down(core, activated, grad_low, side):
    micro = len(activated)
    block, inner_width = activated[0].shape
    width = grad_low[0].shape[1]
    tile = inner_width // 4

    def spot(at, core_ref):
        core = core_ref[0]
        return (0, 2 * (at // 2) + jnp.where(at % 2 == 0, 1 - core, core))

    half = jax.ShapeDtypeStruct((2, tile, width + 128), bf16)
    return pl.pallas_call(
        functools.partial(grad_down_kernel, micro),
        out_shape=(half, half),
        grid_spec=pltpu.PrefetchScalarGridSpec(
            num_scalar_prefetch=1,
            grid=(4,),
            in_specs=[pl.BlockSpec((block, tile), spot)] * micro
            + [pl.BlockSpec((block, width), lambda at, core_ref: (0, 0))] * micro
            + [pl.BlockSpec((8, tile), spot)],
            out_specs=[pl.BlockSpec((1, tile, width + 128), lambda at, core_ref: (at // 2, 0, 0))] * 2,
        ),
        compiler_params=pltpu.CompilerParams(vmem_limit_bytes=VMEM_LIMIT),
        cost_estimate=pl.CostEstimate(flops=5_400_000_000, bytes_accessed=14_000_000, transcendentals=0),
        name="weight_grad_down",
    )(core, *activated, *grad_low, side)


def grad_up_kernel(counts, core_ref, *refs):
    micro = len(counts)
    hidden, inner, branch = (refs[at * micro : (at + 1) * micro] for at in range(3))
    keep_ref, send_ref, refs = refs[-2], refs[-1], refs[3 * micro : -2]
    mixed = []
    for size in counts:
        mixed.append(refs[:size])
        refs = refs[size:]
    last = pl.num_programs(0) - 1
    core = core_ref[0]

    @pl.when(pl.program_id(0) < last)
    def _():
        total = sum(tn(one[...], two[...]) for one, two in zip(hidden, inner))
        put_halves(core, keep_ref, send_ref, slice(None), total.astype(bf16))

    @pl.when(pl.program_id(0) == last)
    def _():
        total = sum(tn(join(one), two[...]) for one, two in zip(mixed, branch))
        put_halves(core, keep_ref, send_ref, slice(None), total.astype(bf16))


def weight_grad_up(core, hidden_low, grad_inner, attended, grad_branch):
    micro = len(hidden_low)
    block, width = hidden_low[0].shape
    tiles = grad_inner[0].shape[1] // width
    fixed = [pl.BlockSpec((block, width), lambda at, core_ref: (0, 0))] * micro
    parts = [part for one in attended for part in one]
    half = jax.ShapeDtypeStruct((2, width // 4, (tiles + 1) * width), bf16)
    return pl.pallas_call(
        functools.partial(grad_up_kernel, tuple(len(one) for one in attended)),
        out_shape=(half, half),
        grid_spec=pltpu.PrefetchScalarGridSpec(
            num_scalar_prefetch=1,
            grid=(tiles + 1,),
            in_specs=fixed
            + [pl.BlockSpec((block, width), lambda at, core_ref: (0, jnp.minimum(at, tiles - 1)))] * micro
            + fixed
            + [pl.BlockSpec(part.shape, lambda at, core_ref: (0, 0)) for part in parts],
            out_specs=[pl.BlockSpec((2, width // 4, width), lambda at, core_ref: (0, 0, at))] * 2,
        ),
        compiler_params=pltpu.CompilerParams(vmem_limit_bytes=VMEM_LIMIT),
        cost_estimate=pl.CostEstimate(flops=6_800_000_000, bytes_accessed=16_000_000, transcendentals=0),
        name="weight_grad_up",
    )(core, *hidden_low, *grad_inner, *grad_branch, *parts)


def permute(value, axis, pairs):
    return lax.ppermute(value, axis, pairs)


def swap_pairs(size, distance):
    return [(at, at ^ distance) for at in range(size)]


def even_pairs(size):
    return [(at, at ^ 1) for at in range(size)]


def odd_pairs(size):
    return [(at, min(max(((at + 1) ^ 1) - 1, 0), size - 1)) for at in range(size)]


def pick(array, index, axis=0):
    return lax.dynamic_index_in_dim(array, index, axis, keepdims=False)


def ordered(first_here, mine, other, axis=0):
    first = jnp.where(first_here, mine, other)
    second = jnp.where(first_here, other, mine)
    return jnp.concatenate([first, second], axis=axis)


def two_level(mesh_shape):
    return mesh_shape["replica"] == 4 and mesh_shape["fsdp"] == 2 and mesh_shape["seq"] == 4


def sync(*values):
    return lax.optimization_barrier(values)


class Fetch:
    def __init__(self, fast):
        self.fast = fast
        self.here = lax.axis_index("fsdp")
        self.spot = 2 * lax.axis_index("x") + lax.axis_index("core") if fast else None

    def quarter(self, shard):
        if not self.fast:
            return shard
        size = shard.shape[0] // 4
        return lax.dynamic_slice_in_dim(shard, self.spot * size, size, 0)

    def far(self, quarter):
        if not self.fast:
            return [lax.all_gather(quarter, "fsdp", axis=0, tiled=True)]
        return [permute(quarter, "fsdp", swap_pairs(2, 1))]

    def across(self, held):
        if not self.fast:
            return held
        return held + [permute(held[0], "x", swap_pairs(2, 1))]

    def beside(self, held):
        if not self.fast:
            return held
        pair = jnp.stack(held)
        return [pair, permute(pair, "core", swap_pairs(2, 1))]

    def half(self, shard):
        if not self.fast:
            return shard
        size = shard.shape[0] // 2
        return lax.dynamic_slice_in_dim(shard, lax.axis_index("core") * size, size, 0)

    def half_beside(self, held):
        if not self.fast:
            return held
        return held + [permute(held[0], "core", swap_pairs(2, 1))]

    def offsets(self, rows):
        size = rows // 4
        there = (1 - self.here) * rows
        return [self.here * rows], [there + (self.spot ^ flip) * size for flip in (0, 2, 1, 3)]

    def one_weight(self, shard, held):
        if not self.fast:
            return jnp.zeros((1,), jnp.int32), held
        mine, others = self.offsets(shard.shape[0])
        return jnp.stack(mine + others).astype(jnp.int32), [shard] + held

    def middle_weights(self, out_shard, up_shard, down_shard, shared, down):
        if not self.fast:
            width = shared[0].shape[0]
            return (jnp.zeros((3,), jnp.int32), shared[0][:, :width], shared[0][:, width:], [], down)
        mine, others = self.offsets(out_shard.shape[0])
        rows = down_shard.shape[0]
        core = lax.axis_index("core")
        there = (1 - self.here) * rows
        rest = [self.here * rows, there + core * (rows // 2), there + (1 - core) * (rows // 2)]
        offsets = jnp.stack(mine + mine + others + rest).astype(jnp.int32)
        return offsets, out_shard, up_shard, shared, [down_shard] + down

    def with_vectors(self, quarter, shards):
        if not self.fast:
            return quarter
        return jnp.concatenate([quarter, jnp.concatenate(shards).reshape(-1, quarter.shape[1])], axis=0)

    def without_vectors(self, held, shards):
        if not self.fast:
            return held, [lax.all_gather(shard, "fsdp", axis=0, tiled=True) for shard in shards]
        moved = held[0]
        rows = sum(shard.shape[0] for shard in shards) // moved.shape[1]
        far = moved[moved.shape[0] - rows :].reshape(-1)
        full, at = [], 0
        for shard in shards:
            size = shard.shape[0]
            full.append(ordered(self.here == 0, shard, far[at : at + size]))
            at += size
        return [moved[: moved.shape[0] - rows]], full


def halved(part):
    return part.reshape(2, part.shape[0] // 2, part.shape[1])


def low_sum(parts):
    if len(parts) == 1:
        return parts[0]
    return sum(part.astype(f32) for part in parts).astype(bf16)


def add_low(left, right):
    return low_sum([left, right])


class Chain:
    def __init__(self, fast, *parts):
        self.fast = fast
        self.name = None
        self.pair = list(parts)
        self.path, self.depth = [], []

    def views(self):
        found = []
        for part, depth in zip(self.pair, self.depth):
            for name, index in self.path[depth:]:
                part = pick(halved(part) if name == "z1" else part, index)
            found.append(part)
        return found

    def restart(self, *pair):
        self.pair, self.path, self.depth = list(pair), [], [0] * len(pair)

    def settle(self):
        name, pair = self.name, self.pair
        if name == "z3":
            return ordered(lax.axis_index("seq") % 2 == 0, *pair)
        if name == "spread_x":
            return both_ways(lax.axis_index("x") == 0, *pair)
        if name == "spread_core":
            return both_ways(lax.axis_index("core") == 0, *pair)
        return low_sum(self.views())

    def go(self, name):
        if not self.fast:
            return
        if name == "core":
            keep = [part[0] for part in self.pair]
            send = low_sum([part[1] for part in self.pair])
            moved = permute(send, "core", swap_pairs(2, 1))
            self.name = name
            self.restart(*[one.reshape(2, 2, one.shape[1] // 2, one.shape[2]) for one in keep + [moved]])
            return
        if name in ("z2", "z3", "spread_x", "spread_core"):
            held = self.settle()
            axis = {"z2": "seq", "z3": "seq", "spread_x": "x", "spread_core": "core"}[name]
            pairs = {"z2": swap_pairs(4, 2), "z3": swap_pairs(4, 1)}.get(name, swap_pairs(2, 1))
            self.name = name
            self.restart(held, permute(held, axis, pairs))
            return
        axis = {"y": "fsdp", "x": "x", "z1": "seq"}[name]
        here = lax.axis_index(axis)
        parts = self.views()
        if name == "z1":
            here = here % 2
            parts = [halved(part) for part in parts]
        send = low_sum([pick(part, 1 - here) for part in parts])
        moved = permute(send, axis, swap_pairs(4 if axis == "seq" else 2, 1))
        self.path.append((name, here))
        self.pair.append(moved)
        self.depth.append(len(self.path))
        self.name = name

    def final(self):
        if not self.fast:
            keep, send = (sum(part[at].astype(f32) for part in self.pair) for at in (0, 1))
            parts = jnp.stack([keep, send], axis=1).astype(bf16)
            share = lax.psum_scatter(
                parts.reshape(-1, parts.shape[3]), "fsdp", scatter_dimension=0, tiled=True
            )
            return lax.psum(share, ("replica", "seq")).astype(f32)
        full = self.settle()
        return full.reshape(-1, full.shape[-1]).astype(f32)


def both_ways(first_here, mine, other):
    return jnp.stack([jnp.where(first_here, mine, other), jnp.where(first_here, other, mine)])


def settle_all(chains, *values):
    pairs, *values = sync([chain.pair for chain in chains], *values)
    for chain, pair in zip(chains, pairs):
        chain.pair = pair
    return values


def body(
    fast,
    tokens,
    segment_ids,
    joined_weight,
    query_bias,
    value_bias,
    out_weight,
    out_bias,
    norm_gain,
    norm_shift,
    up_weight,
    up_bias,
    down_weight,
    down_bias,
    final_gain,
    final_shift,
    cotangent,
):
    micro, block, width = tokens.shape[1:]
    length = segment_ids.shape[-1]
    size = lax.axis_size("seq")
    place = lax.axis_index("seq")
    hops = (length // 2 - 2) // block + 1
    assert size % 2 == 0 and hops in (1, 2)
    count = 2 * hops + 1
    inner_width = up_weight.shape[1]
    all_pairs = width // PAIR
    half_pairs = all_pairs // 2
    spans = [(0, half_pairs), (half_pairs, half_pairs)]
    fetch = Fetch(fast)

    def masks_of(ids):
        ends = ((0, 0), (hops * block, 0)), ((0, 0), (0, hops * block + TK_FWD - ALIGN))
        padded = jnp.pad(jnp.pad(ids, ends[0], constant_values=-1), ends[1], constant_values=1000)
        near = lax.dynamic_slice_in_dim(padded, place * block, count * block + TK_FWD - ALIGN, 1)
        rows = near[:, hops * block : (hops + 1) * block]
        low = jnp.sum(near < rows[:, :1], axis=1)
        high = jnp.sum(near <= rows[:, -1:], axis=1)
        bounds = jnp.stack([low, high, jnp.broadcast_to(1 - 2 * (place % 2), low.shape)], axis=1)
        segq = jnp.broadcast_to(rows[:, None, :], (micro, 8, block))
        segk = jnp.broadcast_to(near[:, :, None], near.shape + (128,))
        return bounds.astype(jnp.int32).reshape(-1), segq, segk

    def mask_at(batch):
        return (batch,) + tuple(masks)

    own = [tokens[0, batch] for batch in range(micro)]
    moves = [None] * micro
    small_shards = [
        query_bias,
        value_bias,
        out_bias,
        norm_gain,
        norm_shift,
        down_bias,
        final_gain,
        final_shift,
        up_bias,
    ]
    def hop_out(batch, step):
        if step == 0:
            one, two = own[batch], own[batch]
            moves[batch] = [one, permute(one, "seq", even_pairs(size)), permute(two, "seq", odd_pairs(size))]
        else:
            _, even, odd = moves[batch]
            moves[batch] = moves[batch] + [
                permute(even, "seq", odd_pairs(size)),
                permute(odd, "seq", even_pairs(size)),
            ]

    joined = fetch.far(fetch.with_vectors(fetch.quarter(joined_weight), small_shards))
    hop_out(0, 0)
    quarters = [
        jnp.concatenate([fetch.quarter(out_weight), fetch.quarter(up_weight)], axis=1),
        fetch.half(down_weight),
    ]
    shared = fetch.far(quarters[0])
    joined, moves[0], ids, quarters[1] = sync(joined, moves[0], segment_ids, quarters[1])
    joined, vectors = fetch.without_vectors(joined, small_shards)
    joined = fetch.across(joined)
    for step in range(1, hops):
        hop_out(0, step)
    joined, ids, vectors = sync(joined, ids, vectors)
    joined = fetch.beside(joined)
    masks = masks_of(ids[0])
    biases = jnp.pad(jnp.stack(vectors[:2]).astype(f32), ((0, 6), (0, 0)))
    rows_six = jnp.pad(jnp.stack(vectors[2:8]).astype(f32), ((0, 2), (0, 0)))
    up_row = jnp.pad(vectors[8].astype(f32)[None, :], ((0, 7), (0, 0)))
    shared, quarters[1] = sync(shared, quarters[1])
    shared = fetch.across(shared)
    down = fetch.far(quarters[1])
    moves[0], joined, own[1:], biases, rows_six, up_row, masks = sync(
        moves[0], joined, own[1:], biases, rows_six, up_row, masks
    )

    attended = [[] for _ in range(micro)]

    def window(batch):
        one, even, odd, *far = moves[batch]
        return [far[0], odd, one, even, far[1]] if far else [odd, one, even]

    windows = [window(0)] + [None] * (micro - 1)
    weight = fetch.one_weight(joined_weight, joined)

    if micro > 1:
        hop_out(1, 0)
    attended[0].append(tuple(attend_forward((0, all_pairs), mask_at(0), windows[0], weight, biases)))
    attended[0], shared, down, masks, windows[0], moves[1:2] = sync(
        attended[0], shared, down, masks, windows[0], moves[1:2]
    )
    shared = fetch.beside(shared)
    down = fetch.half_beside(down)
    attended[0], shared, down, own = sync(attended[0], shared, down, own)
    for step in range(1, hops if micro > 1 else 0):
        hop_out(1, step)
    middle_weights = fetch.middle_weights(out_weight, up_weight, down_weight, shared, down)

    middles = []
    for batch in range(micro):
        later = batch + 1
        if batch > 0:
            windows[batch] = window(batch)
            if later < micro:
                hop_out(later, 0)
            attended[batch].append(
                tuple(attend_forward((0, all_pairs), mask_at(batch), windows[batch], weight, biases))
            )
            if later < micro:
                attended[batch], moves[later] = sync(attended[batch], moves[later])
        if batch > 0 and later < micro:
            for step in range(1, hops):
                hop_out(later, step)
        middles.append(
            middle(
                [one[0] for one in attended[batch]],
                own[batch],
                cotangent[0, batch],
                middle_weights,
                rows_six,
                up_row,
            )
        )
        if later < micro:
            middles[-1], masks, moves[later] = sync(middles[-1], masks, moves[later])
        else:
            middles[-1], masks = sync(middles[-1], masks)

    core = lax.axis_index("core") if fast else jnp.zeros((), jnp.int32)
    core = core.astype(jnp.int32).reshape(1)
    outs = list(zip(*middles))
    small = sum(outs[8])
    grad_upb = sum(outs[9])
    half = width // 2
    gap = inner_width // 2 - half
    spread = jnp.pad(small[:6].reshape(6, 2, half), ((0, 0), (0, 0), (0, gap))).reshape(6, inner_width)
    side = jnp.concatenate([grad_upb[:1], spread, jnp.zeros((1, inner_width), f32)], axis=0)
    down = Chain(fast, weight_grad_down(core, outs[6], outs[7], side))
    up_ins = (outs[4], outs[5], [[part[0] for part in one] for one in attended], outs[3])
    (up_ins,) = settle_all([down], up_ins)
    down.go("core")
    up = Chain(fast, weight_grad_up(core, *up_ins))
    (masks,) = settle_all([down, up], list(masks))

    backs = [None] * micro
    coming = [None] * micro
    joined_sums = [[], []]
    last = micro - 1

    def run_back(which, batch, chains, moving=()):
        before = [outs[1][batch]] if which == 0 else backs[batch]
        *parts, keep, send = attend_backward(
            core, spans[which], mask_at(batch), windows[batch], weight, biases, attended[batch], outs[2][batch], before
        )
        moved = [coming[at] for at in moving]
        backs[batch], grad_joined, masks[:], moved = settle_all(chains, parts, (keep, send), list(masks), moved)
        for at, one in zip(moving, moved):
            coming[at] = one
        joined_sums[which].append(grad_joined)

    def total_of(which):
        return Chain(fast, *joined_sums[which])

    def hop_back(batch, step):
        parts = backs[batch]
        if step == 0 and hops > 1:
            coming[batch] = [
                permute(parts[hops + 2], "seq", even_pairs(size)),
                permute(parts[hops - 2], "seq", odd_pairs(size)),
            ]
            return
        odd, even = parts[hops - 1], parts[hops + 1]
        if hops > 1:
            odd, even = add_low(odd, coming[batch][0]), add_low(even, coming[batch][1])
        coming[batch] = [permute(odd, "seq", odd_pairs(size)), permute(even, "seq", even_pairs(size))]

    down.go("y")
    up.go("core")
    run_back(0, 0, [up, down])
    down.go("x")
    up.go("y")
    run_back(1, 0, [down])
    middle_steps = [
        ([(down, "z1")], [down, up]),
        ([(down, "z2"), (up, "x")], [down, up]),
        ([(down, "z3"), (up, "z1")], [down, up]),
        ([(down, "spread_x"), (up, "z2")], [down, up]),
    ]
    for batch in range(1, micro):
        for which in (0, 1):
            begin, end = middle_steps.pop(0) if middle_steps else ([], [])
            for chain, name in begin:
                chain.go(name)
            moving = []
            if which == 0:
                hop_back(batch - 1, 0)
                moving = [batch - 1]
            else:
                for step in range(1, hops):
                    hop_back(batch - 1, step)
                moving = [batch - 1]
            if batch == last and which == 1:
                joined_one = total_of(0)
                joined_one.go("core")
                end = end + [joined_one]
            run_back(which, batch, end, moving)

    joined_two = total_of(1)
    joined_two.go("core")
    joined_one.go("y")
    hop_back(last, 0)
    (backs,) = settle_all([joined_two], backs)
    joined_two.go("y")
    up.go("z3")
    down.go("spread_core")
    coming, backs = settle_all([joined_one, down], coming, backs)
    joined_one.go("x")
    for step in range(1, hops):
        hop_back(last, step)
    settle_all([joined_two, joined_one, up])
    joined_two.go("x")
    joined_one.go("z1")
    up.go("spread_x")
    (coming,) = settle_all([joined_two, joined_one], coming)
    joined_two.go("z1")
    joined_one.go("z2")
    settle_all([joined_two, joined_one, up])
    joined_two.go("z2")
    joined_one.go("z3")
    up.go("spread_core")
    settle_all([joined_two, joined_one])
    joined_two.go("z3")
    joined_one.go("spread_x")
    settle_all([joined_two, joined_one])
    joined_two.go("spread_x")
    joined_one.go("spread_core")
    settle_all([joined_two])
    joined_two.go("spread_core")

    final_down = down.final()
    final_up = up.final()
    final_up, final_out = final_up[:, :inner_width], final_up[:, inner_width:]
    final_a, final_b = joined_one.final(), joined_two.final()
    grad_tokens = []
    for batch in range(micro):
        total = backs[batch][hops] + sum(one.astype(f32) for one in coming[batch])
        grad_tokens.append(total.astype(bf16))
    low, high = spans[0][1] * PAIR, spans[1][1] * PAIR
    final_joined = jnp.concatenate(
        [
            part
            for at in range(3)
            for part in (final_a[:, at * low : (at + 1) * low], final_b[:, at * high : (at + 1) * high])
        ],
        axis=1,
    )
    bias_sums = final_a[:, 3 * low : 3 * low + 2] + final_b[:, 3 * high : 3 * high + 2]
    if fast:
        own_rows = width // lax.axis_size("fsdp")
        smalls = [final_down[:own_rows, width + 1 + at] for at in range(6)]
    else:
        smalls = [
            lax.psum_scatter(lax.psum(small[at], ("replica", "seq")), "fsdp", scatter_dimension=0, tiled=True)
            for at in range(6)
        ]
    return (
        jnp.stack(outs[0], axis=0)[None],
        jnp.stack(grad_tokens, axis=0)[None],
        final_joined,
        bias_sums[:, 0],
        bias_sums[:, 1],
        final_out,
        smalls[0],
        smalls[1],
        smalls[2],
        final_up,
        final_down[:, width],
        final_down[:, :width],
        smalls[3],
        smalls[4],
        smalls[5],
    )


def solution(mesh):
    fast = two_level(dict(mesh.shape))
    groups = ("replica", "fsdp")
    if fast:
        mesh = jax.sharding.Mesh(mesh.devices.reshape(2, 2, 2, 4), ("x", "core", "fsdp", "seq"))
        groups = ("x", "core", "fsdp")
    rows = P(groups, None, "seq", None)
    matrix, vector = P("fsdp", None), P("fsdp")
    in_specs = (
        rows,
        P(groups, None, None),
        matrix,
        vector,
        vector,
        matrix,
        vector,
        vector,
        vector,
        matrix,
        vector,
        matrix,
        vector,
        vector,
        vector,
        rows,
    )
    out_specs = (
        rows,
        rows,
        matrix,
        vector,
        vector,
        matrix,
        vector,
        vector,
        vector,
        matrix,
        vector,
        matrix,
        vector,
        vector,
        vector,
    )
    return jax.shard_map(
        functools.partial(body, fast),
        mesh=mesh,
        in_specs=in_specs,
        out_specs=out_specs,
        check_vma=False,
    )
```
